32 devices in a mesh: dp: 8 (over z, x), tensor: 4 (over y, core).
Axes of the slice: x: 2, y: 2, z: 4, core: 2. Of those that a mesh axis runs over, the one named last changes fastest.
Arguments:
- block_input: bfloat16 [2, 8192, 1024], P(None, ('dp', 'tensor')), may hold values from -6 to 6
- cotangent: bfloat16 [2, 8192, 1024], P(None, 'dp'), may hold values from -6 to 6
- parent: int32 [2, 2, 16], replicated, may hold values from -1 to 15, as said below
- pre_attn_gain: float32 [1024], replicated, may hold values from 0.25 to 1.75
- qkv_weight: bfloat16 [3, 1024, 1024], P(None, None, 'tensor'), may hold values from -0.1875 to 0.1875
- head_scale: float32 [16], P('tensor'), may hold values from 0.5 to 2
- out_weight: bfloat16 [1024, 1024], P('tensor'), may hold values from -0.1875 to 0.1875
- post_attn_gain: float32 [1024], replicated, may hold values from 0.25 to 1.75
- pre_ffn_gain: float32 [1024], replicated, may hold values from 0.25 to 1.75
- fc1_weight: bfloat16 [1024, 4096], P(None, 'tensor'), may hold values from -0.1875 to 0.1875
- ffn_norm_gain: float32 [4096], P('tensor'), may hold values from 0.25 to 1.75
- fc2_weight: bfloat16 [4096, 1024], P('tensor'), may hold values from -0.09375 to 0.09375
Outputs:
- block_output: bfloat16 [2, 8192, 1024], P(None, ('dp', 'tensor'))
- input_grad: float32 [2, 8192, 1024], P(None, ('dp', 'tensor'))
- pre_attn_gain_grad: float32 [1024], replicated
- qkv_weight_grad: float32 [3, 1024, 1024], P(None, None, 'tensor')
- head_scale_grad: float32 [16], P('tensor')
- out_weight_grad: float32 [1024, 1024], P('tensor')
- post_attn_gain_grad: float32 [1024], replicated
- pre_ffn_gain_grad: float32 [1024], replicated
- fc1_weight_grad: float32 [1024, 4096], P(None, 'tensor')
- ffn_norm_gain_grad: float32 [4096], P('tensor')
- fc2_weight_grad: float32 [4096, 1024], P('tensor')
The draws below stay inside these ranges and needn't reach their ends.
Inputs may be any that keep to these rules, and one draw needn't show every extreme that they name: In each tree exactly one segment has parent -1; it heads a chain of 4 segments, each the parent of the next; 4 branch segments have the chain's last segment as parent; the other 8 segments are leaves, two under each branch. Which position holds which segment is drawn anew for every tree.
All inputs are finite; a program needn't handle non-finite values.
Results may differ from the reference program's by a relative error of at most 0.017.
The reference program's roundings to bfloat16 on the way count: a program that leaves them out, or rounds other values in their place, can miss the bound.
Values may be sent and summed in bfloat16 or wider, within the bound.
A program may use at most 320 MiB of HBM per device.

```python
import math
import jax
import jax.numpy as jnp
from jax import lax

DMODEL = 1024
HEADS = 16
HEAD_DIM = 64
FFN = 4096
SEG_LEN = 256
SEGS = 16
MICRO = 2
TREE_TOK = 4096
TREES = 2
TOKENS = 8192


def tree_parents(tree_key):
    role_key, leaf_key = jax.random.split(tree_key)
    role_at = jax.random.permutation(role_key, SEGS).astype(jnp.int32)
    place_of = jnp.argsort(role_at, stable=True).astype(jnp.int32)
    chain_count = SEGS // 4
    role_index = jnp.arange(SEGS, dtype=jnp.int32)
    leaf_order = jax.random.permutation(leaf_key, SEGS // 2).astype(jnp.int32)
    leaf_index = jnp.clip(role_index - 2 * chain_count, 0, SEGS // 2 - 1)
    leaf_parent = chain_count + jnp.take(leaf_order, leaf_index) // 2
    parent_role = jnp.where(role_index < chain_count, role_index - 1, jnp.where(role_index < 2 * chain_count, chain_count - 1, leaf_parent))
    parent_role_at = jnp.take(parent_role, role_at)
    return jnp.where(parent_role_at < 0, -1, jnp.take(place_of, jnp.maximum(parent_role_at, 0))).astype(jnp.int32)


def draw_parent(key, part):
    tree_keys = jax.random.split(key, MICRO * TREES)
    return jax.vmap(tree_parents)(tree_keys).reshape(MICRO, TREES, SEGS)


def levels(own_key, dims, cuts, low, high):
    def one(dim, blocks):
        steps = jax.random.uniform(jax.random.fold_in(jax.random.fold_in(own_key, 6), dim), (blocks,), jnp.float32, low / len(cuts), high / len(cuts))
        return jnp.repeat(jnp.exp(steps), dims[dim] // blocks).reshape((-1,) + (1,) * (len(dims) - dim - 1))

    loudness = one(*cuts[0])
    for cut in cuts[1:]:
        loudness = loudness * one(*cut)
    return loudness


def normal_values(own_key, dims, scale, reach, shards=(), kind=jnp.bfloat16):
    factor_of = levels(own_key, dims, shards, -0.22, 0.18) if shards else 1.0
    array = jax.random.normal(own_key, dims, jnp.float32) * scale * factor_of
    return jnp.minimum(jnp.maximum(array, -reach), reach).astype(kind)


def setup_inputs(seed: int = 0) -> dict:
    keys = jax.random.split(jax.random.key(seed), 13)
    return {
        "block_input": normal_values(keys[0], (MICRO, TOKENS, DMODEL), 1.0, 6.0, ((1, 32),)),
        "cotangent": normal_values(keys[1], (MICRO, TOKENS, DMODEL), 1.0, 6.0, ((1, 8),)),
        "parent": draw_parent(jax.random.fold_in(keys[12], 71), 0),
        "pre_attn_gain": jnp.clip(1.0 + 0.15 * jax.random.normal(keys[3], (DMODEL,), jnp.float32), 0.25, 1.75),
        "qkv_weight": normal_values(keys[4], (3, DMODEL, HEADS * HEAD_DIM), DMODEL ** -0.5, 0.1875, ((2, 4),)),
        "head_scale": jnp.clip(jnp.exp(math.log(2.0) - 1.3862944 * jax.random.uniform(keys[5], (HEADS,), jnp.float32) ** levels(keys[5], (HEADS,), ((0, 4),), -0.2, 0.2)), 0.5, 2.0),
        "out_weight": normal_values(keys[6], (HEADS * HEAD_DIM, DMODEL), (HEADS * HEAD_DIM) ** -0.5, 0.1875, ((0, 4),)),
        "post_attn_gain": jnp.clip(1.0 + 0.15 * jax.random.normal(keys[7], (DMODEL,), jnp.float32), 0.25, 1.75),
        "pre_ffn_gain": jnp.clip(1.0 + 0.15 * jax.random.normal(keys[8], (DMODEL,), jnp.float32), 0.25, 1.75),
        "fc1_weight": normal_values(keys[9], (DMODEL, FFN), DMODEL ** -0.5, 0.1875, ((1, 4),)),
        "ffn_norm_gain": jnp.clip(1.0 + 0.15 * jax.random.normal(keys[10], (FFN,), jnp.float32), 0.25, 1.75),
        "fc2_weight": normal_values(keys[11], (FFN, DMODEL), FFN ** -0.5, 0.09375, ((0, 4),)),
    }


@jax.custom_vjp
def low(v):
    return lax.optimization_barrier(v.astype(jnp.bfloat16)).astype(jnp.float32)

@jax.custom_vjp
def low_back(v):
    return v

def low_keep(v):
    return (low(v), None)

def low_pass(kept, grad):
    return (grad,)

def back_keep(v):
    return (v, None)

def back_low(kept, grad):
    return (low(grad),)
low.defvjp(low_keep, low_pass)
low_back.defvjp(back_keep, back_low)
EPSILON = 1e-05
NEGATIVE = -1e+30
HIGHEST = lax.Precision.HIGHEST

def normalize(values):
    center = values - lax.optimization_barrier(jnp.mean(values, axis=-1, keepdims=True))
    return center * lax.rsqrt(lax.optimization_barrier(jnp.mean(center * center, axis=-1, keepdims=True)) + EPSILON)

def normalize_wide(values):
    mean_value = lax.optimization_barrier(jnp.mean(values, axis=-1, keepdims=True))
    mean_square = lax.optimization_barrier(jnp.mean(values * values, axis=-1, keepdims=True))
    return (values - mean_value) * lax.rsqrt(mean_square - mean_value * mean_value + EPSILON)

def ancestors(parent_row):
    seg_index = jnp.arange(SEGS, dtype=jnp.int32)

    def climb(step_index, running):
        current, seg_table = running
        reached = seg_index[None, :] == current[:, None]
        upward = lax.optimization_barrier(jnp.sum(jnp.where(reached, parent_row[None, :], 0), axis=1)).astype(jnp.int32)
        return (jnp.where(current >= 0, upward, -1).astype(jnp.int32), jnp.logical_or(seg_table, reached))
    start = (parent_row.astype(jnp.int32), jnp.zeros((SEGS, SEGS), dtype=jnp.bool_))
    return lax.fori_loop(0, SEGS, climb, start)[1]

def tree_attention(queries, tree_keys, values, seg_table):
    block_rows = min(512, TREE_TOK)
    key_pos = jnp.arange(TREE_TOK, dtype=jnp.int32)
    key_seg = key_pos // SEG_LEN

    def one_block(operands):
        query_block, first_row = operands
        query_pos = first_row + jnp.arange(block_rows, dtype=jnp.int32)
        query_seg = query_pos // SEG_LEN
        inside = jnp.logical_and(query_seg[:, None] == key_seg[None, :], key_pos[None, :] <= query_pos[:, None])
        allowed = jnp.logical_or(seg_table[query_seg][:, key_seg], inside)
        scores = low_back(jnp.einsum('qhd,khd->hqk', query_block, tree_keys, precision=HIGHEST) * HEAD_DIM ** (-0.5))
        scores = jnp.where(allowed[None], scores, NEGATIVE)
        soft_probs = jnp.exp(scores - jax.nn.logsumexp(scores, axis=-1, keepdims=True))
        return low_back(jnp.einsum('hqk,khd->qhd', low(soft_probs), values, precision=HIGHEST))
    query_blocks = queries.reshape(TREE_TOK // block_rows, block_rows, HEADS, HEAD_DIM)
    block_starts = block_rows * jnp.arange(TREE_TOK // block_rows, dtype=jnp.int32)
    return lax.map(jax.checkpoint(one_block), (query_blocks, block_starts)).reshape(TREE_TOK, HEADS, HEAD_DIM)

def layer_forward(layer_input, table_set, weights):
    pre_attn_gain, qkv_weight, head_scale, out_weight, post_attn_gain, pre_ffn_gain, fc1_weight, ffn_norm_gain, fc2_weight = weights
    hidden_one = low(normalize(layer_input) * pre_attn_gain)
    projected = low(low_back(jnp.einsum('td,ide->ite', hidden_one, qkv_weight, precision=HIGHEST)))
    shaped = projected.reshape(3, TREES, TREE_TOK, HEADS, HEAD_DIM)
    attended = lax.map(lambda operands: tree_attention(operands[0], operands[1], operands[2], operands[3]), (shaped[0], shaped[1], shaped[2], table_set))
    scaled = low(attended * head_scale[None, None, :, None]).reshape(TOKENS, HEADS * HEAD_DIM)
    mixed = low_back(jnp.dot(scaled, out_weight, precision=HIGHEST))
    residual = layer_input + normalize(mixed) * post_attn_gain
    hidden_two = low(normalize(residual) * pre_ffn_gain)
    pre_act = low_back(jnp.dot(hidden_two, fc1_weight, precision=HIGHEST))
    hidden_wide = low(normalize_wide(jax.nn.gelu(pre_act, approximate=True)) * ffn_norm_gain)
    return residual + low_back(jnp.dot(hidden_wide, fc2_weight, precision=HIGHEST))

def reference(block_input, cotangent, parent, pre_attn_gain, qkv_weight, head_scale, out_weight, post_attn_gain, pre_ffn_gain, fc1_weight, ffn_norm_gain, fc2_weight):
    weights = (pre_attn_gain.astype(jnp.float32), qkv_weight.astype(jnp.float32), head_scale.astype(jnp.float32), out_weight.astype(jnp.float32), post_attn_gain.astype(jnp.float32), pre_ffn_gain.astype(jnp.float32), fc1_weight.astype(jnp.float32), ffn_norm_gain.astype(jnp.float32), fc2_weight.astype(jnp.float32))
    totals = tuple((jnp.zeros(weight_item.shape, jnp.float32) for weight_item in weights))
    outputs = []
    input_grads = []
    for micro_index in range(MICRO):
        table_set = jax.vmap(ancestors)(parent[micro_index])

        def forward_micro(layer_input, weight_tuple):
            return layer_forward(layer_input, table_set, weight_tuple)
        result, pull_back = jax.vjp(forward_micro, block_input[micro_index].astype(jnp.float32), weights)
        input_part, weight_parts = pull_back(cotangent[micro_index].astype(jnp.float32))
        outputs.append(result.astype(jnp.bfloat16))
        input_grads.append(input_part)
        totals = tuple((running_total + addend for running_total, addend in zip(totals, weight_parts)))
    return (jnp.stack(outputs), jnp.stack(input_grads), totals[0], totals[1], totals[2], totals[3], totals[4], totals[5], totals[6], totals[7], totals[8])
```

```python
from functools import partial

import jax
import jax.numpy as jnp
from jax import lax
from jax.experimental import pallas as pl
from jax.experimental.pallas import tpu as pltpu
from jax.sharding import PartitionSpec as P

HEAD_DIM = 64
FFN = 4096
SEG = 256
SEGS = 16
DEPTH = 5
MICRO = 2

EPSILON = 1e-05
NEGATIVE = -1e30
F32 = jnp.float32
BF = jnp.bfloat16
NN = (((1,), (0,)), ((), ()))
NT = (((1,), (1,)), ((), ()))
TN = (((0,), (0,)), ((), ()))


def mm(a, b, dims=NN):
    return lax.dot_general(a, b, dims, preferred_element_type=F32)


def swap(value, axis, mask):
    return lax.ppermute(value, axis, [(i, i ^ mask) for i in range(lax.axis_size(axis))])


def normalize(values):
    center = values - jnp.mean(values, axis=-1, keepdims=True)
    inverse = lax.rsqrt(jnp.mean(center * center, axis=-1, keepdims=True) + EPSILON)
    return (center * inverse, inverse)


def norm_backward(grad_hat, normed, inverse):
    mean_grad = jnp.mean(grad_hat, axis=-1, keepdims=True)
    mean_cross = jnp.mean(grad_hat * normed, axis=-1, keepdims=True)
    return inverse * (grad_hat - mean_grad - normed * mean_cross)


def gather_rows(own):
    far = swap(own, "tensor", 2)
    near = swap(own, "tensor", 1)
    cross = swap(far, "tensor", 1)
    return jnp.concatenate([own, near, far, cross], axis=0)


def scatter_rows(partial_rows):
    rows = partial_rows.shape[0] // 4
    blocks = [partial_rows[r * rows:(r + 1) * rows] for r in range(4)]
    got_far = swap(blocks[3].astype(BF), "tensor", 1)
    got_own = swap(blocks[1].astype(BF), "tensor", 1)
    far = blocks[2].astype(F32) + got_far.astype(F32)
    got = swap(far.astype(BF), "tensor", 2)
    return blocks[0].astype(F32) + got_own.astype(F32) + got.astype(F32)


def sum_small(values, axis):
    mask = 1
    while mask < lax.axis_size(axis):
        values = values + swap(values, axis, mask)
        mask *= 2
    return values


def sum_rows(values):
    blocks = values.reshape(values.shape[0], 4, -1)
    got = swap(blocks, "tensor", 1)
    blocks = blocks + jnp.stack([got[:, r ^ 1] for r in range(4)], axis=1)
    got = swap(blocks, "tensor", 2)
    blocks = blocks + jnp.stack([got[:, r ^ 2] for r in range(4)], axis=1)
    return blocks.reshape(values.shape)


def sum_spread(values):
    bits = [2**b for b in range(lax.axis_size("dp").bit_length() - 1)]
    index = lax.axis_index("dp")
    part = values
    for mask in bits:
        half = part.shape[0] // 2
        upper = (index // mask) % 2
        send = lax.dynamic_slice_in_dim(part, (1 - upper) * half, half, 0)
        keep = lax.dynamic_slice_in_dim(part, upper * half, half, 0)
        part = keep + swap(send.astype(BF), "dp", mask).astype(F32)
    part = part.astype(BF)
    for mask in bits[::-1]:
        got = swap(part, "dp", mask)
        upper = (index // mask) % 2 == 1
        part = jnp.where(upper, jnp.stack([got, part]), jnp.stack([part, got]))
        part = part.reshape((-1,) + part.shape[2:])
    return part.astype(F32)


def climb(parents, base, seg):
    found = []
    current = seg
    count = jnp.int32(0)
    for _ in range(DEPTH):
        up = parents[base + current]
        valid = up >= 0
        count = count + valid.astype(jnp.int32)
        current = jnp.where(valid, up, current)
        found.append(current)
    return count, found


def place_of(seg, per, member, shard):
    return ((seg // per) ^ member) * per + ((seg % per) ^ shard)


def attend_forward(place, parents, q_ref, *rest):
    keys, values = rest[0:4], rest[4:8]
    scale_ref, o_ref, os_ref, lse_ref, tree, picked, sems = rest[8:]
    step = pl.program_id(0)
    width = q_ref.shape[1]
    heads = width // HEAD_DIM
    tokens = keys[0].shape[0]
    per = tokens // SEG
    base, member, shard = place[0], place[1], place[2]

    @pl.when(step == 0)
    def _():
        copies = []
        for r in range(4):
            rows = pl.ds(r * tokens, tokens)
            copies.append(pltpu.make_async_copy(keys[r], tree.at[rows, pl.ds(0, width)], sems.at[r]))
            copies.append(pltpu.make_async_copy(values[r], tree.at[rows, pl.ds(width, width)], sems.at[4 + r]))
        for copy in copies:
            copy.start()
        for copy in copies:
            copy.wait()

    count, found = climb(parents, base, member * per + (step ^ shard))
    for slot in range(DEPTH):
        start = pl.multiple_of(place_of(found[slot], per, member, shard) * SEG, SEG)
        picked[pl.ds(slot * SEG, SEG), :] = tree[pl.ds(start, SEG), :]
    past = DEPTH * SEG
    picked[pl.ds(past, SEG), :] = tree[pl.ds(pl.multiple_of(step * SEG, SEG), SEG), :]
    lane = lax.broadcasted_iota(jnp.int32, (SEG, width), 1) // HEAD_DIM
    row = lax.broadcasted_iota(jnp.int32, (SEG, SEG), 0)
    col = lax.broadcasted_iota(jnp.int32, (SEG, SEG), 1)
    slot_of = lax.broadcasted_iota(jnp.int32, (1, past), 1) // SEG
    bias = jnp.where(slot_of < count, 0.0, NEGATIVE).astype(F32)
    q = q_ref[...] * BF(HEAD_DIM ** -0.5)
    lse_lane = lax.broadcasted_iota(jnp.int32, (SEG, 128), 1)
    lse_all = jnp.zeros((SEG, 128), F32)
    out = jnp.zeros((SEG, width), F32)
    for head in range(heads):
        qh = jnp.where(lane == head, q, jnp.zeros_like(q))
        s_past = mm(qh, picked[0:past, 0:width], NT) + bias
        s_own = jnp.where(col <= row, mm(qh, picked[past:past + SEG, 0:width], NT), NEGATIVE)
        top = jnp.maximum(
            jnp.max(s_past, axis=1, keepdims=True), jnp.max(s_own, axis=1, keepdims=True)
        )
        p_past = jnp.exp(s_past - top)
        p_own = jnp.exp(s_own - top)
        total = jnp.sum(p_past, axis=1, keepdims=True) + jnp.sum(p_own, axis=1, keepdims=True)
        got = mm(p_past.astype(BF), picked[0:past, width:2 * width])
        got = got + mm(p_own.astype(BF), picked[past:past + SEG, width:2 * width])
        out = jnp.where(lane == head, got / total, out)
        lse_all = jnp.where(lse_lane == head, top + jnp.log(total), lse_all)
    o_ref[...] = out
    os_ref[...] = (out * scale_ref[...]).astype(BF)
    lse_ref[...] = jnp.transpose(lse_all)[0:8].reshape(1, 8, SEG)


def attend_backward(place, parents, q_ref, dos_ref, o_ref, lse_ref, scale_ref, *rest):
    keys, values = rest[0:4], rest[4:8]
    dq_ref, dks, dvs, sg_ref = rest[8], rest[9:13], rest[13:17], rest[17]
    tree, acc, dqt, sems = rest[18:]
    step = pl.program_id(0)
    width = q_ref.shape[1]
    heads = width // HEAD_DIM
    tokens = keys[0].shape[0]
    per = tokens // SEG
    base, member, shard = place[0], place[1], place[2]

    @pl.when(step == 0)
    def _():
        copies = []
        for r in range(4):
            rows = pl.ds(r * tokens, tokens)
            copies.append(pltpu.make_async_copy(keys[r], tree.at[rows, pl.ds(0, width)], sems.at[r]))
            copies.append(pltpu.make_async_copy(values[r], tree.at[rows, pl.ds(width, width)], sems.at[4 + r]))
        for copy in copies:
            copy.start()
        acc[...] = jnp.zeros_like(acc)
        sg_ref[...] = jnp.zeros_like(sg_ref)
        for copy in copies:
            copy.wait()

    dos = dos_ref[...].astype(F32)
    cross = dos * o_ref[...]
    sg_ref[...] += jnp.sum(cross.reshape(SEG // 8, 8, width), axis=0)
    scale = scale_ref[...]
    go = (dos * scale).astype(BF)
    cross_t = jnp.transpose(cross * scale)
    lane = lax.broadcasted_iota(jnp.int32, (SEG, width), 1) // HEAD_DIM
    q = q_ref[...] * BF(HEAD_DIM ** -0.5)
    zero = jnp.zeros_like(q)
    q_heads = [jnp.where(lane == h, q, zero) for h in range(heads)]
    g_heads = [jnp.where(lane == h, go, zero) for h in range(heads)]
    deltas = [
        jnp.sum(cross_t[h * HEAD_DIM:(h + 1) * HEAD_DIM], axis=0, keepdims=True) for h in range(heads)
    ]
    lses = [lse_ref[0, h:h + 1, :] for h in range(heads)]
    dqt[...] = jnp.zeros_like(dqt)

    def block(start, own):
        rows = pl.ds(pl.multiple_of(start, SEG), SEG)
        k = tree[rows, 0:width]
        v = tree[rows, width:2 * width]
        kt = jnp.transpose(k)
        dk = jnp.zeros((SEG, width), F32)
        dv = jnp.zeros((SEG, width), F32)
        for h in range(heads):
            p = jnp.exp(mm(k, q_heads[h], NT) - lses[h])
            if own:
                key_row = lax.broadcasted_iota(jnp.int32, (SEG, SEG), 0)
                query_col = lax.broadcasted_iota(jnp.int32, (SEG, SEG), 1)
                p = jnp.where(key_row <= query_col, p, 0.0)
            dv += mm(p.astype(BF), g_heads[h])
            dp = mm(v, g_heads[h], NT)
            ds = (p * (dp - deltas[h])).astype(BF)
            dk += mm(ds, q_heads[h])
            dqt[pl.ds(h * HEAD_DIM, HEAD_DIM), :] += mm(kt[h * HEAD_DIM:(h + 1) * HEAD_DIM], ds)
        acc[rows, 0:width] += dk
        acc[rows, width:2 * width] += dv

    def upward(j, current):
        up = parents[base + current]
        block(place_of(up, per, member, shard) * SEG, False)
        return up

    seg = member * per + (step ^ shard)
    count, _ = climb(parents, base, seg)
    lax.fori_loop(0, count, upward, seg)
    block(step * SEG, True)
    dq_ref[...] = (jnp.transpose(dqt[...]) * HEAD_DIM ** -0.5).astype(BF)

    @pl.when(step == pl.num_programs(0) - 1)
    def _():
        for r in range(4):
            dks[r][...] = acc[r * tokens:(r + 1) * tokens, 0:width].astype(BF)
            dvs[r][...] = acc[r * tokens:(r + 1) * tokens, width:2 * width].astype(BF)


ROW = lambda i, *s: (i, 0)
FIX = lambda i, *s: (0, 0)
HBM = pl.BlockSpec(memory_space=pl.ANY)


def attention(place, parents, q, keys, values, scale_row):
    tokens, width = q.shape
    segs = tokens // SEG
    return pl.pallas_call(
        attend_forward,
        out_shape=(
            jax.ShapeDtypeStruct((tokens, width), F32),
            jax.ShapeDtypeStruct((tokens, width), BF),
            jax.ShapeDtypeStruct((segs, 8, SEG), F32),
        ),
        grid_spec=pltpu.PrefetchScalarGridSpec(
            num_scalar_prefetch=2,
            grid=(segs,),
            in_specs=[pl.BlockSpec((SEG, width), ROW)] + [HBM] * 8 + [pl.BlockSpec((1, width), FIX)],
            out_specs=[
                pl.BlockSpec((SEG, width), ROW),
                pl.BlockSpec((SEG, width), ROW),
                pl.BlockSpec((1, 8, SEG), lambda i, *s: (i, 0, 0)),
            ],
            scratch_shapes=[
                pltpu.VMEM((4 * tokens, 2 * width), BF),
                pltpu.VMEM(((DEPTH + 1) * SEG, 2 * width), BF),
                pltpu.SemaphoreType.DMA((8,)),
            ],
        ),
        compiler_params=pltpu.CompilerParams(
            dimension_semantics=("arbitrary",), vmem_limit_bytes=32 << 20
        ),
        cost_estimate=pl.CostEstimate(flops=16 * 10**9, transcendentals=0, bytes_accessed=8 << 20),
        name="attend_forward",
    )(place, parents, q, *keys, *values, scale_row)


def attention_grad(place, parents, q, dos, o, lse, scale_row, keys, values):
    tokens, width = q.shape
    segs = tokens // SEG
    piece = jax.ShapeDtypeStruct((tokens, width), BF)
    whole = pl.BlockSpec((tokens, width), FIX)
    return pl.pallas_call(
        attend_backward,
        out_shape=(piece,) + (piece,) * 8 + (jax.ShapeDtypeStruct((8, width), F32),),
        grid_spec=pltpu.PrefetchScalarGridSpec(
            num_scalar_prefetch=2,
            grid=(segs,),
            in_specs=[
                pl.BlockSpec((SEG, width), ROW),
                pl.BlockSpec((SEG, width), ROW),
                pl.BlockSpec((SEG, width), ROW),
                pl.BlockSpec((1, 8, SEG), lambda i, *s: (i, 0, 0)),
                pl.BlockSpec((1, width), FIX),
            ]
            + [HBM] * 8,
            out_specs=[pl.BlockSpec((SEG, width), ROW)] + [whole] * 8 + [pl.BlockSpec((8, width), FIX)],
            scratch_shapes=[
                pltpu.VMEM((4 * tokens, 2 * width), BF),
                pltpu.VMEM((4 * tokens, 2 * width), F32),
                pltpu.VMEM((width, SEG), F32),
                pltpu.SemaphoreType.DMA((8,)),
            ],
        ),
        compiler_params=pltpu.CompilerParams(
            dimension_semantics=("arbitrary",), vmem_limit_bytes=40 << 20
        ),
        cost_estimate=pl.CostEstimate(flops=36 * 10**9, transcendentals=0, bytes_accessed=12 << 20),
        name="attend_backward",
    )(place, parents, q, dos, o, lse, scale_row, *keys, *values)


def gelu_parts(c):
    root = 0.7978845608028654
    square = c * c
    tanh = jnp.tanh(root * (c + 0.044715 * (square * c)))
    act = 0.5 * c * (1.0 + tanh)
    slope = 0.5 * (1.0 + tanh) + 0.5 * c * (1.0 - tanh * tanh) * (root * (1.0 + 3 * 0.044715 * square))
    return act, slope


def body(
    block_input,
    cotangent,
    parent,
    pre_attn_gain,
    qkv_weight,
    head_scale,
    out_weight,
    post_attn_gain,
    pre_ffn_gain,
    fc1_weight,
    ffn_norm_gain,
    fc2_weight,
):
    trees = parent.shape[1]
    group = lax.axis_size("dp") // trees
    member = lax.axis_index("dp") % group
    tree_index = lax.axis_index("dp") // group
    shard = lax.axis_index("tensor")
    row_count = block_input.shape[1]
    tokens = cotangent.shape[1]
    width = qkv_weight.shape[2]
    parents = parent.reshape(-1)
    scale_row = jnp.repeat(head_scale, HEAD_DIM)[None, :]

    def place(micro):
        return jnp.stack([(micro * trees + tree_index) * SEGS, member, shard]).astype(jnp.int32)

    state = [dict() for _ in range(MICRO)]
    for micro, s in enumerate(state):
        s["rows"] = block_input[micro].astype(F32)
        s["n1"], s["i1"] = normalize(s["rows"])
        s["full1"] = gather_rows((s["n1"] * pre_attn_gain).astype(BF))
    for micro, s in enumerate(state):
        own_k = mm(s["full1"], qkv_weight[1]).astype(BF)
        own_v = mm(s["full1"], qkv_weight[2]).astype(BF)
        k1, k2 = swap(own_k, "dp", 1), swap(own_k, "dp", 2)
        v1, v2 = swap(own_v, "dp", 1), swap(own_v, "dp", 2)
        k3, v3 = swap(k1, "dp", 2), swap(v2, "dp", 1)
        s["keys"] = (own_k, k1, k2, k3)
        s["values"] = (own_v, v1, v2, v3)
        s["q"] = mm(s["full1"], qkv_weight[0]).astype(BF)
    fc1_grad = fc2_grad = out_grad = wide_gain = 0.0
    for micro, s in enumerate(state):
        s["o"], s["os"], s["lse"] = attention(
            place(micro), parents, s["q"], s["keys"], s["values"], scale_row
        )
        mixed = scatter_rows(mm(s["os"], out_weight))
        s["nu"], s["iu"] = normalize(mixed)
        s["r1"] = s["rows"] + s["nu"] * post_attn_gain
        s["n2"], s["i2"] = normalize(s["r1"])
        s["full2"] = gather_rows((s["n2"] * pre_ffn_gain).astype(BF))
    for micro, s in enumerate(state):
        grad_all = jnp.concatenate(
            [
                lax.dynamic_slice_in_dim(cotangent[micro], (shard ^ r) * row_count, row_count, 0)
                for r in range(4)
            ],
            axis=0,
        )
        s["grad_all"] = grad_all
        s["grad_rows"] = grad_all[0:row_count].astype(F32)
        act, slope = gelu_parts(mm(s["full2"], fc1_weight))
        dz = mm(grad_all, fc2_weight, NT)
        dna = dz * ffn_norm_gain
        sums = jnp.stack(
            [jnp.sum(act, -1), jnp.sum(act * act, -1), jnp.sum(dna, -1), jnp.sum(dna * act, -1)]
        )
        sums = sum_rows(sums) / FFN
        mu, square, m_dna, m_cross = [sums[i][:, None] for i in range(4)]
        rw = lax.rsqrt(square - mu * mu + EPSILON)
        m_dna_na = (m_cross - mu * m_dna) * rw
        na = (act - mu) * rw
        z = (na * ffn_norm_gain).astype(BF)
        wide_gain = wide_gain + jnp.sum(dz * na, axis=0)
        dc = (rw * (dna - m_dna - na * m_dna_na) * slope).astype(BF)
        dh2 = scatter_rows(mm(dc, fc1_weight, NT))
        s["ffn_rows"] = scatter_rows(mm(z, fc2_weight))
        fc2_grad = fc2_grad + mm(z, grad_all, TN)
        fc1_grad = fc1_grad + mm(s["full2"], dc, TN)
        s["two_gain"] = jnp.sum(dh2 * s["n2"], axis=0)
        s["dr1"] = s["grad_rows"] + norm_backward(dh2 * pre_ffn_gain, s["n2"], s["i2"])
        s["post_gain"] = jnp.sum(s["dr1"] * s["nu"], axis=0)
        du = norm_backward(s["dr1"] * post_attn_gain, s["nu"], s["iu"]).astype(BF)
        s["du"] = gather_rows(du)
    ffn_grads = sum_spread(jnp.concatenate([fc1_grad, fc2_grad], axis=0))
    qkv_grad = 0.0
    head_grad = 0.0
    for micro, s in enumerate(state):
        dos = mm(s["du"], out_weight, NT)
        out_grad = out_grad + mm(s["os"], s["du"], TN)
        got = attention_grad(
            place(micro), parents, s["q"], dos, s["o"], s["lse"], scale_row, s["keys"], s["values"]
        )
        dq, dk, dv, sg = got[0], got[1:5], got[5:9], got[9]
        head_grad = head_grad + sg
        add = lambda a, b: (a.astype(F32) + b.astype(F32)).astype(BF)
        k0, k1 = add(dk[0], swap(dk[2], "dp", 2)), add(dk[1], swap(dk[3], "dp", 2))
        v0, v2 = add(dv[0], swap(dv[1], "dp", 1)), add(dv[2], swap(dv[3], "dp", 1))
        own_k = add(k0, swap(k1, "dp", 1))
        own_v = add(v0, swap(v2, "dp", 2))
        grads = [dq, own_k, own_v]
        qkv_grad = qkv_grad + jnp.stack([mm(s["full1"], g, TN) for g in grads])
        dh1 = mm(dq, qkv_weight[0], NT) + mm(own_k, qkv_weight[1], NT) + mm(own_v, qkv_weight[2], NT)
        dh1 = scatter_rows(dh1)
        s["one_gain"] = jnp.sum(dh1 * s["n1"], axis=0)
        s["din"] = s["dr1"] + norm_backward(dh1 * pre_attn_gain, s["n1"], s["i1"])
    attn_grads = sum_spread(
        jnp.concatenate([qkv_grad.reshape(-1, 1024), out_grad], axis=0)
    )
    gains = jnp.stack([sum(s[k] for s in state) for k in ("one_gain", "post_gain", "two_gain")])
    gains = sum_small(gains, "tensor")
    head_row = jnp.sum(head_grad, axis=0).reshape(-1, HEAD_DIM).sum(-1)
    head_row = jnp.pad(head_row, (0, wide_gain.shape[0] - head_row.shape[0]))
    small = sum_small(jnp.concatenate([gains, wide_gain[None], head_row[None]], axis=0), "dp")
    return (
        jnp.stack([(s["r1"] + s["ffn_rows"]).astype(BF) for s in state]),
        jnp.stack([s["din"] for s in state]),
        small[0],
        attn_grads[0:3 * width].reshape(qkv_weight.shape),
        small[4, 0:head_scale.shape[0]],
        attn_grads[3 * width:],
        small[1],
        small[2],
        ffn_grads[0:fc1_weight.shape[0]],
        small[3],
        ffn_grads[fc1_weight.shape[0]:],
    )


def solution(mesh):
    in_specs = (
        P(None, ("dp", "tensor"), None),
        P(None, "dp", None),
        P(),
        P(),
        P(None, None, "tensor"),
        P("tensor"),
        P("tensor", None),
        P(),
        P(),
        P(None, "tensor"),
        P("tensor"),
        P("tensor", None),
    )
    out_specs = (
        P(None, ("dp", "tensor"), None),
        P(None, ("dp", "tensor"), None),
        P(),
        P(None, None, "tensor"),
        P("tensor"),
        P("tensor", None),
        P(),
        P(),
        P(None, "tensor"),
        P("tensor"),
        P("tensor", None),
    )
    return jax.shard_map(body, mesh=mesh, in_specs=in_specs, out_specs=out_specs, check_vma=False)
```

```python
from functools import partial

import jax
import jax.numpy as jnp
from jax import lax
from jax.experimental import pallas as pl
from jax.experimental.pallas import tpu as pltpu
from jax.sharding import PartitionSpec as P

HEAD_DIM = 64
FFN = 4096
SEG = 256
SEGS = 16
DEPTH = 5
MICRO = 2

EPSILON = 1e-05
NEGATIVE = -1e30
F32 = jnp.float32
BF = jnp.bfloat16
NN = (((1,), (0,)), ((), ()))
NT = (((1,), (1,)), ((), ()))
TN = (((0,), (0,)), ((), ()))


def mm(a, b, dims=NN):
    return lax.dot_general(a, b, dims, preferred_element_type=F32)


def swap(value, axis, mask):
    return lax.ppermute(value, axis, [(i, i ^ mask) for i in range(lax.axis_size(axis))])


def normalize(values):
    center = values - jnp.mean(values, axis=-1, keepdims=True)
    inverse = lax.rsqrt(jnp.mean(center * center, axis=-1, keepdims=True) + EPSILON)
    return (center * inverse, inverse)


def norm_backward(grad_hat, normed, inverse):
    mean_grad = jnp.mean(grad_hat, axis=-1, keepdims=True)
    mean_cross = jnp.mean(grad_hat * normed, axis=-1, keepdims=True)
    return inverse * (grad_hat - mean_grad - normed * mean_cross)


def gather_rows(own):
    far = swap(own, "tensor", 2)
    near = swap(own, "tensor", 1)
    cross = swap(far, "tensor", 1)
    return jnp.concatenate([own, near, far, cross], axis=0)


def scatter_rows(partial_rows):
    rows = partial_rows.shape[0] // 4
    blocks = [partial_rows[r * rows:(r + 1) * rows] for r in range(4)]
    got_far = swap(blocks[3].astype(BF), "tensor", 1)
    got_own = swap(blocks[1].astype(BF), "tensor", 1)
    far = blocks[2].astype(F32) + got_far.astype(F32)
    got = swap(far.astype(BF), "tensor", 2)
    return blocks[0].astype(F32) + got_own.astype(F32) + got.astype(F32)


def sum_small(values, axis):
    mask = 1
    while mask < lax.axis_size(axis):
        values = values + swap(values, axis, mask)
        mask *= 2
    return values


def sum_rows(values):
    blocks = values.reshape(values.shape[0], 4, -1)
    got = swap(blocks, "tensor", 1)
    blocks = blocks + jnp.stack([got[:, r ^ 1] for r in range(4)], axis=1)
    got = swap(blocks, "tensor", 2)
    blocks = blocks + jnp.stack([got[:, r ^ 2] for r in range(4)], axis=1)
    return blocks.reshape(values.shape)


def sum_spread(values):
    bits = [2**b for b in range(lax.axis_size("dp").bit_length() - 1)]
    index = lax.axis_index("dp")
    part = values
    for mask in bits:
        half = part.shape[0] // 2
        upper = (index // mask) % 2
        send = lax.dynamic_slice_in_dim(part, (1 - upper) * half, half, 0)
        keep = lax.dynamic_slice_in_dim(part, upper * half, half, 0)
        part = keep + swap(send.astype(BF), "dp", mask).astype(F32)
    part = part.astype(BF)
    for mask in bits[::-1]:
        got = swap(part, "dp", mask)
        upper = (index // mask) % 2 == 1
        part = jnp.where(upper, jnp.stack([got, part]), jnp.stack([part, got]))
        part = part.reshape((-1,) + part.shape[2:])
    return part.astype(F32)


def climb(parents, base, seg):
    found = []
    current = seg
    count = jnp.int32(0)
    for _ in range(DEPTH):
        up = parents[base + current]
        valid = up >= 0
        count = count + valid.astype(jnp.int32)
        current = jnp.where(valid, up, current)
        found.append(current)
    return count, found


def place_of(seg, per, member, shard):
    return ((seg // per) ^ member) * per + ((seg % per) ^ shard)


def attend_forward(place, parents, q_ref, *rest):
    keys, values = rest[0:4], rest[4:8]
    scale_ref, o_ref, os_ref, lse_ref, tree, picked, sems = rest[8:]
    step = pl.program_id(0)
    width = q_ref.shape[1]
    heads = width // HEAD_DIM
    tokens = keys[0].shape[0]
    per = tokens // SEG
    base, member, shard = place[0], place[1], place[2]

    @pl.when(step == 0)
    def _():
        copies = []
        for r in range(4):
            rows = pl.ds(r * tokens, tokens)
            copies.append(pltpu.make_async_copy(keys[r], tree.at[rows, pl.ds(0, width)], sems.at[r]))
            copies.append(pltpu.make_async_copy(values[r], tree.at[rows, pl.ds(width, width)], sems.at[4 + r]))
        for copy in copies:
            copy.start()
        for copy in copies:
            copy.wait()

    count, found = climb(parents, base, member * per + (step ^ shard))
    for slot in range(DEPTH):
        start = pl.multiple_of(place_of(found[slot], per, member, shard) * SEG, SEG)
        picked[pl.ds(slot * SEG, SEG), :] = tree[pl.ds(start, SEG), :]
    past = DEPTH * SEG
    picked[pl.ds(past, SEG), :] = tree[pl.ds(pl.multiple_of(step * SEG, SEG), SEG), :]
    lane = lax.broadcasted_iota(jnp.int32, (SEG, width), 1) // HEAD_DIM
    row = lax.broadcasted_iota(jnp.int32, (SEG, SEG), 0)
    col = lax.broadcasted_iota(jnp.int32, (SEG, SEG), 1)
    slot_of = lax.broadcasted_iota(jnp.int32, (1, past), 1) // SEG
    bias = jnp.where(slot_of < count, 0.0, NEGATIVE).astype(F32)
    q = q_ref[...] * BF(HEAD_DIM ** -0.5)
    lse_lane = lax.broadcasted_iota(jnp.int32, (SEG, 128), 1)
    lse_all = jnp.zeros((SEG, 128), F32)
    out = jnp.zeros((SEG, width), F32)
    for head in range(heads):
        qh = jnp.where(lane == head, q, jnp.zeros_like(q))
        s_past = mm(qh, picked[0:past, 0:width], NT) + bias
        s_own = jnp.where(col <= row, mm(qh, picked[past:past + SEG, 0:width], NT), NEGATIVE)
        top = jnp.maximum(
            jnp.max(s_past, axis=1, keepdims=True), jnp.max(s_own, axis=1, keepdims=True)
        )
        p_past = jnp.exp(s_past - top)
        p_own = jnp.exp(s_own - top)
        total = jnp.sum(p_past, axis=1, keepdims=True) + jnp.sum(p_own, axis=1, keepdims=True)
        got = mm(p_past.astype(BF), picked[0:past, width:2 * width])
        got = got + mm(p_own.astype(BF), picked[past:past + SEG, width:2 * width])
        out = jnp.where(lane == head, got / total, out)
        lse_all = jnp.where(lse_lane == head, top + jnp.log(total), lse_all)
    o_ref[...] = out
    os_ref[...] = (out * scale_ref[...]).astype(BF)
    lse_ref[...] = jnp.transpose(lse_all)[0:8].reshape(1, 8, SEG)


def attend_backward(place, parents, q_ref, dos_ref, o_ref, lse_ref, scale_ref, *rest):
    keys, values = rest[0:4], rest[4:8]
    dq_ref, dk_ref, dv_ref, sg_ref, tree, acc, dqt, sems = rest[8:]
    step = pl.program_id(0)
    width = q_ref.shape[1]
    heads = width // HEAD_DIM
    tokens = keys[0].shape[0]
    per = tokens // SEG
    base, member, shard = place[0], place[1], place[2]

    @pl.when(step == 0)
    def _():
        copies = []
        for r in range(4):
            rows = pl.ds(r * tokens, tokens)
            copies.append(pltpu.make_async_copy(keys[r], tree.at[rows, pl.ds(0, width)], sems.at[r]))
            copies.append(pltpu.make_async_copy(values[r], tree.at[rows, pl.ds(width, width)], sems.at[4 + r]))
        for copy in copies:
            copy.start()
        acc[...] = jnp.zeros_like(acc)
        sg_ref[...] = jnp.zeros_like(sg_ref)
        for copy in copies:
            copy.wait()

    dos = dos_ref[...].astype(F32)
    cross = dos * o_ref[...]
    sg_ref[...] += jnp.sum(cross.reshape(SEG // 8, 8, width), axis=0)
    scale = scale_ref[...]
    go = (dos * scale).astype(BF)
    cross_t = jnp.transpose(cross * scale)
    lane = lax.broadcasted_iota(jnp.int32, (SEG, width), 1) // HEAD_DIM
    q = q_ref[...] * BF(HEAD_DIM ** -0.5)
    zero = jnp.zeros_like(q)
    q_heads = [jnp.where(lane == h, q, zero) for h in range(heads)]
    g_heads = [jnp.where(lane == h, go, zero) for h in range(heads)]
    deltas = [
        jnp.sum(cross_t[h * HEAD_DIM:(h + 1) * HEAD_DIM], axis=0, keepdims=True) for h in range(heads)
    ]
    lses = [lse_ref[0, h:h + 1, :] for h in range(heads)]
    dqt[...] = jnp.zeros_like(dqt)

    def block(start, own):
        rows = pl.ds(pl.multiple_of(start, SEG), SEG)
        k = tree[rows, 0:width]
        v = tree[rows, width:2 * width]
        kt = jnp.transpose(k)
        dk = jnp.zeros((SEG, width), F32)
        dv = jnp.zeros((SEG, width), F32)
        for h in range(heads):
            p = jnp.exp(mm(k, q_heads[h], NT) - lses[h])
            if own:
                key_row = lax.broadcasted_iota(jnp.int32, (SEG, SEG), 0)
                query_col = lax.broadcasted_iota(jnp.int32, (SEG, SEG), 1)
                p = jnp.where(key_row <= query_col, p, 0.0)
            dv += mm(p.astype(BF), g_heads[h])
            dp = mm(v, g_heads[h], NT)
            ds = (p * (dp - deltas[h])).astype(BF)
            dk += mm(ds, q_heads[h])
            dqt[pl.ds(h * HEAD_DIM, HEAD_DIM), :] += mm(kt[h * HEAD_DIM:(h + 1) * HEAD_DIM], ds)
        acc[rows, 0:width] += dk
        acc[rows, width:2 * width] += dv

    def upward(j, current):
        up = parents[base + current]
        block(place_of(up, per, member, shard) * SEG, False)
        return up

    seg = member * per + (step ^ shard)
    count, _ = climb(parents, base, seg)
    lax.fori_loop(0, count, upward, seg)
    block(step * SEG, True)
    dq_ref[...] = (jnp.transpose(dqt[...]) * HEAD_DIM ** -0.5).astype(BF)

    @pl.when(step == pl.num_programs(0) - 1)
    def _():
        for r in range(4):
            dk_ref[r] = acc[r * tokens:(r + 1) * tokens, 0:width].astype(BF)
            dv_ref[r] = acc[r * tokens:(r + 1) * tokens, width:2 * width].astype(BF)


ROW = lambda i, *s: (i, 0)
FIX = lambda i, *s: (0, 0)
HBM = pl.BlockSpec(memory_space=pl.ANY)


def attention(place, parents, q, keys, values, scale_row):
    tokens, width = q.shape
    segs = tokens // SEG
    return pl.pallas_call(
        attend_forward,
        out_shape=(
            jax.ShapeDtypeStruct((tokens, width), F32),
            jax.ShapeDtypeStruct((tokens, width), BF),
            jax.ShapeDtypeStruct((segs, 8, SEG), F32),
        ),
        grid_spec=pltpu.PrefetchScalarGridSpec(
            num_scalar_prefetch=2,
            grid=(segs,),
            in_specs=[pl.BlockSpec((SEG, width), ROW)] + [HBM] * 8 + [pl.BlockSpec((1, width), FIX)],
            out_specs=[
                pl.BlockSpec((SEG, width), ROW),
                pl.BlockSpec((SEG, width), ROW),
                pl.BlockSpec((1, 8, SEG), lambda i, *s: (i, 0, 0)),
            ],
            scratch_shapes=[
                pltpu.VMEM((4 * tokens, 2 * width), BF),
                pltpu.VMEM(((DEPTH + 1) * SEG, 2 * width), BF),
                pltpu.SemaphoreType.DMA((8,)),
            ],
        ),
        compiler_params=pltpu.CompilerParams(
            dimension_semantics=("arbitrary",), vmem_limit_bytes=32 << 20
        ),
        cost_estimate=pl.CostEstimate(flops=16 * 10**9, transcendentals=0, bytes_accessed=8 << 20),
        name="attend_forward",
    )(place, parents, q, *keys, *values, scale_row)


def attention_grad(place, parents, q, dos, o, lse, scale_row, keys, values):
    tokens, width = q.shape
    segs = tokens // SEG
    pieces = jax.ShapeDtypeStruct((4, tokens, width), BF)
    whole = pl.BlockSpec((4, tokens, width), lambda i, *s: (0, 0, 0))
    return pl.pallas_call(
        attend_backward,
        out_shape=(
            jax.ShapeDtypeStruct((tokens, width), BF),
            pieces,
            pieces,
            jax.ShapeDtypeStruct((8, width), F32),
        ),
        grid_spec=pltpu.PrefetchScalarGridSpec(
            num_scalar_prefetch=2,
            grid=(segs,),
            in_specs=[
                pl.BlockSpec((SEG, width), ROW),
                pl.BlockSpec((SEG, width), ROW),
                pl.BlockSpec((SEG, width), ROW),
                pl.BlockSpec((1, 8, SEG), lambda i, *s: (i, 0, 0)),
                pl.BlockSpec((1, width), FIX),
            ]
            + [HBM] * 8,
            out_specs=[pl.BlockSpec((SEG, width), ROW)] + [whole] * 2 + [pl.BlockSpec((8, width), FIX)],
            scratch_shapes=[
                pltpu.VMEM((4 * tokens, 2 * width), BF),
                pltpu.VMEM((4 * tokens, 2 * width), F32),
                pltpu.VMEM((width, SEG), F32),
                pltpu.SemaphoreType.DMA((8,)),
            ],
        ),
        compiler_params=pltpu.CompilerParams(
            dimension_semantics=("arbitrary",), vmem_limit_bytes=40 << 20
        ),
        cost_estimate=pl.CostEstimate(flops=36 * 10**9, transcendentals=0, bytes_accessed=12 << 20),
        name="attend_backward",
    )(place, parents, q, dos, o, lse, scale_row, *keys, *values)


def gelu_parts(c):
    root = 0.7978845608028654
    square = c * c
    tanh = jnp.tanh(root * (c + 0.044715 * (square * c)))
    act = 0.5 * c * (1.0 + tanh)
    slope = 0.5 * (1.0 + tanh) + 0.5 * c * (1.0 - tanh * tanh) * (root * (1.0 + 3 * 0.044715 * square))
    return act, slope


def other(shard, mask):
    near = shard + 1 - 2 * (shard % 2)
    return {0: shard, 1: near, 2: (shard + 2) % 4, 3: (near + 2) % 4}[mask]


def middle(
    os0, os1, x, g_hbm, fc1_hbm, fc2_hbm, out_w, post, pre, wide,
    z_hbm, dc_hbm, h2_hbm, du_hbm, dos, dr1, f_own, f_far, gains,
    fc1, fc2, gd, act, slz, dzc, full, core_out, core_in, y_out, y_in, nu, inv, st_out, st_in, sums, cols,
    send, recv, local,
):
    shard = lax.axis_index("tensor")
    peers = [other(shard, k) for k in range(4)]
    rows = x.shape[1]
    model = x.shape[2]
    hidden = fc1.shape[1]
    parts = hidden // SEG
    used = [0]
    pending = []

    def remote(src, dst, mask):
        i = used[0]
        used[0] += 1
        copy = pltpu.make_async_remote_copy(
            src_ref=src, dst_ref=dst, send_sem=send.at[i], recv_sem=recv.at[i],
            device_id={"tensor": peers[mask]}, device_id_type=pl.DeviceIdType.MESH,
        )
        copy.start()
        pending.append(copy)
        return copy

    stored = [0]
    stores = []

    def store(src, dst):
        i = stored[0]
        stored[0] += 1
        copy = pltpu.make_async_copy(src, dst, local.at[i])
        copy.start()
        stores.append(copy)

    def fetch(src, dst):
        i = stored[0]
        stored[0] += 1
        copy = pltpu.make_async_copy(src, dst, local.at[i])
        copy.start()
        return copy

    got_fc2 = fetch(fc2_hbm, fc2)
    got_g = [
        [fetch(g_hbm.at[m, pl.ds(peers[r] * rows, rows), :], gd.at[m, r]) for r in range(4)] for m in range(MICRO)
    ]
    got_fc1 = fetch(fc1_hbm, fc1)
    barrier = pltpu.get_barrier_semaphore()
    for mask in (1, 2, 3):
        pl.semaphore_signal(
            barrier, inc=1, device_id={"tensor": peers[mask]}, device_id_type=pl.DeviceIdType.MESH
        )
    pl.semaphore_wait(barrier, 3)
    gains[...] = jnp.zeros_like(gains)

    def each(count, fn):
        lax.fori_loop(0, count, lambda i, c: (fn(i), c)[1], 0)

    def tile(n):
        return pl.ds(pl.multiple_of(n * SEG, SEG), SEG)

    def first_hop(kind, m, block, out):
        block(3, core_out.at[kind, m, 0])
        hop3 = remote(core_out.at[kind, m, 0], core_in.at[kind, m, 0], 1)
        block(1, core_out.at[kind, m, 1])
        hop1 = remote(core_out.at[kind, m, 1], core_in.at[kind, m, 1], 1)
        block(2, None)
        block(0, out)
        return hop3, hop1

    chunk = 32

    def chunks(fn):
        each(rows // chunk, lambda i: fn(pl.ds(pl.multiple_of(i * chunk, chunk), chunk)))

    def add_far(kind, m):
        def one(at):
            y_out[kind, m, at] = (sums_far[m][at] + core_in[kind, m, 0, at].astype(F32)).astype(BF)

        chunks(one)

    sums_far = [f_own.at[m] for m in range(MICRO)]
    oss = (os0, os1)

    def mixed_block(m):
        def block(r, out):
            part = mm(oss[m][r * rows:(r + 1) * rows, :], out_w[...])
            if r == 2:
                sums_far[m][...] = part
            else:
                out[...] = part.astype(out.dtype)

        return block

    hops = [first_hop(0, m, mixed_block(m), nu.at[m]) for m in range(MICRO)]
    far_hops = []
    for m in range(MICRO):
        hops[m][0].wait_recv()
        add_far(0, m)
        far_hops.append(remote(y_out.at[0, m], y_in.at[0, m], 2))

    got_fc2.wait()

    def project_grad(m):
        for r in range(4):
            got_g[m][r].wait()

        def one(i):
            r, n = i // parts, i % parts
            dzc[m, r, :, tile(n)] = mm(gd[m, r], fc2[tile(n), :], NT).astype(BF)

        each(4 * parts, one)

    def own_sum(kind, m, base, at):
        return base + core_in[kind, m, 1, at].astype(F32) + y_in[kind, m, at].astype(F32)

    def norm_two(m, at, residual):
        center = residual - jnp.mean(residual, axis=-1, keepdims=True)
        inverse = lax.rsqrt(jnp.mean(center * center, axis=-1, keepdims=True) + EPSILON)
        return center * inverse, inverse

    def forward_norms(m):
        hops[m][1].wait_recv()
        far_hops[m].wait_recv()

        def one(at):
            mixed, inverse = norm_two(m, at, own_sum(0, m, nu[m, at], at))
            nu[m, at] = mixed
            inv[m, at] = jnp.broadcast_to(inverse, (chunk, 128))
            residual = x[m, at].astype(F32) + mixed * post[...]
            normed, _ = norm_two(m, at, residual)
            full[m, 0, at] = (normed * pre[...]).astype(BF)

        chunks(one)

    def spread(m, buf):
        return remote(buf.at[m, 0], buf.at[m, 2], 2), remote(buf.at[m, 0], buf.at[m, 1], 1)

    def ffn_forward(m, r):
        sums[...] = jnp.zeros_like(sums)

        def one(n):
            value, slope = gelu_parts(mm(full[m, r], fc1[:, tile(n)]))
            act[m, r, :, tile(n)] = value
            slz[m, r, :, tile(n)] = slope.astype(BF)
            dna = dzc[m, r, :, tile(n)].astype(F32) * wide[:, tile(n)]
            for i, term in enumerate((value, value * value, dna, dna * value)):
                sums[i] += term[:, 0:128] + term[:, 128:256]

        each(parts, one)
        lane = lax.broadcasted_iota(jnp.int32, (rows, 128), 1)
        merged = jnp.zeros((rows, 128), F32)
        for i in range(4):
            merged = jnp.where(lane == i, jnp.sum(sums[i], axis=-1, keepdims=True), merged)
        st_out[m, :, r * rows:(r + 1) * rows] = jnp.transpose(merged)[0:8]

    def send_stats(m):
        return [remote(st_out.at[m], st_in.at[m, mask - 1], mask) for mask in (1, 2, 3)]

    def ffn_backward_rows(m, r):
        total = st_out[m, :, r * rows:(r + 1) * rows]
        for mask in (1, 2, 3):
            b = r ^ mask
            total = total + st_in[m, mask - 1, :, b * rows:(b + 1) * rows]
        cols[0:8, :] = total * (1.0 / FFN)
        flipped = jnp.transpose(cols[...])
        mu, square, m_dna, m_cross = [flipped[:, i:i + 1] for i in range(4)]
        rw = lax.rsqrt(square - mu * mu + EPSILON)
        m_both = (m_cross - mu * m_dna) * rw

        def one(n):
            gain = wide[:, tile(n)]
            dz = dzc[m, r, :, tile(n)].astype(F32)
            na = (act[m, r, :, tile(n)] - mu) * rw
            slope = slz[m, r, :, tile(n)].astype(F32)
            slz[m, r, :, tile(n)] = (na * gain).astype(BF)
            gains[16:24, tile(n)] += jnp.sum((dz * na).reshape(rows // 8, 8, SEG), axis=0)
            dzc[m, r, :, tile(n)] = (rw * (dz * gain - m_dna - na * m_both) * slope).astype(BF)

        each(parts, one)

    def grad_block(m):
        def block(r, out):
            ffn_backward_rows(m, r)
            if r == 2:
                out = sums_far[m]

            def one(n):
                out[:, tile(n)] = mm(dzc[m, r], fc1[tile(n), :], NT).astype(out.dtype)

            each(model // SEG, one)
            store(slz.at[m, r], z_hbm.at[m, pl.ds(peers[r] * rows, rows), :])
            store(dzc.at[m, r], dc_hbm.at[m, pl.ds(r * rows, rows), :])

        return block

    def ffn_out_block(m):
        def block(r, out):
            if r == 2:
                out = sums_far[m]

            def one(n):
                out[:, tile(n)] = mm(slz[m, r], fc2[:, tile(n)]).astype(out.dtype)

            each(model // SEG, one)

        return block

    def backward_norms(m, hop1, far_hop):
        hop1.wait_recv()
        far_hop.wait_recv()

        def one(at):
            dh2 = own_sum(1, m, dr1[m, at], at)
            mixed = nu[m, at]
            residual = x[m, at].astype(F32) + mixed * post[...]
            normed, inverse = norm_two(m, at, residual)
            gains[8:16, :] += jnp.sum((dh2 * normed).reshape(chunk // 8, 8, model), axis=0)
            grad = gd[m, 0, at].astype(F32) + norm_backward(dh2 * pre[...], normed, inverse)
            gains[0:8, :] += jnp.sum((grad * mixed).reshape(chunk // 8, 8, model), axis=0)
            dr1[m, at] = grad
            back = norm_backward(grad * post[...], mixed, inv[m, at][:, 0:1])
            gd[m, 0, at] = back.astype(BF)

        chunks(one)

    def unmix(m, r):
        dos[m, r * rows:(r + 1) * rows, :] = mm(gd[m, r], out_w[...], NT)

    project_grad(0)
    project_grad(1)
    forward_norms(0)
    far0, near0 = spread(0, full)
    got_fc1.wait()
    ffn_forward(0, 0)
    near0.wait_recv()
    ffn_forward(0, 1)
    forward_norms(1)
    far1, near1 = spread(1, full)
    ffn_forward(1, 0)
    far0.wait_recv()
    cross0 = remote(full.at[0, 2], full.at[0, 3], 1)
    ffn_forward(0, 2)
    cross0.wait_recv()
    ffn_forward(0, 3)
    stats0 = send_stats(0)
    near1.wait_recv()
    ffn_forward(1, 1)
    far1.wait_recv()
    cross1 = remote(full.at[1, 2], full.at[1, 3], 1)
    ffn_forward(1, 2)
    for copy in stats0:
        copy.wait_recv()
    hop_a = first_hop(1, 0, grad_block(0), dr1.at[0])
    hop_a[0].wait_recv()
    add_far(1, 0)
    far_a = remote(y_out.at[1, 0], y_in.at[1, 0], 2)
    cross1.wait_recv()
    ffn_forward(1, 3)
    stats1 = send_stats(1)
    for m in range(MICRO):
        for r in range(4):
            store(full.at[m, r], h2_hbm.at[m, pl.ds(r * rows, rows), :])
    for copy in stats1:
        copy.wait_recv()
    hop_b = first_hop(1, 1, grad_block(1), dr1.at[1])
    hop_b[0].wait_recv()
    add_far(1, 1)
    far_b = remote(y_out.at[1, 1], y_in.at[1, 1], 2)
    backward_norms(0, hop_a[1], far_a)
    du_far0, du_near0 = spread(0, gd)

    for hop in hops:
        hop[0].wait_send()
        hop[1].wait_send()
        pending.remove(hop[0])
        pending.remove(hop[1])

    def ffn_out(m):
        hop3, hop1 = first_hop(0, m, ffn_out_block(m), f_far_f32)
        hop3.wait_recv()

        def one(at):
            f_far[m, at] = (sums_far[m][at] + core_in[0, m, 0, at].astype(F32)).astype(BF)

        chunks(one)
        hop1.wait_recv()

        def two(at):
            residual = x[m, at].astype(F32) + nu[m, at] * post[...]
            f_own[m, at] = residual + f_far_f32[at] + core_in[0, m, 1, at].astype(F32)

        chunks(two)

    f_far_f32 = act.at[0, 0]
    ffn_out(0)
    backward_norms(1, hop_b[1], far_b)
    du_far1, du_near1 = spread(1, gd)
    unmix(0, 0)
    du_near0.wait_recv()
    unmix(0, 1)
    du_far0.wait_recv()
    du_cross0 = remote(gd.at[0, 2], gd.at[0, 3], 1)
    unmix(0, 2)
    ffn_out(1)
    du_cross0.wait_recv()
    unmix(0, 3)
    unmix(1, 0)
    du_near1.wait_recv()
    unmix(1, 1)
    for r in range(4):
        store(gd.at[0, r], du_hbm.at[0, pl.ds(r * rows, rows), :])
    du_far1.wait_recv()
    du_cross1 = remote(gd.at[1, 2], gd.at[1, 3], 1)
    unmix(1, 2)
    du_cross1.wait_recv()
    unmix(1, 3)
    for r in range(4):
        store(gd.at[1, r], du_hbm.at[1, pl.ds(r * rows, rows), :])
    for copy in pending:
        copy.wait_send()
    for copy in stores:
        copy.wait()


def middle_call(os_pair, x, g, fc1, fc2, out_w, post, pre, wide):
    micro, rows, model = x.shape
    hidden = fc1.shape[1]
    width = out_w.shape[0]
    tokens = 4 * rows
    vmem = pl.BlockSpec(memory_space=pltpu.VMEM)
    big = jax.ShapeDtypeStruct((micro, tokens, hidden), BF)
    wide_rows = jax.ShapeDtypeStruct((micro, tokens, model), BF)
    own = jax.ShapeDtypeStruct((micro, rows, model), F32)
    return pl.pallas_call(
        middle,
        out_shape=(
            big, big, wide_rows, wide_rows,
            jax.ShapeDtypeStruct((micro, tokens, width), F32),
            own, own,
            jax.ShapeDtypeStruct((micro, rows, model), BF),
            jax.ShapeDtypeStruct((24, model), F32),
        ),
        in_specs=[vmem, vmem, vmem, HBM, HBM, HBM, vmem, vmem, vmem, vmem],
        out_specs=(HBM, HBM, HBM, HBM, vmem, vmem, vmem, vmem, vmem),
        scratch_shapes=[
            pltpu.VMEM((model, hidden), BF),
            pltpu.VMEM((hidden, model), BF),
            pltpu.VMEM((micro, 4, rows, model), BF),
            pltpu.VMEM((micro, 4, rows, hidden), F32),
            pltpu.VMEM((micro, 4, rows, hidden), BF),
            pltpu.VMEM((micro, 4, rows, hidden), BF),
            pltpu.VMEM((micro, 4, rows, model), BF),
            pltpu.VMEM((2, micro, 2, rows, model), BF),
            pltpu.VMEM((2, micro, 2, rows, model), BF),
            pltpu.VMEM((2, micro, rows, model), BF),
            pltpu.VMEM((2, micro, rows, model), BF),
            pltpu.VMEM((micro, rows, model), F32),
            pltpu.VMEM((micro, rows, 128), F32),
            pltpu.VMEM((micro, 8, tokens), F32),
            pltpu.VMEM((micro, 3, 8, tokens), F32),
            pltpu.VMEM((4, rows, 128), F32),
            pltpu.VMEM((128, rows), F32),
            pltpu.SemaphoreType.DMA((40,)),
            pltpu.SemaphoreType.DMA((40,)),
            pltpu.SemaphoreType.DMA((48,)),
        ],
        compiler_params=pltpu.CompilerParams(
            collective_id=0, has_side_effects=True, vmem_limit_bytes=58 << 20
        ),
        cost_estimate=pl.CostEstimate(flops=100 * 10**9, transcendentals=0, bytes_accessed=40 << 20),
        name="middle",
    )(*os_pair, x, g, fc1, fc2, out_w, post, pre, wide)


def finish(
    bits, dq0, dq1, dk0, dk1, dv0, dv1, full0, full1, x, dr1, weight, pre, mid_gains, head0, head1,
    din, grad, small_out,
    piece, inbox, inner, grads, acc, stage, arrived, res, core_out, core_in, y_out, y_in, small, small_in,
    send, recv, local,
):
    shard = lax.axis_index("tensor")
    index = lax.axis_index("dp")
    near, far = other(shard, 1), other(shard, 2)
    rows, model = x.shape[1], x.shape[2]
    tokens, width = dq0.shape
    dqs, dks, dvs, fulls = (dq0, dq1), (dk0, dk1), (dv0, dv1), (full0, full1)

    def bit_of(mask):
        return (index // mask) % 2

    def dp_peer(mask):
        return {"dp": index + mask - 2 * mask * bit_of(mask)}

    used = [0]
    pending = []

    def remote(src, dst, target):
        i = used[0]
        used[0] += 1
        copy = pltpu.make_async_remote_copy(
            src_ref=src, dst_ref=dst, send_sem=send.at[i], recv_sem=recv.at[i],
            device_id=target, device_id_type=pl.DeviceIdType.MESH,
        )
        copy.start()
        pending.append(copy)
        return copy

    fetched = [0]

    def fetch(src, dst):
        i = fetched[0]
        fetched[0] += 1
        copy = pltpu.make_async_copy(src, dst, local.at[i])
        copy.start()
        return copy

    def each(count, fn):
        lax.fori_loop(0, count, lambda i, c: (fn(i), c)[1], 0)

    def tile(n):
        return pl.ds(pl.multiple_of(n * SEG, SEG), SEG)

    barrier = pltpu.get_barrier_semaphore()
    targets = [{"tensor": near}, {"tensor": far}] + [dp_peer(mask) for mask in bits]
    for target in targets:
        pl.semaphore_signal(barrier, inc=1, device_id=target, device_id_type=pl.DeviceIdType.MESH)
    got = [
        [fetch(dks[m].at[0], piece.at[m, 0]), fetch(dks[m].at[1], piece.at[m, 1]),
         fetch(dvs[m].at[0], piece.at[m, 2]), fetch(dvs[m].at[2], piece.at[m, 3])]
        for m in range(MICRO)
    ]
    pl.semaphore_wait(barrier, len(targets))

    def first_sends(m):
        return [
            remote(dks[m].at[3], inbox.at[m, 0], dp_peer(2)),
            remote(dvs[m].at[3], inbox.at[m, 1], dp_peer(1)),
            remote(dks[m].at[2], inbox.at[m, 2], dp_peer(2)),
            remote(dvs[m].at[1], inbox.at[m, 3], dp_peer(1)),
        ]

    def add_rows(out, terms):
        def one(n):
            total = terms[0][tile(n), :].astype(F32)
            for term in terms[1:]:
                total = total + term[tile(n), :].astype(F32)
            out[tile(n), :] = total.astype(out.dtype)

        each(tokens // SEG, one)

    def second_sends(m, first):
        for copy in got[m]:
            copy.wait()
        first[0].wait_recv()
        add_rows(inner.at[m, 0], [piece.at[m, 1], inbox.at[m, 0]])
        one = remote(inner.at[m, 0], inbox.at[m, 4], dp_peer(1))
        first[1].wait_recv()
        add_rows(inner.at[m, 1], [piece.at[m, 3], inbox.at[m, 1]])
        two = remote(inner.at[m, 1], inbox.at[m, 5], dp_peer(2))
        return one, two

    def own_sums(m, first, second):
        first[2].wait_recv()
        second[0].wait_recv()
        add_rows(grads.at[m, :, width:2 * width], [piece.at[m, 0], inbox.at[m, 2], inbox.at[m, 4]])
        first[3].wait_recv()
        second[1].wait_recv()
        add_rows(grads.at[m, :, 2 * width:3 * width], [piece.at[m, 2], inbox.at[m, 3], inbox.at[m, 5]])

    def weight_rows(m, kind):
        cols = slice(kind * width, (kind + 1) * width)

        def one(n):
            part = mm(fulls[m][:, tile(n)], grads[m, :, cols], TN)
            acc[kind, tile(n), :] = part if m == 0 else acc[kind, tile(n), :] + part

        each(model // SEG, one)

    def input_rows(m):
        def block(r, out):
            def one(n):
                part = jnp.zeros((rows, SEG), F32)
                for kind in range(3):
                    part += mm(
                        grads[m, r * rows:(r + 1) * rows, kind * width:(kind + 1) * width],
                        weight[kind, tile(n), :],
                        NT,
                    )
                out[:, tile(n)] = part.astype(out.dtype)

            each(model // SEG, one)

        block(3, core_out.at[m, 0])
        hop3 = remote(core_out.at[m, 0], core_in.at[m, 0], {"tensor": near})
        block(1, core_out.at[m, 1])
        hop1 = remote(core_out.at[m, 1], core_in.at[m, 1], {"tensor": near})
        block(2, din.at[m])
        hop3.wait_recv()
        y_out[m] = (din[m] + core_in[m, 0].astype(F32)).astype(BF)
        hop = remote(y_out.at[m], y_in.at[m], {"tensor": far})
        block(0, din.at[m])
        return hop1, hop

    chunk = 32

    def input_norms(m, hops):
        hops[0].wait_recv()
        hops[1].wait_recv()

        def one(i):
            at = pl.ds(pl.multiple_of(i * chunk, chunk), chunk)
            dh1 = din[m, at] + core_in[m, 1, at].astype(F32) + y_in[m, at].astype(F32)
            values = x[m, at].astype(F32)
            center = values - jnp.mean(values, axis=-1, keepdims=True)
            inverse = lax.rsqrt(jnp.mean(center * center, axis=-1, keepdims=True) + EPSILON)
            normed = center * inverse
            small[0] += jnp.sum((dh1 * normed).reshape(chunk // 8, 8, model), axis=0)
            din[m, at] = dr1[m, at] + norm_backward(dh1 * pre[...], normed, inverse)

        each(rows // chunk, one)

    class Chain:
        def __init__(self, kind):
            self.kind, self.base, self.size, self.at, self.step = kind, 0, model, 0, 0
            self.copy = None

        def reduce_send(self):
            mask = bits[self.step]
            half = self.size // 2
            out = pl.ds(pl.multiple_of(self.base + (1 - bit_of(mask)) * half, 16), half)
            slot = pl.ds(self.at, half)
            stage[self.kind, slot, :] = acc[self.kind, out, :].astype(BF)
            self.copy = remote(stage.at[self.kind, slot, :], arrived.at[self.kind, slot, :], dp_peer(mask))
            self.base, self.size = self.base + bit_of(mask) * half, half

        def reduce_wait(self):
            self.copy.wait_recv()
            mine = pl.ds(pl.multiple_of(self.base, 16), self.size)
            total = acc[self.kind, mine, :] + arrived[self.kind, pl.ds(self.at, self.size), :].astype(F32)
            self.at += self.size
            self.step += 1
            if self.step < len(bits):
                acc[self.kind, mine, :] = total
            else:
                res[self.kind, mine, :] = total.astype(BF)

        def gather_send(self):
            self.step -= 1
            mask = bits[self.step]
            mine = pl.ds(pl.multiple_of(self.base, 16), self.size)
            self.copy = remote(res.at[self.kind, mine, :], res.at[self.kind, mine, :], dp_peer(mask))
            self.base, self.size = self.base - bit_of(mask) * self.size, 2 * self.size

        def gather_wait(self):
            self.copy.wait_recv()

    for m in range(MICRO):
        grads[m, :, 0:width] = dqs[m][...]
    small[...] = jnp.zeros_like(small)
    small[1:4] = mid_gains[...].reshape(3, 8, model)
    small[4, :, 0:width] = head0[...] + head1[...]

    first0 = first_sends(0)
    weight_rows(0, 0)
    weight_rows(1, 0)
    second0 = second_sends(0, first0)
    first1 = first_sends(1)
    query = Chain(0)
    query.reduce_send()
    own_sums(0, first0, second0)
    hops0 = input_rows(0)
    second1 = second_sends(1, first1)
    weight_rows(0, 1)
    weight_rows(0, 2)
    query.reduce_wait()
    query.reduce_send()
    input_norms(0, hops0)
    own_sums(1, first1, second1)
    weight_rows(1, 1)
    key = Chain(1)
    key.reduce_send()
    weight_rows(1, 2)
    value = Chain(2)
    value.reduce_send()
    hops1 = input_rows(1)
    query.reduce_wait()
    chains = [query, key, value]
    for _ in range(len(bits) - 2):
        query.reduce_send()
        query.reduce_wait()
    query.gather_send()
    for step in range(len(bits)):
        for chain in (key, value):
            chain.reduce_wait()
            if step + 1 < len(bits):
                chain.reduce_send()
        if step == 0:
            input_norms(1, hops1)
            totals = jnp.zeros((8, model), F32)
            place_row = lax.broadcasted_iota(jnp.int32, (8, model), 0)
            for i in range(5):
                totals = jnp.where(place_row == i, jnp.sum(small[i], axis=0, keepdims=True), totals)
            small[0] = totals
            small_copy = remote(small.at[0], small_in.at[0], {"tensor": near})
    key.gather_send()
    value.gather_send()
    place_row = lax.broadcasted_iota(jnp.int32, (8, model), 0)
    small_copy.wait_recv()
    small[1] = small[0] + jnp.where(place_row < 3, small_in[0], 0.0)
    small_copy = remote(small.at[1], small_in.at[1], {"tensor": far})
    small_copy.wait_recv()
    small[2] = small[1] + jnp.where(place_row < 3, small_in[1], 0.0)
    small_step = [0]

    def small_send():
        i = small_step[0]
        return remote(small.at[2 + i], small_in.at[2 + i], dp_peer(bits[i]))

    small_copy = small_send()
    for step in range(len(bits)):
        small_copy.wait_recv()
        small[3 + step] = small[2 + step] + small_in[2 + step]
        small_step[0] += 1
        if step + 1 < len(bits):
            small_copy = small_send()
        for chain in chains:
            chain.gather_wait()
            if step + 1 < len(bits):
                chain.gather_send()
    small_out[...] = small[2 + len(bits)]

    def widen(n):
        for kind in range(3):
            grad[kind, tile(n), :] = res[kind, tile(n), :].astype(F32)

    each(model // SEG, widen)
    for copy in pending:
        copy.wait_send()


def finish_call(dqs, dks, dvs, fulls, x, dr1, weight, pre, mid_gains, heads):
    micro, rows, model = x.shape
    tokens, width = dqs[0].shape
    bits = tuple(2**b for b in range(lax.axis_size("dp").bit_length() - 1))
    vmem = pl.BlockSpec(memory_space=pltpu.VMEM)
    return pl.pallas_call(
        partial(finish, bits),
        out_shape=(
            jax.ShapeDtypeStruct((micro, rows, model), F32),
            jax.ShapeDtypeStruct((3, model, width), F32),
            jax.ShapeDtypeStruct((8, model), F32),
        ),
        in_specs=[vmem] * 2 + [HBM] * 4 + [vmem] * 9,
        out_specs=(vmem,) * 3,
        scratch_shapes=[
            pltpu.VMEM((micro, 4, tokens, width), BF),
            pltpu.VMEM((micro, 6, tokens, width), BF),
            pltpu.VMEM((micro, 2, tokens, width), BF),
            pltpu.VMEM((micro, tokens, 3 * width), BF),
            pltpu.VMEM((3, model, width), F32),
            pltpu.VMEM((3, model, width), BF),
            pltpu.VMEM((3, model, width), BF),
            pltpu.VMEM((3, model, width), BF),
            pltpu.VMEM((micro, 2, rows, model), BF),
            pltpu.VMEM((micro, 2, rows, model), BF),
            pltpu.VMEM((micro, rows, model), BF),
            pltpu.VMEM((micro, rows, model), BF),
            pltpu.VMEM((3 + len(bits) + 2, 8, model), F32),
            pltpu.VMEM((2 + len(bits), 8, model), F32),
            pltpu.SemaphoreType.DMA((24 + 7 * len(bits),)),
            pltpu.SemaphoreType.DMA((24 + 7 * len(bits),)),
            pltpu.SemaphoreType.DMA((8,)),
        ],
        compiler_params=pltpu.CompilerParams(
            collective_id=1, has_side_effects=True, vmem_limit_bytes=56 << 20
        ),
        cost_estimate=pl.CostEstimate(flops=60 * 10**9, transcendentals=0, bytes_accessed=30 << 20),
        name="finish",
    )(*dqs, *dks, *dvs, *fulls, x, dr1, weight, pre, mid_gains, *heads)


def body(
    block_input,
    cotangent,
    parent,
    pre_attn_gain,
    qkv_weight,
    head_scale,
    out_weight,
    post_attn_gain,
    pre_ffn_gain,
    fc1_weight,
    ffn_norm_gain,
    fc2_weight,
):
    trees = parent.shape[1]
    group = lax.axis_size("dp") // trees
    member = lax.axis_index("dp") % group
    tree_index = lax.axis_index("dp") // group
    shard = lax.axis_index("tensor")
    row_count = block_input.shape[1]
    tokens = cotangent.shape[1]
    width = qkv_weight.shape[2]
    parents = parent.reshape(-1)
    scale_row = jnp.repeat(head_scale, HEAD_DIM)[None, :]

    def place(micro):
        return jnp.stack([(micro * trees + tree_index) * SEGS, member, shard]).astype(jnp.int32)

    state = [dict() for _ in range(MICRO)]
    for micro, s in enumerate(state):
        s["rows"] = block_input[micro].astype(F32)
        s["n1"], s["i1"] = normalize(s["rows"])
        s["full1"] = gather_rows((s["n1"] * pre_attn_gain).astype(BF))
    for micro, s in enumerate(state):
        own_k = mm(s["full1"], qkv_weight[1]).astype(BF)
        own_v = mm(s["full1"], qkv_weight[2]).astype(BF)
        k1, k2 = swap(own_k, "dp", 1), swap(own_k, "dp", 2)
        v1, v2 = swap(own_v, "dp", 1), swap(own_v, "dp", 2)
        k3, v3 = swap(k1, "dp", 2), swap(v2, "dp", 1)
        s["keys"] = (own_k, k1, k2, k3)
        s["values"] = (own_v, v1, v2, v3)
        s["q"] = mm(s["full1"], qkv_weight[0]).astype(BF)
    for micro, s in enumerate(state):
        s["o"], s["os"], s["lse"] = attention(
            place(micro), parents, s["q"], s["keys"], s["values"], scale_row
        )
    z, dc, h2, du, dos, dr1, f_own, f_far, mid_gains = middle_call(
        [s["os"] for s in state],
        block_input,
        cotangent,
        fc1_weight,
        fc2_weight,
        out_weight,
        post_attn_gain[None],
        pre_ffn_gain[None],
        ffn_norm_gain[None],
    )
    over = (((0, 1), (0, 1)), ((), ()))
    fc1_grad = lax.dot_general(h2, dc, over, preferred_element_type=F32).astype(BF)
    fc2_grad = lax.dot_general(z, cotangent, over, preferred_element_type=F32).astype(BF)
    out_grad = lax.dot_general(
        jnp.stack([s["os"] for s in state]), du, over, preferred_element_type=F32
    ).astype(BF)
    early = (fc1_grad, jnp.concatenate([fc2_grad, out_grad], axis=0))
    early, dos = lax.optimization_barrier((early, dos))
    early = lax.psum(early, "dp")
    f_got = swap(f_far, "tensor", 2)
    outputs = (f_own + f_got.astype(F32)).astype(BF)
    backs = [
        attention_grad(
            place(m), parents, s["q"], dos[m], s["o"], s["lse"], scale_row, s["keys"], s["values"]
        )
        for m, s in enumerate(state)
    ]
    din, qkv_grad, small = finish_call(
        [b[0] for b in backs],
        [b[1] for b in backs],
        [b[2] for b in backs],
        [s["full1"] for s in state],
        block_input,
        dr1,
        qkv_weight,
        pre_attn_gain[None],
        mid_gains,
        [b[3] for b in backs],
    )
    head_grad = small[4, 0:width].reshape(-1, HEAD_DIM).sum(-1)
    return (
        outputs,
        din,
        small[0],
        qkv_grad,
        head_grad,
        early[1][fc2_weight.shape[0]:].astype(F32),
        small[1],
        small[2],
        early[0].astype(F32),
        small[3],
        early[1][:fc2_weight.shape[0]].astype(F32),
    )


def solution(mesh):
    in_specs = (
        P(None, ("dp", "tensor"), None),
        P(None, "dp", None),
        P(),
        P(),
        P(None, None, "tensor"),
        P("tensor"),
        P("tensor", None),
        P(),
        P(),
        P(None, "tensor"),
        P("tensor"),
        P("tensor", None),
    )
    out_specs = (
        P(None, ("dp", "tensor"), None),
        P(None, ("dp", "tensor"), None),
        P(),
        P(None, None, "tensor"),
        P("tensor"),
        P("tensor", None),
        P(),
        P(),
        P(None, "tensor"),
        P("tensor"),
        P("tensor", None),
    )
    return jax.shard_map(body, mesh=mesh, in_specs=in_specs, out_specs=out_specs, check_vma=False)
```

```python
from functools import partial

import jax
import jax.numpy as jnp
from jax import lax
from jax.experimental import pallas as pl
from jax.experimental.pallas import tpu as pltpu
from jax.sharding import PartitionSpec as P

HEAD_DIM = 64
FFN = 4096
SEG = 256
SEGS = 16
DEPTH = 5
MICRO = 2

EPSILON = 1e-05
NEGATIVE = -1e30
F32 = jnp.float32
BF = jnp.bfloat16
NN = (((1,), (0,)), ((), ()))
NT = (((1,), (1,)), ((), ()))
TN = (((0,), (0,)), ((), ()))


def mm(a, b, dims=NN):
    return lax.dot_general(a, b, dims, preferred_element_type=F32)


def swap(value, axis, mask):
    return lax.ppermute(value, axis, [(i, i ^ mask) for i in range(lax.axis_size(axis))])


def normalize(values):
    center = values - jnp.mean(values, axis=-1, keepdims=True)
    inverse = lax.rsqrt(jnp.mean(center * center, axis=-1, keepdims=True) + EPSILON)
    return (center * inverse, inverse)


def norm_backward(grad_hat, normed, inverse):
    mean_grad = jnp.mean(grad_hat, axis=-1, keepdims=True)
    mean_cross = jnp.mean(grad_hat * normed, axis=-1, keepdims=True)
    return inverse * (grad_hat - mean_grad - normed * mean_cross)


def climb(parents, base, seg):
    found = []
    current = seg
    count = jnp.int32(0)
    for _ in range(DEPTH):
        up = parents[base + current]
        valid = up >= 0
        count = count + valid.astype(jnp.int32)
        current = jnp.where(valid, up, current)
        found.append(current)
    return count, found


def place_of(seg, per, member, shard):
    return ((seg // per) ^ member) * per + ((seg % per) ^ shard)


def attend_backward(micro, place, parents, q_ref, dos_ref, o_ref, lse_ref, scale_ref, keys, values, *rest):
    dq_ref, dks, dvs, sg_ref = rest[0], rest[1:5], rest[5:9], rest[9]
    key_tree, value_tree, acc, dqt, sems = rest[10:]
    step = pl.program_id(0)
    width = q_ref.shape[1]
    heads = width // HEAD_DIM
    tokens = keys.shape[2]
    per = tokens // SEG
    base, member, shard = place[0], place[1], place[2]

    @pl.when(step == 0)
    def _():
        copies = [
            pltpu.make_async_copy(keys.at[micro], key_tree, sems.at[0]),
            pltpu.make_async_copy(values.at[micro], value_tree, sems.at[1]),
        ]
        for copy in copies:
            copy.start()
        acc[...] = jnp.zeros_like(acc)
        sg_ref[...] = jnp.zeros_like(sg_ref)
        for copy in copies:
            copy.wait()

    dos = dos_ref[...].astype(F32)
    cross = dos * o_ref[...]
    sg_ref[...] += jnp.sum(cross.reshape(SEG // 8, 8, width), axis=0)
    scale = scale_ref[...]
    go = (dos * scale).astype(BF)
    cross_t = jnp.transpose(cross * scale)
    lane = lax.broadcasted_iota(jnp.int32, (SEG, width), 1) // HEAD_DIM
    q = q_ref[...] * BF(HEAD_DIM ** -0.5)
    zero = jnp.zeros_like(q)
    q_heads = [jnp.where(lane == h, q, zero) for h in range(heads)]
    g_heads = [jnp.where(lane == h, go, zero) for h in range(heads)]
    deltas = [
        jnp.sum(cross_t[h * HEAD_DIM:(h + 1) * HEAD_DIM], axis=0, keepdims=True) for h in range(heads)
    ]
    lses = [lse_ref[0, h:h + 1, :] for h in range(heads)]
    dqt[...] = jnp.zeros_like(dqt)

    def block(start, own):
        rows = pl.ds(pl.multiple_of(start, SEG), SEG)
        part = pl.ds(pl.multiple_of(start % tokens, SEG), SEG)
        k = key_tree[start // tokens, part, :]
        v = value_tree[start // tokens, part, :]
        kt = jnp.transpose(k)
        dk = jnp.zeros((SEG, width), F32)
        dv = jnp.zeros((SEG, width), F32)
        for h in range(heads):
            p = jnp.exp(mm(k, q_heads[h], NT) - lses[h])
            if own:
                key_row = lax.broadcasted_iota(jnp.int32, (SEG, SEG), 0)
                query_col = lax.broadcasted_iota(jnp.int32, (SEG, SEG), 1)
                p = jnp.where(key_row <= query_col, p, 0.0)
            dv += mm(p.astype(BF), g_heads[h])
            dp = mm(v, g_heads[h], NT)
            ds = (p * (dp - deltas[h])).astype(BF)
            dk += mm(ds, q_heads[h])
            dqt[pl.ds(h * HEAD_DIM, HEAD_DIM), :] += mm(kt[h * HEAD_DIM:(h + 1) * HEAD_DIM], ds)
        acc[rows, 0:width] += dk
        acc[rows, width:2 * width] += dv

    def upward(j, current):
        up = parents[base + current]
        block(place_of(up, per, member, shard) * SEG, False)
        return up

    seg = member * per + (step ^ shard)
    count, _ = climb(parents, base, seg)
    lax.fori_loop(0, count, upward, seg)
    block(step * SEG, True)
    dq_ref[...] = (jnp.transpose(dqt[...]) * HEAD_DIM ** -0.5).astype(BF)

    @pl.when(step == pl.num_programs(0) - 1)
    def _():
        for r in range(4):
            dks[r][...] = acc[r * tokens:(r + 1) * tokens, 0:width].astype(BF)
            dvs[r][...] = acc[r * tokens:(r + 1) * tokens, width:2 * width].astype(BF)


ROW = lambda i, *s: (i, 0)
FIX = lambda i, *s: (0, 0)
HBM = pl.BlockSpec(memory_space=pl.ANY)


def attention_grad(micro, place, parents, q, dos, o, lse, scale_row, keys, values):
    tokens, width = q.shape
    segs = tokens // SEG
    piece = jax.ShapeDtypeStruct((tokens, width), BF)
    whole = pl.BlockSpec((tokens, width), FIX)
    return pl.pallas_call(
        partial(attend_backward, micro),
        out_shape=(piece,) * 9 + (jax.ShapeDtypeStruct((8, width), F32),),
        grid_spec=pltpu.PrefetchScalarGridSpec(
            num_scalar_prefetch=2,
            grid=(segs,),
            in_specs=[
                pl.BlockSpec((SEG, width), ROW),
                pl.BlockSpec((SEG, width), ROW),
                pl.BlockSpec((SEG, width), ROW),
                pl.BlockSpec((1, 8, SEG), lambda i, *s: (i, 0, 0)),
                pl.BlockSpec((1, width), FIX),
            ]
            + [HBM] * 2,
            out_specs=[pl.BlockSpec((SEG, width), ROW)] + [whole] * 8 + [pl.BlockSpec((8, width), FIX)],
            scratch_shapes=[
                pltpu.VMEM((4, tokens, width), BF),
                pltpu.VMEM((4, tokens, width), BF),
                pltpu.VMEM((4 * tokens, 2 * width), F32),
                pltpu.VMEM((width, SEG), F32),
                pltpu.SemaphoreType.DMA((2,)),
            ],
        ),
        compiler_params=pltpu.CompilerParams(
            dimension_semantics=("arbitrary",), vmem_limit_bytes=61 << 20
        ),
        cost_estimate=pl.CostEstimate(flops=4 * 10**9, transcendentals=0, bytes_accessed=12 << 20),
        name="attend_backward",
    )(place, parents, q, dos, o, lse, scale_row, keys, values)


def gelu_parts(c):
    root = 0.7978845608028654
    square = c * c
    tanh = jnp.tanh(root * (c + 0.044715 * (square * c)))
    act = 0.5 * c * (1.0 + tanh)
    slope = 0.5 * (1.0 + tanh) + 0.5 * c * (1.0 - tanh * tanh) * (root * (1.0 + 3 * 0.044715 * square))
    return act, slope


def other(shard, mask):
    near = shard + 1 - 2 * (shard % 2)
    return {0: shard, 1: near, 2: (shard + 2) % 4, 3: (near + 2) % 4}[mask]


def xor4(a, b):
    return 2 * lax.rem(lax.div(a, 2) + lax.div(b, 2), 2) + lax.rem(a + b, 2)


def opening(
    parents, x, gain, weight, scale_ref, out_w,
    q0, q1, o0, o1, os0, os1, lse0, lse1, mixed, full_hbm, kt_hbm, vt_hbm,
    full, kt0, kt1, vt0, vt1, picked_k, picked_v, core_out, core_in, y_out, y_in, send, recv, local,
):
    shard = lax.axis_index("tensor")
    index = lax.axis_index("dp")
    near, far = {"tensor": other(shard, 1)}, {"tensor": other(shard, 2)}
    beside, beyond = [{"dp": index + mask - 2 * mask * ((index // mask) % 2)} for mask in (1, 2)]
    rows, model = x.shape[1], x.shape[2]
    width = q0.shape[1]
    heads = width // HEAD_DIM
    tokens = 4 * rows
    per = tokens // SEG
    member, tree = index % 4, index // 4
    trees = parents.shape[0] // (MICRO * SEGS)
    qs, os_, oss, lses = (q0, q1), (o0, o1), (os0, os1), (lse0, lse1)
    kts, vts = (kt0, kt1), (vt0, vt1)
    used = [0]
    pending = []

    def remote(src, dst, target):
        i = used[0]
        used[0] += 1
        copy = pltpu.make_async_remote_copy(
            src_ref=src, dst_ref=dst, send_sem=send.at[i], recv_sem=recv.at[i],
            device_id=target, device_id_type=pl.DeviceIdType.MESH,
        )
        copy.start()
        pending.append(copy)
        return copy

    stores = []

    def store(src, dst):
        copy = pltpu.make_async_copy(src, dst, local.at[len(stores)])
        copy.start()
        stores.append(copy)

    def each(count, fn):
        lax.fori_loop(0, count, lambda i, c: (fn(i), c)[1], 0)

    barrier = pltpu.get_barrier_semaphore()
    for target in (near, far, beside, beyond):
        pl.semaphore_signal(barrier, inc=1, device_id=target, device_id_type=pl.DeviceIdType.MESH)

    chunk = 32

    def norms(m):
        def one(i):
            at = pl.ds(pl.multiple_of(i * chunk, chunk), chunk)
            values = x[m, at].astype(F32)
            center = values - jnp.mean(values, axis=-1, keepdims=True)
            inverse = lax.rsqrt(jnp.mean(center * center, axis=-1, keepdims=True) + EPSILON)
            full[m, 0, at] = (center * inverse * gain[...]).astype(BF)

        each(rows // chunk, one)

    def spread(m):
        return remote(full.at[m, 0], full.at[m, 2], far), remote(full.at[m, 0], full.at[m, 1], near)

    def project(m, first):
        for r in (first, first + 1):
            kts[m][r] = mm(full[m, r], weight[1]).astype(BF)
            vts[m][r] = mm(full[m, r], weight[2]).astype(BF)

    def queries(m):
        for r in range(4):
            qs[m][r * rows:(r + 1) * rows, :] = mm(full[m, r], weight[0]).astype(BF)

    def piece(ref, r, half):
        return ref.at[pl.ds(4 * r + 2 * half, 2)]

    def share(m, half):
        k, v = kts[m], vts[m]
        return [
            remote(piece(k, 0, half), piece(k, 1, half), beside),
            remote(piece(v, 0, half), piece(v, 2, half), beyond),
            remote(piece(k, 0, half), piece(k, 2, half), beyond),
            remote(piece(v, 0, half), piece(v, 1, half), beside),
        ]

    def forward(m, half, copies):
        copies[0].wait_recv()
        one = remote(piece(kts[m], 1, half), piece(kts[m], 3, half), beyond)
        copies[1].wait_recv()
        return copies[2:] + [one, remote(piece(vts[m], 2, half), piece(vts[m], 3, half), beside)]

    def settle(*groups):
        for copies in groups:
            for copy in copies:
                copy.wait_recv()

    def attend(m, step):
        seg = member * per + xor4(step, shard)
        count, found = climb(parents, (m * trees + tree) * SEGS, seg)
        past = DEPTH * SEG
        for slot in range(DEPTH):
            s = found[slot]
            at = 4 * xor4(lax.div(s, 4), member) + xor4(lax.rem(s, 4), shard)
            picked_k[slot * SEG:(slot + 1) * SEG, :] = kts[m][at]
            picked_v[slot * SEG:(slot + 1) * SEG, :] = vts[m][at]
        here = pl.ds(pl.multiple_of(step * SEG, SEG), SEG)
        picked_k[past:past + SEG, :] = kts[m][step]
        picked_v[past:past + SEG, :] = vts[m][step]
        lane = lax.broadcasted_iota(jnp.int32, (SEG, width), 1) // HEAD_DIM
        row = lax.broadcasted_iota(jnp.int32, (SEG, SEG), 0)
        col = lax.broadcasted_iota(jnp.int32, (SEG, SEG), 1)
        slot_of = lax.broadcasted_iota(jnp.int32, (1, past), 1) // SEG
        bias = jnp.where(slot_of < count, 0.0, NEGATIVE).astype(F32)
        q = qs[m][here, :] * BF(HEAD_DIM ** -0.5)
        lse_lane = lax.broadcasted_iota(jnp.int32, (SEG, 128), 1)
        lse_all = jnp.zeros((SEG, 128), F32)
        out = jnp.zeros((SEG, width), F32)
        for head in range(heads):
            qh = jnp.where(lane == head, q, jnp.zeros_like(q))
            s_past = mm(qh, picked_k[0:past, :], NT) + bias
            s_own = jnp.where(col <= row, mm(qh, picked_k[past:past + SEG, :], NT), NEGATIVE)
            top = jnp.maximum(
                jnp.max(s_past, axis=1, keepdims=True), jnp.max(s_own, axis=1, keepdims=True)
            )
            p_past = jnp.exp(s_past - top)
            p_own = jnp.exp(s_own - top)
            total = jnp.sum(p_past, axis=1, keepdims=True) + jnp.sum(p_own, axis=1, keepdims=True)
            got = mm(p_past.astype(BF), picked_v[0:past, :]) + mm(p_own.astype(BF), picked_v[past:past + SEG, :])
            out = jnp.where(lane == head, got / total, out)
            lse_all = jnp.where(lse_lane == head, top + jnp.log(total), lse_all)
        os_[m][here, :] = out
        oss[m][here, :] = (out * scale_ref[...]).astype(BF)
        lses[m][pl.ds(step, 1)] = jnp.transpose(lse_all)[0:8].reshape(1, 8, SEG)

    norms(0)
    pl.semaphore_wait(barrier, 4)
    far0, near0 = spread(0)
    norms(1)
    far1, near1 = spread(1)
    near0.wait_recv()
    project(0, 0)
    a0 = share(0, 0)
    near1.wait_recv()
    project(1, 0)
    far0.wait_recv()
    cross0 = remote(full.at[0, 2], full.at[0, 3], near)
    cross0.wait_recv()
    project(0, 2)
    b0 = share(0, 1)
    a0 = forward(0, 0, a0)
    queries(0)
    far1.wait_recv()
    cross1 = remote(full.at[1, 2], full.at[1, 3], near)
    b0 = forward(0, 1, b0)
    a1 = share(1, 0)
    cross1.wait_recv()
    project(1, 2)
    b1 = share(1, 1)
    queries(1)
    for m in range(MICRO):
        store(full.at[m], full_hbm.at[m])
    settle(a0, b0)
    lax.fori_loop(0, 2, lambda i, c: (attend(0, i), c)[1], 0)
    a1 = forward(1, 0, a1)
    lax.fori_loop(2, 4, lambda i, c: (attend(0, i), c)[1], 0)
    b1 = forward(1, 1, b1)

    def mix(r):
        return mm(os0[r * rows:(r + 1) * rows, :], out_w[...])

    core_out[0] = mix(3).astype(BF)
    hop3 = remote(core_out.at[0], core_in.at[0], near)
    core_out[1] = mix(1).astype(BF)
    hop1 = remote(core_out.at[1], core_in.at[1], near)
    mixed[...] = mix(2)
    hop3.wait_recv()
    y_out[...] = (mixed[...] + core_in[0].astype(F32)).astype(BF)
    hop2 = remote(y_out, y_in, far)
    hop1.wait_recv()
    mixed[...] = mix(0) + core_in[1].astype(F32)
    store(kt0, kt_hbm.at[0])
    store(vt0, vt_hbm.at[0])
    settle(a1, b1)
    store(kt1, kt_hbm.at[1])
    store(vt1, vt_hbm.at[1])
    lax.fori_loop(0, 4, lambda i, c: (attend(1, i), c)[1], 0)
    hop2.wait_recv()
    mixed[...] = mixed[...] + y_in[...].astype(F32)
    for copy in pending:
        copy.wait_send()
    for copy in stores:
        copy.wait()


def opening_call(parents, x, gain, weight, scale_row, out_w):
    micro, rows, model = x.shape
    width = weight.shape[2]
    tokens = 4 * rows
    vmem = pl.BlockSpec(memory_space=pltpu.VMEM)
    narrow = jax.ShapeDtypeStruct((tokens, width), BF)
    narrow_wide = jax.ShapeDtypeStruct((tokens, width), F32)
    tops = jax.ShapeDtypeStruct((tokens // SEG, 8, SEG), F32)
    trees = jax.ShapeDtypeStruct((micro, 4 * tokens // SEG, SEG, width), BF)
    return pl.pallas_call(
        opening,
        out_shape=(
            narrow, narrow, narrow_wide, narrow_wide, narrow, narrow, tops, tops,
            jax.ShapeDtypeStruct((rows, model), F32),
            jax.ShapeDtypeStruct((micro, 4, rows, model), BF),
            trees, trees,
        ),
        in_specs=[pl.BlockSpec(memory_space=pltpu.SMEM)] + [vmem] * 5,
        out_specs=(vmem,) * 9 + (HBM,) * 3,
        scratch_shapes=[pltpu.VMEM((micro, 4, rows, model), BF)]
        + [pltpu.VMEM((4 * tokens // SEG, SEG, width), BF)] * 4
        + [pltpu.VMEM(((DEPTH + 1) * SEG, width), BF)] * 2
        + [pltpu.VMEM((2, rows, model), BF)] * 2
        + [pltpu.VMEM((rows, model), BF)] * 2
        + [
            pltpu.SemaphoreType.DMA((36,)),
            pltpu.SemaphoreType.DMA((36,)),
            pltpu.SemaphoreType.DMA((8,)),
        ],
        compiler_params=pltpu.CompilerParams(
            collective_id=2, has_side_effects=True, vmem_limit_bytes=61 << 20
        ),
        cost_estimate=pl.CostEstimate(flops=60 * 10**9, transcendentals=0, bytes_accessed=20 << 20),
        name="opening",
    )(parents, x, gain, weight, scale_row, out_w)


def middle(
    bits, os0, os1, mixed0, x, g_hbm, fc1_hbm, fc2_hbm, out_w, post, pre, wide,
    du_hbm, dos, dr1, f_own, f_far, gains, shares,
    fc1, fc2, gd, du, act, slz, dzc, full, core_out, core_in, y_out, y_in, nu, inv, st_out, st_in, sums, cols,
    arrived, send, recv, local,
):
    shard = lax.axis_index("tensor")
    index = lax.axis_index("dp")

    def bit_of(mask):
        return (index // mask) % 2

    def dp_peer(mask):
        return {"dp": index + mask - 2 * mask * bit_of(mask)}

    peers = [other(shard, k) for k in range(4)]
    rows = x.shape[1]
    model = x.shape[2]
    hidden = fc1.shape[1]
    parts = hidden // SEG
    used = [0]
    pending = []

    def remote(src, dst, target):
        i = used[0]
        used[0] += 1
        if not isinstance(target, dict):
            target = {"tensor": peers[target]}
        copy = pltpu.make_async_remote_copy(
            src_ref=src, dst_ref=dst, send_sem=send.at[i], recv_sem=recv.at[i],
            device_id=target, device_id_type=pl.DeviceIdType.MESH,
        )
        copy.start()
        pending.append(copy)
        return copy

    stored = [0]
    stores = []

    def store(src, dst):
        i = stored[0]
        stored[0] += 1
        copy = pltpu.make_async_copy(src, dst, local.at[i])
        copy.start()
        stores.append(copy)

    def fetch(src, dst):
        i = stored[0]
        stored[0] += 1
        copy = pltpu.make_async_copy(src, dst, local.at[i])
        copy.start()
        return copy

    got_fc2 = fetch(fc2_hbm, fc2)
    got_g = [
        [fetch(g_hbm.at[m, pl.ds(peers[r] * rows, rows), :], gd.at[m, r]) for r in range(4)] for m in range(MICRO)
    ]
    got_fc1 = fetch(fc1_hbm, fc1)
    barrier = pltpu.get_barrier_semaphore()
    targets = [{"tensor": peers[mask]} for mask in (1, 2, 3)] + [dp_peer(mask) for mask in bits]
    for target in targets:
        pl.semaphore_signal(barrier, inc=1, device_id=target, device_id_type=pl.DeviceIdType.MESH)
    pl.semaphore_wait(barrier, len(targets))
    gains[...] = jnp.zeros_like(gains)

    def each(count, fn):
        lax.fori_loop(0, count, lambda i, c: (fn(i), c)[1], 0)

    def tile(n):
        return pl.ds(pl.multiple_of(n * SEG, SEG), SEG)

    def merge(value):
        return value.reshape((-1,) + value.shape[2:])

    def reuse(*groups):
        for copies in groups:
            for copy in copies if isinstance(copies, tuple) else (copies,):
                copy.wait_send()
                pending[:] = [other_copy for other_copy in pending if other_copy is not copy]

    def first_hop(kind, m, block, out):
        block(3, core_out.at[m, 0])
        hop3 = remote(core_out.at[m, 0], core_in.at[kind, m, 0], 1)
        block(1, core_out.at[m, 1])
        hop1 = remote(core_out.at[m, 1], core_in.at[kind, m, 1], 1)
        block(2, None)
        block(0, out)
        return hop3, hop1

    chunk = 32

    def chunks(fn):
        each(rows // chunk, lambda i: fn(pl.ds(pl.multiple_of(i * chunk, chunk), chunk)))

    def add_far(kind, m):
        def one(at):
            y_out[m, at] = (sums_far[m][at] + core_in[kind, m, 0, at].astype(F32)).astype(BF)

        chunks(one)

    sums_far = [f_own.at[m] for m in range(MICRO)]
    def mixed_block():
        def block(r, out):
            part = mm(os1[r * rows:(r + 1) * rows, :], out_w[...])
            if r == 2:
                sums_far[1][...] = part
            else:
                out[...] = part.astype(out.dtype)

        return block

    hops = first_hop(0, 1, mixed_block(), nu.at[1])
    hops[0].wait_recv()
    add_far(0, 1)
    far_hop = remote(y_out.at[1], y_in.at[0, 1], 2)
    def project_grad(m):
        for r in range(4):
            got_g[m][r].wait()

        def one(i):
            r, n = i // parts, i % parts
            dzc[m, pl.ds(pl.multiple_of(r * rows, rows), rows), tile(n)] = mm(gd[m, r], fc2[tile(n), :], NT).astype(BF)

        each(4 * parts, one)

    def own_sum(kind, m, base, at):
        return base + core_in[kind, m, 1, at].astype(F32) + y_in[kind, m, at].astype(F32)

    def norm_two(m, at, residual):
        center = residual - jnp.mean(residual, axis=-1, keepdims=True)
        inverse = lax.rsqrt(jnp.mean(center * center, axis=-1, keepdims=True) + EPSILON)
        return center * inverse, inverse

    def forward_norms(m):
        if m:
            hops[1].wait_recv()
            far_hop.wait_recv()

        def one(at):
            mixed, inverse = norm_two(m, at, own_sum(0, m, nu[m, at], at) if m else mixed0[at, :])
            nu[m, at] = mixed
            inv[m, at] = jnp.broadcast_to(inverse, (chunk, 128))
            residual = x[m, at].astype(F32) + mixed * post[...]
            normed, _ = norm_two(m, at, residual)
            full[m, 0, at] = (normed * pre[...]).astype(BF)

        chunks(one)

    def spread(m, buf):
        return remote(buf.at[m, 0], buf.at[m, 2], 2), remote(buf.at[m, 0], buf.at[m, 1], 1)

    def ffn_forward(m, r):
        sums[...] = jnp.zeros_like(sums)

        def one(n):
            value, slope = gelu_parts(mm(full[m, r], fc1[:, tile(n)]))
            act[m, r * rows:(r + 1) * rows, tile(n)] = value
            slz[m, r, :, tile(n)] = slope.astype(BF)
            dna = dzc[m, pl.ds(pl.multiple_of(r * rows, rows), rows), tile(n)].astype(F32) * wide[:, tile(n)]
            for i, term in enumerate((value, value * value, dna, dna * value)):
                sums[i] += term[:, 0:128] + term[:, 128:256]

        each(parts, one)
        lane = lax.broadcasted_iota(jnp.int32, (rows, 128), 1)
        merged = jnp.zeros((rows, 128), F32)
        for i in range(4):
            merged = jnp.where(lane == i, jnp.sum(sums[i], axis=-1, keepdims=True), merged)
        st_out[m, :, r * rows:(r + 1) * rows] = jnp.transpose(merged)[0:8]

    def send_stats(m):
        return [remote(st_out.at[m], st_in.at[m, mask - 1], mask) for mask in (1, 2, 3)]

    def ffn_backward_rows(m, r):
        total = st_out[m, :, r * rows:(r + 1) * rows]
        for mask in (1, 2, 3):
            b = r ^ mask
            total = total + st_in[m, mask - 1, :, b * rows:(b + 1) * rows]
        cols[0:8, :] = total * (1.0 / FFN)
        flipped = jnp.transpose(cols[...])
        mu, square, m_dna, m_cross = [flipped[:, i:i + 1] for i in range(4)]
        rw = lax.rsqrt(square - mu * mu + EPSILON)
        m_both = (m_cross - mu * m_dna) * rw

        def one(n):
            gain = wide[:, tile(n)]
            dz = dzc[m, pl.ds(pl.multiple_of(r * rows, rows), rows), tile(n)].astype(F32)
            na = (act[m, r * rows:(r + 1) * rows, tile(n)] - mu) * rw
            slope = slz[m, r, :, tile(n)].astype(F32)
            slz[m, r, :, tile(n)] = (na * gain).astype(BF)
            gains[16:24, tile(n)] += jnp.sum((dz * na).reshape(rows // 8, 8, SEG), axis=0)
            dzc[m, pl.ds(pl.multiple_of(r * rows, rows), rows), tile(n)] = (rw * (dz * gain - m_dna - na * m_both) * slope).astype(BF)

        each(parts, one)

    def grad_block(m):
        def block(r, out):
            ffn_backward_rows(m, r)
            if r == 2:
                out = sums_far[m]

            def one(n):
                out[:, tile(n)] = mm(dzc[m, r * rows:(r + 1) * rows, :], fc1[tile(n), :], NT).astype(out.dtype)

            each(model // SEG, one)

        return block

    def ffn_out_block(m):
        def block(r, out):
            def one(n):
                out[:, tile(n)] = mm(slz[m, r], fc2[:, tile(n)]).astype(out.dtype)

            each(model // SEG, one)

        return block

    def backward_norms(m, hop1, far_hop):
        hop1.wait_recv()
        far_hop.wait_recv()

        def one(at):
            dh2 = own_sum(1, m, dr1[m, at], at)
            mixed = nu[m, at]
            residual = x[m, at].astype(F32) + mixed * post[...]
            normed, inverse = norm_two(m, at, residual)
            gains[8:16, :] += jnp.sum((dh2 * normed).reshape(chunk // 8, 8, model), axis=0)
            grad = gd[m, 0, at].astype(F32) + norm_backward(dh2 * pre[...], normed, inverse)
            gains[0:8, :] += jnp.sum((grad * mixed).reshape(chunk // 8, 8, model), axis=0)
            dr1[m, at] = grad
            back = norm_backward(grad * post[...], mixed, inv[m, at][:, 0:1])
            du[m, 0, at] = back.astype(BF)

        chunks(one)

    def unmix(m, r):
        dos[m, r * rows:(r + 1) * rows, :] = mm(du[m, r], out_w[...], NT)

    forward_norms(0)
    far0, near0 = spread(0, full)
    got_fc2.wait()
    project_grad(0)
    got_fc1.wait()
    ffn_forward(0, 0)
    near0.wait_recv()
    ffn_forward(0, 1)
    project_grad(1)
    forward_norms(1)
    far1, near1 = spread(1, full)
    ffn_forward(1, 0)
    far0.wait_recv()
    cross0 = remote(full.at[0, 2], full.at[0, 3], 1)
    ffn_forward(0, 2)
    cross0.wait_recv()
    ffn_forward(0, 3)
    stats0 = send_stats(0)
    near1.wait_recv()
    ffn_forward(1, 1)
    far1.wait_recv()
    cross1 = remote(full.at[1, 2], full.at[1, 3], 1)
    ffn_forward(1, 2)
    for copy in stats0:
        copy.wait_recv()
    hop_a = first_hop(1, 0, grad_block(0), dr1.at[0])
    hop_a[0].wait_recv()
    add_far(1, 0)
    far_a = remote(y_out.at[0], y_in.at[1, 0], 2)
    cross1.wait_recv()
    ffn_forward(1, 3)
    stats1 = send_stats(1)

    def first_grad(m):
        def one(n):
            part = mm(merge(full[m, :, :, tile(n)]), dzc[m], TN)
            act[0, tile(n), :] = part if m == 0 else act[0, tile(n), :] + part

        each(parts, one)

    def second_grad(n):
        part = mm(merge(slz[0, :, :, tile(n)]), merge(gd[0]), TN)
        act[1, tile(n), :] = part + mm(merge(slz[1, :, :, tile(n)]), merge(gd[1]), TN)

    first_grad(0)
    for copy in stats1:
        copy.wait_recv()
    reuse(hops, far_hop)
    hop_b = first_hop(1, 1, grad_block(1), dr1.at[1])
    hop_b[0].wait_recv()
    add_far(1, 1)
    far_b = remote(y_out.at[1], y_in.at[1, 1], 2)
    backward_norms(0, hop_a[1], far_a)
    du_far0, du_near0 = spread(0, du)
    first_grad(1)
    group = hidden // (shares.shape[0] // 2)

    class Chain:
        def __init__(self, number):
            self.number, self.which = number, number // (hidden // group)
            self.start = (number % (hidden // group)) * group
            self.base, self.size, self.at, self.step = self.start, group, self.start, 0

        def send(self):
            mask = bits[self.step]
            half = self.size // 2
            away = self.base + (1 - bit_of(mask)) * half
            where = self.at

            def one(i):
                src = pl.ds(pl.multiple_of(away + i * 16, 16), 16)
                staged[self.which, pl.ds(pl.multiple_of(where + i * 16, 16), 16), :] = act[
                    self.which, src, :
                ].astype(BF)

            each(half // 16, one)
            slot = pl.ds(where, half)
            self.copy = remote(
                staged.at[self.which, slot, :], arrived.at[self.which, slot, :], dp_peer(mask)
            )
            self.base, self.size = self.base + bit_of(mask) * half, half

        def wait(self):
            self.copy.wait_recv()
            self.step += 1
            base, where, last = self.base, self.at, self.step == len(bits)

            def one(i):
                mine = pl.ds(pl.multiple_of(base + i * 16, 16), 16)
                total = act[self.which, mine, :] + arrived[
                    self.which, pl.ds(pl.multiple_of(where + i * 16, 16), 16), :
                ].astype(F32)
                if last:
                    shares[self.number, pl.ds(pl.multiple_of(i * 16, 16), 16), :] = total.astype(BF)
                else:
                    act[self.which, mine, :] = total

            each(self.size // 16, one)
            self.at += self.size

        def go(self):
            self.wait()
            if self.step < len(bits):
                self.send()

    chains = [Chain(i) for i in range(shares.shape[0])]
    half_chains = len(chains) // 2
    staged = dzc
    for chain in chains[:half_chains]:
        chain.send()
    per_chain = parts // half_chains
    for i, chain in enumerate(chains[half_chains:]):
        each(per_chain, lambda n: second_grad(n + i * per_chain))
        chain.send()
    backward_norms(1, hop_b[1], far_b)
    du_far1, du_near1 = spread(1, du)

    def ffn_out(m, hop_old):
        reuse(hop_old, ())
        block = ffn_out_block(m)
        block(3, core_out.at[m, 0])
        hop3 = remote(core_out.at[m, 0], core_in.at[0, m, 0], 1)
        block(1, core_out.at[m, 1])
        hop1 = remote(core_out.at[m, 1], core_in.at[0, m, 1], 1)
        block(2, f_own.at[m])
        hop3.wait_recv()

        def one(at):
            f_far[m, at] = (f_own[m, at] + core_in[0, m, 0, at].astype(F32)).astype(BF)

        chunks(one)
        block(0, f_own.at[m])
        hop1.wait_recv()

        def two(at):
            residual = x[m, at].astype(F32) + nu[m, at] * post[...]
            f_own[m, at] = residual + f_own[m, at] + core_in[0, m, 1, at].astype(F32)

        chunks(two)

    todo = [
        chains[turn - level]
        for turn in range(len(chains) + len(bits) - 1)
        for level in range(len(bits))
        if 0 <= turn - level < len(chains)
    ]

    def advance(count):
        for _ in range(min(count, len(todo))):
            todo.pop(0).go()

    slice_of = -(-len(todo) // 5)
    ffn_out(0, hop_a)
    unmix(0, 0)
    du_near0.wait_recv()
    unmix(0, 1)
    du_far0.wait_recv()
    du_cross0 = remote(du.at[0, 2], du.at[0, 3], 1)
    unmix(0, 2)
    advance(slice_of)
    du_cross0.wait_recv()
    unmix(0, 3)
    ffn_out(1, hop_b)
    advance(slice_of)
    unmix(1, 0)
    du_near1.wait_recv()
    unmix(1, 1)
    for r in range(4):
        store(du.at[0, r], du_hbm.at[0, pl.ds(r * rows, rows), :])
    du_far1.wait_recv()
    du_cross1 = remote(du.at[1, 2], du.at[1, 3], 1)
    unmix(1, 2)
    advance(slice_of)
    du_cross1.wait_recv()
    unmix(1, 3)
    for r in range(4):
        store(du.at[1, r], du_hbm.at[1, pl.ds(r * rows, rows), :])
    advance(len(todo))
    for copy in pending:
        copy.wait_send()
    for copy in stores:
        copy.wait()


def middle_call(os_pair, mixed, x, g, fc1, fc2, out_w, post, pre, wide):
    micro, rows, model = x.shape
    hidden = fc1.shape[1]
    width = out_w.shape[0]
    tokens = 4 * rows
    vmem = pl.BlockSpec(memory_space=pltpu.VMEM)
    wide_rows = jax.ShapeDtypeStruct((micro, tokens, model), BF)
    own = jax.ShapeDtypeStruct((micro, rows, model), F32)
    size = lax.axis_size("dp")
    bits = tuple(2**b for b in range(size.bit_length() - 1))
    group = max(SEG, 16 * size)
    count = 2 * hidden // group
    return pl.pallas_call(
        partial(middle, bits),
        out_shape=(
            wide_rows,
            jax.ShapeDtypeStruct((micro, tokens, width), F32),
            own, own,
            jax.ShapeDtypeStruct((micro, rows, model), BF),
            jax.ShapeDtypeStruct((24, model), F32),
            jax.ShapeDtypeStruct((count, group // size, model), BF),
        ),
        in_specs=[vmem, vmem, vmem, vmem, HBM, HBM, HBM, vmem, vmem, vmem, vmem],
        out_specs=(HBM, vmem, vmem, vmem, vmem, vmem, vmem),
        scratch_shapes=[
            pltpu.VMEM((model, hidden), BF),
            pltpu.VMEM((hidden, model), BF),
            pltpu.VMEM((micro, 4, rows, model), BF),
            pltpu.VMEM((micro, 4, rows, model), BF),
            pltpu.VMEM((micro, tokens, hidden), F32),
            pltpu.VMEM((micro, 4, rows, hidden), BF),
            pltpu.VMEM((micro, tokens, hidden), BF),
            pltpu.VMEM((micro, 4, rows, model), BF),
            pltpu.VMEM((micro, 2, rows, model), BF),
            pltpu.VMEM((2, micro, 2, rows, model), BF),
            pltpu.VMEM((micro, rows, model), BF),
            pltpu.VMEM((2, micro, rows, model), BF),
            pltpu.VMEM((micro, rows, model), F32),
            pltpu.VMEM((micro, rows, 128), F32),
            pltpu.VMEM((micro, 8, tokens), F32),
            pltpu.VMEM((micro, 3, 8, tokens), F32),
            pltpu.VMEM((4, rows, 128), F32),
            pltpu.VMEM((128, rows), F32),
            pltpu.VMEM((2, hidden, model), BF),
            pltpu.SemaphoreType.DMA((40 + count * len(bits),)),
            pltpu.SemaphoreType.DMA((40 + count * len(bits),)),
            pltpu.SemaphoreType.DMA((20,)),
        ],
        compiler_params=pltpu.CompilerParams(
            collective_id=0, has_side_effects=True, vmem_limit_bytes=61 << 20
        ),
        cost_estimate=pl.CostEstimate(flops=100 * 10**9, transcendentals=0, bytes_accessed=40 << 20),
        name="middle",
    )(*os_pair, mixed, x, g, fc1, fc2, out_w, post, pre, wide)


def finish(bits, *refs):
    dq0, dq1, os0, os1, weight, pre, mid_gains, head0, head1 = refs[0:9]
    held, came, dk1, dv1 = refs[9:13], refs[13:17], refs[17:21], refs[21:25]
    full_hbm, du_hbm, x_hbm, dr1_hbm = refs[25:29]
    din, grad, out_grad, small_out = refs[29:33]
    piece, inbox, inner, grads, acc, stage, arrived, res, core_out, core_in, y_out, y_in, small, small_in = refs[33:47]
    full, du, x, dr1, send, recv, local = refs[47:54]
    shard = lax.axis_index("tensor")
    index = lax.axis_index("dp")
    near, far = other(shard, 1), other(shard, 2)
    rows, model = x.shape[1], x.shape[2]
    tokens, width = dq0.shape
    dqs = (dq0, dq1)

    def bit_of(mask):
        return (index // mask) % 2

    def dp_peer(mask):
        return {"dp": index + mask - 2 * mask * bit_of(mask)}

    used = [0]
    pending = []

    def remote(src, dst, target):
        i = used[0]
        used[0] += 1
        copy = pltpu.make_async_remote_copy(
            src_ref=src, dst_ref=dst, send_sem=send.at[i], recv_sem=recv.at[i],
            device_id=target, device_id_type=pl.DeviceIdType.MESH,
        )
        copy.start()
        pending.append(copy)
        return copy

    fetched = [0]

    def fetch(src, dst):
        i = fetched[0]
        fetched[0] += 1
        copy = pltpu.make_async_copy(src, dst, local.at[i])
        copy.start()
        return copy

    def each(count, fn):
        lax.fori_loop(0, count, lambda i, c: (fn(i), c)[1], 0)

    def tile(n):
        return pl.ds(pl.multiple_of(n * SEG, SEG), SEG)

    barrier = pltpu.get_barrier_semaphore()
    targets = [{"tensor": near}, {"tensor": far}] + [dp_peer(mask) for mask in bits]
    for target in targets:
        pl.semaphore_signal(barrier, inc=1, device_id=target, device_id_type=pl.DeviceIdType.MESH)
    mine1 = (dk1[0], dk1[1], dv1[0], dv1[2])
    in_came = [fetch(came[i], inbox.at[0, i]) for i in range(4)]
    got = [[fetch(src, piece.at[0, i]) for i, src in enumerate(held)]]
    in_full = [fetch(full_hbm, full)]
    got.append([fetch(src, piece.at[1, i]) for i, src in enumerate(mine1)])
    in_rest = [fetch(du_hbm, du), fetch(x_hbm, x), fetch(dr1_hbm, dr1)]
    pl.semaphore_wait(barrier, len(targets))

    def first_sends():
        return [
            remote(dk1[3], inbox.at[1, 0], dp_peer(2)),
            remote(dv1[3], inbox.at[1, 1], dp_peer(1)),
            remote(dk1[2], inbox.at[1, 2], dp_peer(2)),
            remote(dv1[1], inbox.at[1, 3], dp_peer(1)),
        ]

    class Here:
        def __init__(self, copy):
            self.copy = copy

        def wait_recv(self):
            self.copy.wait()

    def add_rows(out, terms):
        def one(n):
            total = terms[0][tile(n), :].astype(F32)
            for term in terms[1:]:
                total = total + term[tile(n), :].astype(F32)
            out[tile(n), :] = total.astype(out.dtype)

        each(tokens // SEG, one)

    def second_sends(m, first):
        for copy in got[m]:
            copy.wait()
        first[0].wait_recv()
        add_rows(inner.at[m, 0], [piece.at[m, 1], inbox.at[m, 0]])
        one = remote(inner.at[m, 0], inbox.at[m, 4], dp_peer(1))
        first[1].wait_recv()
        add_rows(inner.at[m, 1], [piece.at[m, 3], inbox.at[m, 1]])
        two = remote(inner.at[m, 1], inbox.at[m, 5], dp_peer(2))
        return one, two

    def own_key(m, first, second):
        first[2].wait_recv()
        second[0].wait_recv()
        add_rows(grads.at[m, :, width:2 * width], [piece.at[m, 0], inbox.at[m, 2], inbox.at[m, 4]])

    def own_value(m, first, second):
        first[3].wait_recv()
        second[1].wait_recv()
        add_rows(grads.at[m, :, 2 * width:3 * width], [piece.at[m, 2], inbox.at[m, 3], inbox.at[m, 5]])

    def out_rows(n):
        acc[3, tile(n), :] = mm(du[0, :, tile(n)], os0[...], TN) + mm(du[1, :, tile(n)], os1[...], TN)

    def weight_rows(m, kind):
        cols = slice(kind * width, (kind + 1) * width)

        def one(n):
            part = mm(full[m, :, tile(n)], grads[m, :, cols], TN)
            acc[kind, tile(n), :] = part if m == 0 else acc[kind, tile(n), :] + part

        each(model // SEG, one)

    def input_rows(m):
        def block(r, out):
            def one(n):
                part = jnp.zeros((rows, SEG), F32)
                for kind in range(3):
                    part += mm(
                        grads[m, r * rows:(r + 1) * rows, kind * width:(kind + 1) * width],
                        weight[kind, tile(n), :],
                        NT,
                    )
                out[:, tile(n)] = part.astype(out.dtype)

            each(model // SEG, one)

        block(3, core_out.at[m, 0])
        hop3 = remote(core_out.at[m, 0], core_in.at[m, 0], {"tensor": near})
        block(1, core_out.at[m, 1])
        hop1 = remote(core_out.at[m, 1], core_in.at[m, 1], {"tensor": near})
        block(2, din.at[m])
        hop3.wait_recv()
        y_out[m] = (din[m] + core_in[m, 0].astype(F32)).astype(BF)
        hop = remote(y_out.at[m], y_in.at[m], {"tensor": far})
        block(0, din.at[m])
        return hop1, hop

    chunk = 32

    def input_norms(m, hops):
        hops[0].wait_recv()
        hops[1].wait_recv()

        def one(i):
            at = pl.ds(pl.multiple_of(i * chunk, chunk), chunk)
            dh1 = din[m, at] + core_in[m, 1, at].astype(F32) + y_in[m, at].astype(F32)
            values = x[m, at].astype(F32)
            center = values - jnp.mean(values, axis=-1, keepdims=True)
            inverse = lax.rsqrt(jnp.mean(center * center, axis=-1, keepdims=True) + EPSILON)
            normed = center * inverse
            small[0] += jnp.sum((dh1 * normed).reshape(chunk // 8, 8, model), axis=0)
            din[m, at] = dr1[m, at] + norm_backward(dh1 * pre[...], normed, inverse)

        each(rows // chunk, one)

    class Chain:
        def __init__(self, kind):
            self.kind, self.base, self.size, self.at, self.step = kind, 0, model, 0, 0
            self.copy, self.back, self.done = None, False, False

        def reduce_send(self):
            mask = bits[self.step]
            half = self.size // 2
            out = pl.ds(pl.multiple_of(self.base + (1 - bit_of(mask)) * half, 16), half)
            slot = pl.ds(self.at, half)
            stage[self.kind, slot, :] = acc[self.kind, out, :].astype(BF)
            self.copy = remote(stage.at[self.kind, slot, :], arrived.at[self.kind, slot, :], dp_peer(mask))
            self.base, self.size = self.base + bit_of(mask) * half, half

        def reduce_wait(self):
            self.copy.wait_recv()
            mine = pl.ds(pl.multiple_of(self.base, 16), self.size)
            total = acc[self.kind, mine, :] + arrived[self.kind, pl.ds(self.at, self.size), :].astype(F32)
            self.at += self.size
            self.step += 1
            if self.step < len(bits):
                acc[self.kind, mine, :] = total
            else:
                res[self.kind, mine, :] = total.astype(BF)

        def gather_send(self):
            self.step -= 1
            mask = bits[self.step]
            mine = pl.ds(pl.multiple_of(self.base, 16), self.size)
            self.copy = remote(res.at[self.kind, mine, :], res.at[self.kind, mine, :], dp_peer(mask))
            self.base, self.size = self.base - bit_of(mask) * self.size, 2 * self.size

        def go(self):
            if self.back:
                self.copy.wait_recv()
                if self.step:
                    self.gather_send()
                else:
                    self.done = True
            else:
                self.reduce_wait()
                if self.step < len(bits):
                    self.reduce_send()
                else:
                    self.back = True
                    self.gather_send()

    for m in range(MICRO):
        grads[m, :, 0:width] = dqs[m][...]
    small[...] = jnp.zeros_like(small)
    small[1:4] = mid_gains[...].reshape(3, 8, model)
    small[4, :, 0:width] = head0[...] + head1[...]

    first0 = [Here(copy) for copy in in_came]
    second0 = second_sends(0, first0)
    first1 = first_sends()
    for copy in in_full:
        copy.wait()
    weight_rows(0, 0)
    weight_rows(1, 0)
    query, mixer, key, value = [Chain(kind) for kind in (0, 3, 1, 2)]
    query.reduce_send()
    for copy in in_rest:
        copy.wait()
    each(model // SEG, out_rows)
    mixer.reduce_send()
    own_key(0, first0, second0)
    own_value(0, first0, second0)
    hops0 = input_rows(0)
    weight_rows(0, 1)
    weight_rows(0, 2)
    second1 = second_sends(1, first1)
    query.go()
    mixer.go()
    input_norms(0, hops0)
    query.go()
    mixer.go()
    own_key(1, first1, second1)
    weight_rows(1, 1)
    key.reduce_send()
    own_value(1, first1, second1)
    weight_rows(1, 2)
    value.reduce_send()
    hops1 = input_rows(1)
    query.go()
    mixer.go()
    key.go()
    value.go()
    query.go()
    mixer.go()
    input_norms(1, hops1)
    totals = jnp.zeros((8, model), F32)
    place_row = lax.broadcasted_iota(jnp.int32, (8, model), 0)
    for i in range(5):
        totals = jnp.where(place_row == i, jnp.sum(small[i], axis=0, keepdims=True), totals)
    small[0] = totals
    small_copy = remote(small.at[0], small_in.at[0], {"tensor": near})
    key.go()
    value.go()
    query.go()
    mixer.go()
    small_copy.wait_recv()
    small[1] = small[0] + jnp.where(place_row < 3, small_in[0], 0.0)
    small_copy = remote(small.at[1], small_in.at[1], {"tensor": far})
    key.go()
    value.go()
    small_copy.wait_recv()
    small[2] = small[1] + jnp.where(place_row < 3, small_in[1], 0.0)
    for step, mask in enumerate(bits):
        small_copy = remote(small.at[2 + step], small_in.at[2 + step], dp_peer(mask))
        for chain in (key, value, query, mixer):
            if not chain.done:
                chain.go()
        small_copy.wait_recv()
        small[3 + step] = small[2 + step] + small_in[2 + step]
    while not (key.done and value.done and query.done and mixer.done):
        for chain in (key, value, query, mixer):
            if not chain.done:
                chain.go()
    small_out[...] = small[2 + len(bits)]

    def widen(n):
        for kind in range(3):
            grad[kind, tile(n), :] = res[kind, tile(n), :].astype(F32)
        out_grad[:, tile(n)] = jnp.transpose(res[3, tile(n), :].astype(F32))

    each(model // SEG, widen)
    for copy in pending:
        copy.wait_send()


def finish_call(dqs, held, came, dk1, dv1, full, os_pair, du, x, dr1, weight, pre, mid_gains, heads):
    micro, rows, model = x.shape
    tokens, width = dqs[0].shape
    bits = tuple(2**b for b in range(lax.axis_size("dp").bit_length() - 1))
    vmem = pl.BlockSpec(memory_space=pltpu.VMEM)
    return pl.pallas_call(
        partial(finish, bits),
        out_shape=(
            jax.ShapeDtypeStruct((micro, rows, model), F32),
            jax.ShapeDtypeStruct((3, model, width), F32),
            jax.ShapeDtypeStruct((width, model), F32),
            jax.ShapeDtypeStruct((8, model), F32),
        ),
        in_specs=[vmem] * 9 + [HBM] * 20,
        out_specs=(vmem,) * 4,
        scratch_shapes=[
            pltpu.VMEM((micro, 4, tokens, width), BF),
            pltpu.VMEM((micro, 6, tokens, width), BF),
            pltpu.VMEM((micro, 2, tokens, width), BF),
            pltpu.VMEM((micro, tokens, 3 * width), BF),
            pltpu.VMEM((4, model, width), F32),
            pltpu.VMEM((4, model, width), BF),
            pltpu.VMEM((4, model, width), BF),
            pltpu.VMEM((4, model, width), BF),
            pltpu.VMEM((micro, 2, rows, model), BF),
            pltpu.VMEM((micro, 2, rows, model), BF),
            pltpu.VMEM((micro, rows, model), BF),
            pltpu.VMEM((micro, rows, model), BF),
            pltpu.VMEM((3 + len(bits) + 2, 8, model), F32),
            pltpu.VMEM((2 + len(bits), 8, model), F32),
            pltpu.VMEM((micro, tokens, model), BF),
            pltpu.VMEM((micro, tokens, model), BF),
            pltpu.VMEM((micro, rows, model), BF),
            pltpu.VMEM((micro, rows, model), F32),
            pltpu.SemaphoreType.DMA((24 + 9 * len(bits),)),
            pltpu.SemaphoreType.DMA((24 + 9 * len(bits),)),
            pltpu.SemaphoreType.DMA((20,)),
        ],
        compiler_params=pltpu.CompilerParams(
            collective_id=1, has_side_effects=True, vmem_limit_bytes=61 << 20
        ),
        cost_estimate=pl.CostEstimate(flops=60 * 10**9, transcendentals=0, bytes_accessed=30 << 20),
        name="finish",
    )(
        *dqs, *os_pair, weight, pre, mid_gains, *heads, *held, *came, *dk1, *dv1, full, du, x, dr1
    )


def body(
    block_input,
    cotangent,
    parent,
    pre_attn_gain,
    qkv_weight,
    head_scale,
    out_weight,
    post_attn_gain,
    pre_ffn_gain,
    fc1_weight,
    ffn_norm_gain,
    fc2_weight,
):
    trees = parent.shape[1]
    group = lax.axis_size("dp") // trees
    member = lax.axis_index("dp") % group
    tree_index = lax.axis_index("dp") // group
    shard = lax.axis_index("tensor")
    row_count = block_input.shape[1]
    tokens = cotangent.shape[1]
    width = qkv_weight.shape[2]
    parents = parent.reshape(-1)
    scale_row = jnp.repeat(head_scale, HEAD_DIM)[None, :]

    def place(micro):
        return jnp.stack([(micro * trees + tree_index) * SEGS, member, shard]).astype(jnp.int32)

    q0, q1, o0, o1, os0, os1, lse0, lse1, mixed, full1, keys, values = opening_call(
        parents, block_input, pre_attn_gain[None], qkv_weight, scale_row, out_weight
    )
    full1 = full1.reshape(MICRO, tokens, -1)
    keys, values = [tree.reshape(MICRO, 4, tokens, width) for tree in (keys, values)]
    du, dos, dr1, f_own, f_far, mid_gains, shares = middle_call(
        (os0, os1),
        mixed,
        block_input,
        cotangent,
        fc1_weight,
        fc2_weight,
        out_weight,
        post_attn_gain[None],
        pre_ffn_gain[None],
        ffn_norm_gain[None],
    )
    count, lines, model = shares.shape
    whole = lax.all_gather(shares, "dp", axis=0)
    f_got = swap(f_far, "tensor", 2)
    outputs = (f_own + f_got.astype(F32)).astype(BF)
    backs = [
        attention_grad(m, place(m), parents, q, dos[m], o, lse, scale_row, keys, values)
        for m, (q, o, lse) in enumerate(((q0, o0, lse0), (q1, o1, lse1)))
    ]
    dk0, dv0 = backs[0][1:5], backs[0][5:9]
    came = (swap(dk0[3], "dp", 2), swap(dv0[3], "dp", 1), swap(dk0[2], "dp", 2), swap(dv0[1], "dp", 1))
    din, qkv_grad, out_grad, small = finish_call(
        [b[0] for b in backs],
        (dk0[0], dk0[1], dv0[0], dv0[2]),
        came,
        backs[1][1:5],
        backs[1][5:9],
        full1,
        (os0, os1),
        du,
        block_input,
        dr1,
        qkv_weight,
        pre_attn_gain[None],
        mid_gains,
        [b[9] for b in backs],
    )
    head_grad = small[4, 0:width].reshape(-1, HEAD_DIM).sum(-1)
    levels = lax.axis_size("dp").bit_length() - 1
    whole = whole.reshape((2,) * levels + (2, count // 2, lines, model))
    whole = jnp.transpose(whole, (levels, levels + 1) + tuple(range(levels))[::-1] + (levels + 2, levels + 3))
    whole = whole.reshape(2, -1, model)
    return (
        outputs,
        din,
        small[0],
        qkv_grad,
        head_grad,
        out_grad,
        small[1],
        small[2],
        whole[0].astype(F32),
        small[3],
        whole[1].astype(F32),
    )


def solution(mesh):
    in_specs = (
        P(None, ("dp", "tensor"), None),
        P(None, "dp", None),
        P(),
        P(),
        P(None, None, "tensor"),
        P("tensor"),
        P("tensor", None),
        P(),
        P(),
        P(None, "tensor"),
        P("tensor"),
        P("tensor", None),
    )
    out_specs = (
        P(None, ("dp", "tensor"), None),
        P(None, ("dp", "tensor"), None),
        P(),
        P(None, None, "tensor"),
        P("tensor"),
        P("tensor", None),
        P(),
        P(),
        P(None, "tensor"),
        P("tensor"),
        P("tensor", None),
    )
    return jax.shard_map(body, mesh=mesh, in_specs=in_specs, out_specs=out_specs, check_vma=False)
```

```python
from functools import partial

import jax
import jax.numpy as jnp
from jax import lax
from jax.experimental import pallas as pl
from jax.experimental.pallas import tpu as pltpu
from jax.sharding import PartitionSpec as P

HEAD_DIM = 64
FFN = 4096
SEG = 256
SEGS = 16
DEPTH = 5
MICRO = 2

EPSILON = 1e-05
NEGATIVE = -1e30
F32 = jnp.float32
BF = jnp.bfloat16
NN = (((1,), (0,)), ((), ()))
NT = (((1,), (1,)), ((), ()))
TN = (((0,), (0,)), ((), ()))


def mm(a, b, dims=NN):
    return lax.dot_general(a, b, dims, preferred_element_type=F32)


def swap(value, axis, mask):
    return lax.ppermute(value, axis, [(i, i ^ mask) for i in range(lax.axis_size(axis))])


def normalize(values):
    center = values - jnp.mean(values, axis=-1, keepdims=True)
    inverse = lax.rsqrt(jnp.mean(center * center, axis=-1, keepdims=True) + EPSILON)
    return (center * inverse, inverse)


def norm_backward(grad_hat, normed, inverse):
    mean_grad = jnp.mean(grad_hat, axis=-1, keepdims=True)
    mean_cross = jnp.mean(grad_hat * normed, axis=-1, keepdims=True)
    return inverse * (grad_hat - mean_grad - normed * mean_cross)


def climb(parents, base, seg):
    found = []
    current = seg
    count = jnp.int32(0)
    for _ in range(DEPTH):
        up = parents[base + current]
        valid = up >= 0
        count = count + valid.astype(jnp.int32)
        current = jnp.where(valid, up, current)
        found.append(current)
    return count, found


HBM = pl.BlockSpec(memory_space=pl.ANY)


def gelu_parts(c):
    root = 0.7978845608028654
    square = c * c
    tanh = jnp.tanh(root * (c + 0.044715 * (square * c)))
    act = 0.5 * c * (1.0 + tanh)
    slope = 0.5 * (1.0 + tanh) + 0.5 * c * (1.0 - tanh * tanh) * (root * (1.0 + 3 * 0.044715 * square))
    return act, slope


def other(shard, mask):
    near = shard + 1 - 2 * (shard % 2)
    return {0: shard, 1: near, 2: (shard + 2) % 4, 3: (near + 2) % 4}[mask]


def xor4(a, b):
    return 2 * lax.rem(lax.div(a, 2) + lax.div(b, 2), 2) + lax.rem(a + b, 2)


def opening(
    parents, x, gain, weight, scale_ref, out_w,
    q0, q1, o0, o1, os0, os1, lse0, lse1, mixed, full_hbm, kt_hbm, vt_hbm,
    full, kt0, kt1, vt0, vt1, picked_k, picked_v, core_out, core_in, y_out, y_in, send, recv, local,
):
    shard = lax.axis_index("tensor")
    index = lax.axis_index("dp")
    near, far = {"tensor": other(shard, 1)}, {"tensor": other(shard, 2)}
    beside, beyond = [{"dp": index + mask - 2 * mask * ((index // mask) % 2)} for mask in (1, 2)]
    rows, model = x.shape[1], x.shape[2]
    width = q0.shape[1]
    heads = width // HEAD_DIM
    tokens = 4 * rows
    per = tokens // SEG
    member, tree = index % 4, index // 4
    trees = parents.shape[0] // (MICRO * SEGS)
    qs, os_, oss, lses = (q0, q1), (o0, o1), (os0, os1), (lse0, lse1)
    kts, vts = (kt0, kt1), (vt0, vt1)
    used = [0]
    pending = []

    def remote(src, dst, target):
        i = used[0]
        used[0] += 1
        copy = pltpu.make_async_remote_copy(
            src_ref=src, dst_ref=dst, send_sem=send.at[i], recv_sem=recv.at[i],
            device_id=target, device_id_type=pl.DeviceIdType.MESH,
        )
        copy.start()
        pending.append(copy)
        return copy

    stores = []

    def store(src, dst):
        copy = pltpu.make_async_copy(src, dst, local.at[len(stores)])
        copy.start()
        stores.append(copy)

    def each(count, fn):
        lax.fori_loop(0, count, lambda i, c: (fn(i), c)[1], 0)

    barrier = pltpu.get_barrier_semaphore()
    for target in (near, far, beside, beyond):
        pl.semaphore_signal(barrier, inc=1, device_id=target, device_id_type=pl.DeviceIdType.MESH)

    chunk = 32

    def norms(m):
        def one(i):
            at = pl.ds(pl.multiple_of(i * chunk, chunk), chunk)
            values = x[m, at].astype(F32)
            center = values - jnp.mean(values, axis=-1, keepdims=True)
            inverse = lax.rsqrt(jnp.mean(center * center, axis=-1, keepdims=True) + EPSILON)
            full[m, 0, at] = (center * inverse * gain[...]).astype(BF)

        each(rows // chunk, one)

    def spread(m):
        return remote(full.at[m, 0], full.at[m, 2], far), remote(full.at[m, 0], full.at[m, 1], near)

    def project(m, first):
        for r in (first, first + 1):
            kts[m][r] = mm(full[m, r], weight[1]).astype(BF)
            vts[m][r] = mm(full[m, r], weight[2]).astype(BF)

    def queries(m):
        for r in range(4):
            qs[m][r * rows:(r + 1) * rows, :] = mm(full[m, r], weight[0]).astype(BF)

    def piece(ref, r, half):
        return ref.at[pl.ds(4 * r + 2 * half, 2)]

    def share(m, half):
        k, v = kts[m], vts[m]
        return [
            remote(piece(k, 0, half), piece(k, 1, half), beside),
            remote(piece(v, 0, half), piece(v, 2, half), beyond),
            remote(piece(k, 0, half), piece(k, 2, half), beyond),
            remote(piece(v, 0, half), piece(v, 1, half), beside),
        ]

    def forward(m, half, copies):
        copies[0].wait_recv()
        one = remote(piece(kts[m], 1, half), piece(kts[m], 3, half), beyond)
        copies[1].wait_recv()
        return copies[2:] + [one, remote(piece(vts[m], 2, half), piece(vts[m], 3, half), beside)]

    def settle(*groups):
        for copies in groups:
            for copy in copies:
                copy.wait_recv()

    def attend(m, step):
        seg = member * per + xor4(step, shard)
        count, found = climb(parents, (m * trees + tree) * SEGS, seg)
        past = DEPTH * SEG
        for slot in range(DEPTH):
            s = found[slot]
            at = 4 * xor4(lax.div(s, 4), member) + xor4(lax.rem(s, 4), shard)
            picked_k[slot * SEG:(slot + 1) * SEG, :] = kts[m][at]
            picked_v[slot * SEG:(slot + 1) * SEG, :] = vts[m][at]
        here = pl.ds(pl.multiple_of(step * SEG, SEG), SEG)
        picked_k[past:past + SEG, :] = kts[m][step]
        picked_v[past:past + SEG, :] = vts[m][step]
        lane = lax.broadcasted_iota(jnp.int32, (SEG, width), 1) // HEAD_DIM
        row = lax.broadcasted_iota(jnp.int32, (SEG, SEG), 0)
        col = lax.broadcasted_iota(jnp.int32, (SEG, SEG), 1)
        slot_of = lax.broadcasted_iota(jnp.int32, (1, past), 1) // SEG
        bias = jnp.where(slot_of < count, 0.0, NEGATIVE).astype(F32)
        q = qs[m][here, :] * BF(HEAD_DIM ** -0.5)
        lse_lane = lax.broadcasted_iota(jnp.int32, (SEG, 128), 1)
        lse_all = jnp.zeros((SEG, 128), F32)
        out = jnp.zeros((SEG, width), F32)
        for head in range(heads):
            qh = jnp.where(lane == head, q, jnp.zeros_like(q))
            s_past = mm(qh, picked_k[0:past, :], NT) + bias
            s_own = jnp.where(col <= row, mm(qh, picked_k[past:past + SEG, :], NT), NEGATIVE)
            top = jnp.maximum(
                jnp.max(s_past, axis=1, keepdims=True), jnp.max(s_own, axis=1, keepdims=True)
            )
            p_past = jnp.exp(s_past - top)
            p_own = jnp.exp(s_own - top)
            total = jnp.sum(p_past, axis=1, keepdims=True) + jnp.sum(p_own, axis=1, keepdims=True)
            got = mm(p_past.astype(BF), picked_v[0:past, :]) + mm(p_own.astype(BF), picked_v[past:past + SEG, :])
            out = jnp.where(lane == head, got / total, out)
            lse_all = jnp.where(lse_lane == head, top + jnp.log(total), lse_all)
        os_[m][here, :] = out
        oss[m][here, :] = (out * scale_ref[...]).astype(BF)
        lses[m][pl.ds(step, 1)] = jnp.transpose(lse_all)[0:8].reshape(1, 8, SEG)

    norms(0)
    pl.semaphore_wait(barrier, 4)
    far0, near0 = spread(0)
    norms(1)
    far1, near1 = spread(1)
    near0.wait_recv()
    project(0, 0)
    a0 = share(0, 0)
    near1.wait_recv()
    project(1, 0)
    far0.wait_recv()
    cross0 = remote(full.at[0, 2], full.at[0, 3], near)
    cross0.wait_recv()
    project(0, 2)
    b0 = share(0, 1)
    a0 = forward(0, 0, a0)
    queries(0)
    far1.wait_recv()
    cross1 = remote(full.at[1, 2], full.at[1, 3], near)
    b0 = forward(0, 1, b0)
    a1 = share(1, 0)
    cross1.wait_recv()
    project(1, 2)
    b1 = share(1, 1)
    queries(1)
    for m in range(MICRO):
        store(full.at[m], full_hbm.at[m])
    settle(a0, b0)
    lax.fori_loop(0, 2, lambda i, c: (attend(0, i), c)[1], 0)
    a1 = forward(1, 0, a1)
    lax.fori_loop(2, 4, lambda i, c: (attend(0, i), c)[1], 0)
    b1 = forward(1, 1, b1)

    def mix(r):
        return mm(os0[r * rows:(r + 1) * rows, :], out_w[...])

    core_out[0] = mix(3).astype(BF)
    hop3 = remote(core_out.at[0], core_in.at[0], near)
    core_out[1] = mix(1).astype(BF)
    hop1 = remote(core_out.at[1], core_in.at[1], near)
    mixed[...] = mix(2)
    hop3.wait_recv()
    y_out[...] = (mixed[...] + core_in[0].astype(F32)).astype(BF)
    hop2 = remote(y_out, y_in, far)
    hop1.wait_recv()
    mixed[...] = mix(0) + core_in[1].astype(F32)
    store(kt0, kt_hbm.at[0])
    store(vt0, vt_hbm.at[0])
    settle(a1, b1)
    store(kt1, kt_hbm.at[1])
    store(vt1, vt_hbm.at[1])
    lax.fori_loop(0, 4, lambda i, c: (attend(1, i), c)[1], 0)
    hop2.wait_recv()
    mixed[...] = mixed[...] + y_in[...].astype(F32)
    for copy in pending:
        copy.wait_send()
    for copy in stores:
        copy.wait()


def opening_call(parents, x, gain, weight, scale_row, out_w):
    micro, rows, model = x.shape
    width = weight.shape[2]
    tokens = 4 * rows
    vmem = pl.BlockSpec(memory_space=pltpu.VMEM)
    narrow = jax.ShapeDtypeStruct((tokens, width), BF)
    narrow_wide = jax.ShapeDtypeStruct((tokens, width), F32)
    tops = jax.ShapeDtypeStruct((tokens // SEG, 8, SEG), F32)
    trees = jax.ShapeDtypeStruct((micro, 4 * tokens // SEG, SEG, width), BF)
    return pl.pallas_call(
        opening,
        out_shape=(
            narrow, narrow, narrow_wide, narrow_wide, narrow, narrow, tops, tops,
            jax.ShapeDtypeStruct((rows, model), F32),
            jax.ShapeDtypeStruct((micro, 4, rows, model), BF),
            trees, trees,
        ),
        in_specs=[pl.BlockSpec(memory_space=pltpu.SMEM)] + [vmem] * 5,
        out_specs=(vmem,) * 9 + (HBM,) * 3,
        scratch_shapes=[pltpu.VMEM((micro, 4, rows, model), BF)]
        + [pltpu.VMEM((4 * tokens // SEG, SEG, width), BF)] * 4
        + [pltpu.VMEM(((DEPTH + 1) * SEG, width), BF)] * 2
        + [pltpu.VMEM((2, rows, model), BF)] * 2
        + [pltpu.VMEM((rows, model), BF)] * 2
        + [
            pltpu.SemaphoreType.DMA((36,)),
            pltpu.SemaphoreType.DMA((36,)),
            pltpu.SemaphoreType.DMA((8,)),
        ],
        compiler_params=pltpu.CompilerParams(
            collective_id=2, has_side_effects=True, vmem_limit_bytes=61 << 20
        ),
        cost_estimate=pl.CostEstimate(flops=60 * 10**9, transcendentals=0, bytes_accessed=20 << 20),
        name="opening",
    )(parents, x, gain, weight, scale_row, out_w)


def middle(
    bits, os0, os1, mixed0, x, g_hbm, fc1_hbm, fc2_hbm, out_w, post, pre, wide,
    du_hbm, dos, dr1, f_own, f_far, gains, shares,
    fc1, fc2, gd, du, act, slz, dzc, full, core_out, core_in, y_out, y_in, nu, inv, st_out, st_in, sums, cols,
    arrived, send, recv, local,
):
    shard = lax.axis_index("tensor")
    index = lax.axis_index("dp")

    def bit_of(mask):
        return (index // mask) % 2

    def dp_peer(mask):
        return {"dp": index + mask - 2 * mask * bit_of(mask)}

    peers = [other(shard, k) for k in range(4)]
    rows = x.shape[1]
    model = x.shape[2]
    hidden = fc1.shape[1]
    parts = hidden // SEG
    used = [0]
    pending = []

    def remote(src, dst, target):
        i = used[0]
        used[0] += 1
        if not isinstance(target, dict):
            target = {"tensor": peers[target]}
        copy = pltpu.make_async_remote_copy(
            src_ref=src, dst_ref=dst, send_sem=send.at[i], recv_sem=recv.at[i],
            device_id=target, device_id_type=pl.DeviceIdType.MESH,
        )
        copy.start()
        pending.append(copy)
        return copy

    stored = [0]
    stores = []

    def store(src, dst):
        i = stored[0]
        stored[0] += 1
        copy = pltpu.make_async_copy(src, dst, local.at[i])
        copy.start()
        stores.append(copy)

    def fetch(src, dst):
        i = stored[0]
        stored[0] += 1
        copy = pltpu.make_async_copy(src, dst, local.at[i])
        copy.start()
        return copy

    got_fc2 = fetch(fc2_hbm, fc2)
    got_g = [
        [fetch(g_hbm.at[m, pl.ds(peers[r] * rows, rows), :], gd.at[m, r]) for r in range(4)] for m in range(MICRO)
    ]
    got_fc1 = fetch(fc1_hbm, fc1)
    barrier = pltpu.get_barrier_semaphore()
    targets = [{"tensor": peers[mask]} for mask in (1, 2, 3)] + [dp_peer(mask) for mask in bits]
    for target in targets:
        pl.semaphore_signal(barrier, inc=1, device_id=target, device_id_type=pl.DeviceIdType.MESH)
    pl.semaphore_wait(barrier, len(targets))
    gains[...] = jnp.zeros_like(gains)

    def each(count, fn):
        lax.fori_loop(0, count, lambda i, c: (fn(i), c)[1], 0)

    def tile(n):
        return pl.ds(pl.multiple_of(n * SEG, SEG), SEG)

    def merge(value):
        return value.reshape((-1,) + value.shape[2:])

    def reuse(*groups):
        for copies in groups:
            for copy in copies if isinstance(copies, tuple) else (copies,):
                copy.wait_send()
                pending[:] = [other_copy for other_copy in pending if other_copy is not copy]

    def first_hop(kind, m, block, out):
        block(3, core_out.at[m, 0])
        hop3 = remote(core_out.at[m, 0], core_in.at[kind, m, 0], 1)
        block(1, core_out.at[m, 1])
        hop1 = remote(core_out.at[m, 1], core_in.at[kind, m, 1], 1)
        block(2, None)
        block(0, out)
        return hop3, hop1

    chunk = 32

    def chunks(fn):
        each(rows // chunk, lambda i: fn(pl.ds(pl.multiple_of(i * chunk, chunk), chunk)))

    def add_far(kind, m):
        def one(at):
            y_out[m, at] = (sums_far[m][at] + core_in[kind, m, 0, at].astype(F32)).astype(BF)

        chunks(one)

    sums_far = [f_own.at[m] for m in range(MICRO)]
    def mixed_block():
        def block(r, out):
            part = mm(os1[r * rows:(r + 1) * rows, :], out_w[...])
            if r == 2:
                sums_far[1][...] = part
            else:
                out[...] = part.astype(out.dtype)

        return block

    hops = first_hop(0, 1, mixed_block(), nu.at[1])
    hops[0].wait_recv()
    add_far(0, 1)
    far_hop = remote(y_out.at[1], y_in.at[0, 1], 2)
    def project_grad(m):
        for r in range(4):
            got_g[m][r].wait()

        def one(i):
            r, n = i // parts, i % parts
            dzc[m, pl.ds(pl.multiple_of(r * rows, rows), rows), tile(n)] = mm(gd[m, r], fc2[tile(n), :], NT).astype(BF)

        each(4 * parts, one)

    def own_sum(kind, m, base, at):
        return base + core_in[kind, m, 1, at].astype(F32) + y_in[kind, m, at].astype(F32)

    def norm_two(m, at, residual):
        center = residual - jnp.mean(residual, axis=-1, keepdims=True)
        inverse = lax.rsqrt(jnp.mean(center * center, axis=-1, keepdims=True) + EPSILON)
        return center * inverse, inverse

    def forward_norms(m):
        if m:
            hops[1].wait_recv()
            far_hop.wait_recv()

        def one(at):
            mixed, inverse = norm_two(m, at, own_sum(0, m, nu[m, at], at) if m else mixed0[at, :])
            nu[m, at] = mixed
            inv[m, at] = jnp.broadcast_to(inverse, (chunk, 128))
            residual = x[m, at].astype(F32) + mixed * post[...]
            normed, _ = norm_two(m, at, residual)
            full[m, 0, at] = (normed * pre[...]).astype(BF)

        chunks(one)

    def spread(m, buf):
        return remote(buf.at[m, 0], buf.at[m, 2], 2), remote(buf.at[m, 0], buf.at[m, 1], 1)

    def ffn_forward(m, r):
        sums[...] = jnp.zeros_like(sums)

        def one(n):
            value, slope = gelu_parts(mm(full[m, r], fc1[:, tile(n)]))
            act[m, r * rows:(r + 1) * rows, tile(n)] = value
            slz[m, r, :, tile(n)] = slope.astype(BF)
            dna = dzc[m, pl.ds(pl.multiple_of(r * rows, rows), rows), tile(n)].astype(F32) * wide[:, tile(n)]
            for i, term in enumerate((value, value * value, dna, dna * value)):
                sums[i] += term[:, 0:128] + term[:, 128:256]

        each(parts, one)
        lane = lax.broadcasted_iota(jnp.int32, (rows, 128), 1)
        merged = jnp.zeros((rows, 128), F32)
        for i in range(4):
            merged = jnp.where(lane == i, jnp.sum(sums[i], axis=-1, keepdims=True), merged)
        st_out[m, :, r * rows:(r + 1) * rows] = jnp.transpose(merged)[0:8]

    def send_stats(m):
        return [remote(st_out.at[m], st_in.at[m, mask - 1], mask) for mask in (1, 2, 3)]

    def ffn_backward_rows(m, r):
        total = st_out[m, :, r * rows:(r + 1) * rows]
        for mask in (1, 2, 3):
            b = r ^ mask
            total = total + st_in[m, mask - 1, :, b * rows:(b + 1) * rows]
        cols[0:8, :] = total * (1.0 / FFN)
        flipped = jnp.transpose(cols[...])
        mu, square, m_dna, m_cross = [flipped[:, i:i + 1] for i in range(4)]
        rw = lax.rsqrt(square - mu * mu + EPSILON)
        m_both = (m_cross - mu * m_dna) * rw

        def one(n):
            gain = wide[:, tile(n)]
            dz = dzc[m, pl.ds(pl.multiple_of(r * rows, rows), rows), tile(n)].astype(F32)
            na = (act[m, r * rows:(r + 1) * rows, tile(n)] - mu) * rw
            slope = slz[m, r, :, tile(n)].astype(F32)
            slz[m, r, :, tile(n)] = (na * gain).astype(BF)
            gains[16:24, tile(n)] += jnp.sum((dz * na).reshape(rows // 8, 8, SEG), axis=0)
            dzc[m, pl.ds(pl.multiple_of(r * rows, rows), rows), tile(n)] = (rw * (dz * gain - m_dna - na * m_both) * slope).astype(BF)

        each(parts, one)

    def grad_block(m):
        def block(r, out):
            ffn_backward_rows(m, r)
            if r == 2:
                out = sums_far[m]

            def one(n):
                out[:, tile(n)] = mm(dzc[m, r * rows:(r + 1) * rows, :], fc1[tile(n), :], NT).astype(out.dtype)

            each(model // SEG, one)

        return block

    def ffn_out_block(m):
        def block(r, out):
            def one(n):
                out[:, tile(n)] = mm(slz[m, r], fc2[:, tile(n)]).astype(out.dtype)

            each(model // SEG, one)

        return block

    def backward_norms(m, hop1, far_hop):
        hop1.wait_recv()
        far_hop.wait_recv()

        def one(at):
            dh2 = own_sum(1, m, dr1[m, at], at)
            mixed = nu[m, at]
            residual = x[m, at].astype(F32) + mixed * post[...]
            normed, inverse = norm_two(m, at, residual)
            gains[8:16, :] += jnp.sum((dh2 * normed).reshape(chunk // 8, 8, model), axis=0)
            grad = gd[m, 0, at].astype(F32) + norm_backward(dh2 * pre[...], normed, inverse)
            gains[0:8, :] += jnp.sum((grad * mixed).reshape(chunk // 8, 8, model), axis=0)
            dr1[m, at] = grad
            back = norm_backward(grad * post[...], mixed, inv[m, at][:, 0:1])
            du[m, 0, at] = back.astype(BF)

        chunks(one)

    def unmix(m, r):
        dos[m, r * rows:(r + 1) * rows, :] = mm(du[m, r], out_w[...], NT)

    forward_norms(0)
    far0, near0 = spread(0, full)
    got_fc2.wait()
    project_grad(0)
    got_fc1.wait()
    ffn_forward(0, 0)
    near0.wait_recv()
    ffn_forward(0, 1)
    project_grad(1)
    forward_norms(1)
    far1, near1 = spread(1, full)
    ffn_forward(1, 0)
    far0.wait_recv()
    cross0 = remote(full.at[0, 2], full.at[0, 3], 1)
    ffn_forward(0, 2)
    cross0.wait_recv()
    ffn_forward(0, 3)
    stats0 = send_stats(0)
    near1.wait_recv()
    ffn_forward(1, 1)
    far1.wait_recv()
    cross1 = remote(full.at[1, 2], full.at[1, 3], 1)
    ffn_forward(1, 2)
    for copy in stats0:
        copy.wait_recv()
    hop_a = first_hop(1, 0, grad_block(0), dr1.at[0])
    hop_a[0].wait_recv()
    add_far(1, 0)
    far_a = remote(y_out.at[0], y_in.at[1, 0], 2)
    cross1.wait_recv()
    ffn_forward(1, 3)
    stats1 = send_stats(1)

    def first_grad(m):
        def one(n):
            part = mm(merge(full[m, :, :, tile(n)]), dzc[m], TN)
            act[0, tile(n), :] = part if m == 0 else act[0, tile(n), :] + part

        each(parts, one)

    def second_grad(n):
        part = mm(merge(slz[0, :, :, tile(n)]), merge(gd[0]), TN)
        act[1, tile(n), :] = part + mm(merge(slz[1, :, :, tile(n)]), merge(gd[1]), TN)

    first_grad(0)
    for copy in stats1:
        copy.wait_recv()
    reuse(hops, far_hop)
    hop_b = first_hop(1, 1, grad_block(1), dr1.at[1])
    hop_b[0].wait_recv()
    add_far(1, 1)
    far_b = remote(y_out.at[1], y_in.at[1, 1], 2)
    backward_norms(0, hop_a[1], far_a)
    du_far0, du_near0 = spread(0, du)
    first_grad(1)
    group = hidden // (shares.shape[0] // 2)

    class Chain:
        def __init__(self, number):
            self.number, self.which = number, number // (hidden // group)
            self.start = (number % (hidden // group)) * group
            self.base, self.size, self.at, self.step = self.start, group, self.start, 0

        def send(self):
            mask = bits[self.step]
            half = self.size // 2
            away = self.base + (1 - bit_of(mask)) * half
            where = self.at

            def one(i):
                src = pl.ds(pl.multiple_of(away + i * 16, 16), 16)
                staged[self.which, pl.ds(pl.multiple_of(where + i * 16, 16), 16), :] = act[
                    self.which, src, :
                ].astype(BF)

            each(half // 16, one)
            slot = pl.ds(where, half)
            self.copy = remote(
                staged.at[self.which, slot, :], arrived.at[self.which, slot, :], dp_peer(mask)
            )
            self.base, self.size = self.base + bit_of(mask) * half, half

        def wait(self):
            self.copy.wait_recv()
            self.step += 1
            base, where, last = self.base, self.at, self.step == len(bits)

            def one(i):
                mine = pl.ds(pl.multiple_of(base + i * 16, 16), 16)
                total = act[self.which, mine, :] + arrived[
                    self.which, pl.ds(pl.multiple_of(where + i * 16, 16), 16), :
                ].astype(F32)
                if last:
                    shares[self.number, pl.ds(pl.multiple_of(i * 16, 16), 16), :] = total.astype(BF)
                else:
                    act[self.which, mine, :] = total

            each(self.size // 16, one)
            self.at += self.size

        def go(self):
            self.wait()
            if self.step < len(bits):
                self.send()

    chains = [Chain(i) for i in range(shares.shape[0])]
    half_chains = len(chains) // 2
    staged = dzc
    for chain in chains[:half_chains]:
        chain.send()
    per_chain = parts // half_chains
    for i, chain in enumerate(chains[half_chains:]):
        each(per_chain, lambda n: second_grad(n + i * per_chain))
        chain.send()
    backward_norms(1, hop_b[1], far_b)
    du_far1, du_near1 = spread(1, du)

    def ffn_out(m, hop_old):
        reuse(hop_old, ())
        block = ffn_out_block(m)
        block(3, core_out.at[m, 0])
        hop3 = remote(core_out.at[m, 0], core_in.at[0, m, 0], 1)
        block(1, core_out.at[m, 1])
        hop1 = remote(core_out.at[m, 1], core_in.at[0, m, 1], 1)
        block(2, f_own.at[m])
        hop3.wait_recv()

        def one(at):
            f_far[m, at] = (f_own[m, at] + core_in[0, m, 0, at].astype(F32)).astype(BF)

        chunks(one)
        block(0, f_own.at[m])
        hop1.wait_recv()

        def two(at):
            residual = x[m, at].astype(F32) + nu[m, at] * post[...]
            f_own[m, at] = residual + f_own[m, at] + core_in[0, m, 1, at].astype(F32)

        chunks(two)

    todo = [
        chains[turn - level]
        for turn in range(len(chains) + len(bits) - 1)
        for level in range(len(bits))
        if 0 <= turn - level < len(chains)
    ]

    def advance(count):
        for _ in range(min(count, len(todo))):
            todo.pop(0).go()

    slice_of = -(-len(todo) // 5)
    ffn_out(0, hop_a)
    unmix(0, 0)
    du_near0.wait_recv()
    unmix(0, 1)
    du_far0.wait_recv()
    du_cross0 = remote(du.at[0, 2], du.at[0, 3], 1)
    unmix(0, 2)
    advance(slice_of)
    du_cross0.wait_recv()
    unmix(0, 3)
    ffn_out(1, hop_b)
    advance(slice_of)
    unmix(1, 0)
    du_near1.wait_recv()
    unmix(1, 1)
    for r in range(4):
        store(du.at[0, r], du_hbm.at[0, pl.ds(r * rows, rows), :])
    du_far1.wait_recv()
    du_cross1 = remote(du.at[1, 2], du.at[1, 3], 1)
    unmix(1, 2)
    advance(slice_of)
    du_cross1.wait_recv()
    unmix(1, 3)
    for r in range(4):
        store(du.at[1, r], du_hbm.at[1, pl.ds(r * rows, rows), :])
    advance(len(todo))
    for copy in pending:
        copy.wait_send()
    for copy in stores:
        copy.wait()


def middle_call(os_pair, mixed, x, g, fc1, fc2, out_w, post, pre, wide):
    micro, rows, model = x.shape
    hidden = fc1.shape[1]
    width = out_w.shape[0]
    tokens = 4 * rows
    vmem = pl.BlockSpec(memory_space=pltpu.VMEM)
    wide_rows = jax.ShapeDtypeStruct((micro, tokens, model), BF)
    own = jax.ShapeDtypeStruct((micro, rows, model), F32)
    size = lax.axis_size("dp")
    bits = tuple(2**b for b in range(size.bit_length() - 1))
    group = max(SEG, 16 * size)
    count = 2 * hidden // group
    return pl.pallas_call(
        partial(middle, bits),
        out_shape=(
            wide_rows,
            jax.ShapeDtypeStruct((micro, tokens, width), F32),
            own, own,
            jax.ShapeDtypeStruct((micro, rows, model), BF),
            jax.ShapeDtypeStruct((24, model), F32),
            jax.ShapeDtypeStruct((count, group // size, model), BF),
        ),
        in_specs=[vmem, vmem, vmem, vmem, HBM, HBM, HBM, vmem, vmem, vmem, vmem],
        out_specs=(HBM, vmem, vmem, vmem, vmem, vmem, vmem),
        scratch_shapes=[
            pltpu.VMEM((model, hidden), BF),
            pltpu.VMEM((hidden, model), BF),
            pltpu.VMEM((micro, 4, rows, model), BF),
            pltpu.VMEM((micro, 4, rows, model), BF),
            pltpu.VMEM((micro, tokens, hidden), F32),
            pltpu.VMEM((micro, 4, rows, hidden), BF),
            pltpu.VMEM((micro, tokens, hidden), BF),
            pltpu.VMEM((micro, 4, rows, model), BF),
            pltpu.VMEM((micro, 2, rows, model), BF),
            pltpu.VMEM((2, micro, 2, rows, model), BF),
            pltpu.VMEM((micro, rows, model), BF),
            pltpu.VMEM((2, micro, rows, model), BF),
            pltpu.VMEM((micro, rows, model), F32),
            pltpu.VMEM((micro, rows, 128), F32),
            pltpu.VMEM((micro, 8, tokens), F32),
            pltpu.VMEM((micro, 3, 8, tokens), F32),
            pltpu.VMEM((4, rows, 128), F32),
            pltpu.VMEM((128, rows), F32),
            pltpu.VMEM((2, hidden, model), BF),
            pltpu.SemaphoreType.DMA((40 + count * len(bits),)),
            pltpu.SemaphoreType.DMA((40 + count * len(bits),)),
            pltpu.SemaphoreType.DMA((20,)),
        ],
        compiler_params=pltpu.CompilerParams(
            collective_id=0, has_side_effects=True, vmem_limit_bytes=61 << 20
        ),
        cost_estimate=pl.CostEstimate(flops=100 * 10**9, transcendentals=0, bytes_accessed=40 << 20),
        name="middle",
    )(*os_pair, mixed, x, g, fc1, fc2, out_w, post, pre, wide)


def closing(bits, parents, *refs):
    q0, q1, os0, os1, lse0, lse1, scale_ref, weight, pre, mid_gains, shares = refs[0:11]
    kt_hbm, vt_hbm, dos_hbm, o0_hbm, o1_hbm, full_hbm, du_hbm, x_hbm, dr1_hbm = refs[11:20]
    din, res, small_out, ffn = refs[20:24]
    (
        kt, vt, dos, o, bias, dqt, contrib_k, contrib_v, dkp0, dkp1, dvp0, dvp1, inbox, inner, grads, acc, stage,
        arrived, core_out, core_in, y_out, y_in, small, small_in, big, x, dr1, send, recv, local,
    ) = refs[24:]
    shard = lax.axis_index("tensor")
    index = lax.axis_index("dp")
    near, far = other(shard, 1), other(shard, 2)
    rows, model = x.shape[1], x.shape[2]
    tokens, width = q0.shape
    heads = width // HEAD_DIM
    per = tokens // SEG
    member, tree = index % 4, index // 4
    trees = parents.shape[0] // (MICRO * SEGS)
    qs, lses, os_hbm = (q0, q1), (lse0, lse1), (o0_hbm, o1_hbm)
    dkp, dvp = (dkp0, dkp1), (dvp0, dvp1)
    slots = DEPTH + 1

    def bit_of(mask):
        return (index // mask) % 2

    def dp_peer(mask):
        return {"dp": index + mask - 2 * mask * bit_of(mask)}

    used = [0]
    pending = []

    def prepare(src, dst, target):
        i = used[0]
        used[0] += 1
        copy = pltpu.make_async_remote_copy(
            src_ref=src, dst_ref=dst, send_sem=send.at[i], recv_sem=recv.at[i],
            device_id=target, device_id_type=pl.DeviceIdType.MESH,
        )
        pending.append(copy)
        return copy

    def remote(src, dst, target):
        copy = prepare(src, dst, target)
        copy.start()
        return copy

    fetched = [0]

    def fetch(src, dst):
        i = fetched[0]
        fetched[0] += 1
        copy = pltpu.make_async_copy(src, dst, local.at[i])
        copy.start()
        return copy

    def each(count, fn):
        lax.fori_loop(0, count, lambda i, c: (fn(i), c)[1], 0)

    def tile(n):
        return pl.ds(pl.multiple_of(n * SEG, SEG), SEG)

    barrier = pltpu.get_barrier_semaphore()
    targets = [{"tensor": near}, {"tensor": far}] + [dp_peer(mask) for mask in bits]
    for target in targets:
        pl.semaphore_signal(barrier, inc=1, device_id=target, device_id_type=pl.DeviceIdType.MESH)

    def fetch_tree(m):
        return [
            fetch(kt_hbm.at[m], kt), fetch(vt_hbm.at[m], vt), fetch(dos_hbm.at[m], dos), fetch(os_hbm[m], o)
        ]

    count = shares.shape[0] // 2
    group = ffn.shape[2]
    lines = group // 2 ** len(bits)
    base = 0
    for step, mask in enumerate(bits):
        base = base + bit_of(mask) * (group // 2 ** (step + 1))
    base = pl.multiple_of(base, 16)
    cut = max(1, count // 2)
    parts = [(k, at) for k in range(2) for at in range(0, count, cut)]
    in_share = [
        fetch(shares.at[pl.ds(k * count + at, cut)], ffn.at[k, pl.ds(at, cut), pl.ds(base, lines), :])
        for k, at in parts
    ]
    in_tree = fetch_tree(0)
    in_du = fetch(du_hbm, big)
    pl.semaphore_wait(barrier, len(targets))
    gathers = []
    size = lines
    for mask in bits[::-1]:
        rows_at = pl.ds(pl.multiple_of(base, 16), size)
        level = []
        for k, at in parts:
            where = ffn.at[k, pl.ds(at, cut), rows_at, :]
            level.append(prepare(where, where, dp_peer(mask)))
        gathers.append(level)
        base, size = base - bit_of(mask) * size, 2 * size
    events = {}
    for level in range(1, len(bits)):
        for part in range(len(parts)):
            turn = (1, 4, 8, 11)[part] if level < len(bits) - 1 else (7, 10, 14, 18)[part]
            events.setdefault(min(23, turn), []).append((level, part))

    def gather_turn(step, slot):
        for turn, moves in sorted(events.items()):

            @pl.when(step * 6 + slot == turn)
            def _():
                for level, part in moves:
                    gathers[level - 1][part].wait_recv()
                    gathers[level][part].start()

    def attend_back(m, step):
        seg = member * per + xor4(step, shard)
        steps_up, found = climb(parents, (m * trees + tree) * SEGS, seg)
        here = pl.ds(pl.multiple_of(step * SEG, SEG), SEG)
        grad_out = dos[here, :]
        cross = grad_out * o[here, :]
        small[4, :, 0:width] += jnp.sum(cross.reshape(SEG // 8, 8, width), axis=0)
        scale = scale_ref[...]
        go = (grad_out * scale).astype(BF)
        cross_t = jnp.transpose(cross * scale)
        lane = lax.broadcasted_iota(jnp.int32, (SEG, width), 1) // HEAD_DIM
        q = qs[m][here, :] * BF(HEAD_DIM ** -0.5)
        zero = jnp.zeros_like(q)
        q_heads = [jnp.where(lane == h, q, zero) for h in range(heads)]
        g_heads = [jnp.where(lane == h, go, zero) for h in range(heads)]
        deltas = [
            jnp.sum(cross_t[h * HEAD_DIM:(h + 1) * HEAD_DIM], axis=0, keepdims=True) for h in range(heads)
        ]
        tops = lses[m][step]
        dqt[...] = jnp.zeros_like(dqt)

        def slot_block(slot):
            here_slot = slot == DEPTH
            source = seg
            for j in range(DEPTH):
                source = jnp.where(slot == j, found[j], source)
            at = 4 * xor4(lax.div(source, 4), member) + xor4(lax.rem(source, 4), shard)
            key_row = lax.broadcasted_iota(jnp.int32, (SEG, SEG), 0)
            query_col = lax.broadcasted_iota(jnp.int32, (SEG, SEG), 1)
            last = jnp.where(here_slot, 0, jnp.where(slot < steps_up, SEG, -SEG))
            bias[...] = jnp.where(key_row <= query_col + last, 0.0, NEGATIVE)
            k = kt[at]
            v = vt[at]
            k_t = jnp.transpose(k)
            dk = jnp.zeros((SEG, width), F32)
            dv = jnp.zeros((SEG, width), F32)
            for h in range(heads):
                p = jnp.exp(mm(k, q_heads[h], NT) + bias[...] - tops[h:h + 1, :])
                dv += mm(p.astype(BF), g_heads[h])
                dp = mm(v, g_heads[h], NT)
                ds = (p * (dp - deltas[h])).astype(BF)
                dk += mm(ds, q_heads[h])
                dqt[pl.ds(h * HEAD_DIM, HEAD_DIM), :] += mm(k_t[h * HEAD_DIM:(h + 1) * HEAD_DIM], ds)
            contrib_k[step * slots + slot] = dk.astype(BF)
            contrib_v[step * slots + slot] = dv.astype(BF)
            if m == 0:
                gather_turn(step, slot)

        each(slots, slot_block)
        grads[m, here, 0:width] = (jnp.transpose(dqt[...]) * HEAD_DIM ** -0.5).astype(BF)

    def combine(m, r):
        def one(line):
            seg = xor4(jnp.int32(r), member) * per + xor4(line, shard)
            dk = jnp.zeros((SEG, width), F32)
            dv = jnp.zeros((SEG, width), F32)
            for step in range(4):
                own = member * per + other(shard, step)
                steps_up, found = climb(parents, (m * trees + tree) * SEGS, own)
                at = jnp.where(seg == own, step * slots + DEPTH, 4 * slots)
                for j in range(DEPTH):
                    hit = jnp.logical_and(found[j] == seg, j < steps_up)
                    at = jnp.where(hit, step * slots + j, at)
                dk = dk + contrib_k[at].astype(F32)
                dv = dv + contrib_v[at].astype(F32)
            dkp[m][4 * r + line] = dk.astype(BF)
            dvp[m][4 * r + line] = dv.astype(BF)

        each(4, one)

    def piece(ref, r):
        return ref.at[pl.ds(4 * r, 4)]

    def first_sends(m):
        combine(m, 3)
        copies = [
            remote(piece(dkp[m], 3), inbox.at[m, 0], dp_peer(2)),
            remote(piece(dvp[m], 3), inbox.at[m, 1], dp_peer(1)),
        ]
        combine(m, 2)
        copies.append(remote(piece(dkp[m], 2), inbox.at[m, 2], dp_peer(2)))
        combine(m, 1)
        copies.append(remote(piece(dvp[m], 1), inbox.at[m, 3], dp_peer(1)))
        combine(m, 0)
        return copies

    def second_pair(m):
        return [
            prepare(inner.at[m, 0], inbox.at[m, 4], dp_peer(1)),
            prepare(inner.at[m, 1], inbox.at[m, 5], dp_peer(2)),
        ]

    def second_sends(m, first, second):
        for i, own in enumerate((piece(dkp[m], 1), piece(dvp[m], 2))):
            first[i].wait_recv()

            def one(n):
                inner[m, i, n] = (own[n].astype(F32) + inbox[m, i, n].astype(F32)).astype(BF)

            each(4, one)
            second[i].start()

    def own_rows(m, kind, own, slots_in):
        def one(n):
            total = own[n].astype(F32)
            for i in slots_in:
                total = total + inbox[m, i, n].astype(F32)
            grads[m, tile(n), kind * width:(kind + 1) * width] = total.astype(BF)

        each(4, one)

    def own_key(m, first, second):
        first[2].wait_recv()
        second[0].wait_recv()
        own_rows(m, 1, piece(dkp[m], 0), (2, 4))

    def own_value(m, first, second):
        first[3].wait_recv()
        second[1].wait_recv()
        own_rows(m, 2, piece(dvp[m], 0), (3, 5))

    def out_rows(n):
        acc[3, tile(n), :] = mm(big[0, :, tile(n)], os0[...], TN) + mm(big[1, :, tile(n)], os1[...], TN)

    def weight_rows(m, kind):
        cols = slice(kind * width, (kind + 1) * width)

        def one(n):
            part = mm(big[m, :, tile(n)], grads[m, :, cols], TN)
            acc[kind, tile(n), :] = part if m == 0 else acc[kind, tile(n), :] + part

        each(model // SEG, one)

    def input_rows(m, old):
        def block(r, out):
            def one(n):
                part = jnp.zeros((rows, SEG), F32)
                for kind in range(3):
                    part += mm(
                        grads[m, r * rows:(r + 1) * rows, kind * width:(kind + 1) * width],
                        weight[kind, tile(n), :],
                        NT,
                    )
                out[:, tile(n)] = part.astype(out.dtype)

            each(model // SEG, one)

        for copy in old:
            copy.wait_send()
            pending[:] = [kept for kept in pending if kept is not copy]
        block(3, core_out.at[0])
        hop3 = remote(core_out.at[0], core_in.at[m, 0], {"tensor": near})
        block(2, din.at[m])
        hop3.wait_recv()
        y_out[...] = (din[m] + core_in[m, 0].astype(F32)).astype(BF)
        hop = remote(y_out, y_in.at[m], {"tensor": far})
        block(1, core_out.at[1])
        hop1 = remote(core_out.at[1], core_in.at[m, 1], {"tensor": near})
        block(0, din.at[m])
        return hop1, hop, hop3

    chunk = 32

    def input_norms(m, hops):
        hops[0].wait_recv()
        hops[1].wait_recv()

        def one(i):
            at = pl.ds(pl.multiple_of(i * chunk, chunk), chunk)
            dh1 = din[m, at] + core_in[m, 1, at].astype(F32) + y_in[m, at].astype(F32)
            values = x[m, at].astype(F32)
            center = values - jnp.mean(values, axis=-1, keepdims=True)
            inverse = lax.rsqrt(jnp.mean(center * center, axis=-1, keepdims=True) + EPSILON)
            normed = center * inverse
            small[0] += jnp.sum((dh1 * normed).reshape(chunk // 8, 8, model), axis=0)
            din[m, at] = dr1[m, at] + norm_backward(dh1 * pre[...], normed, inverse)

        each(rows // chunk, one)

    class Chain:
        def __init__(self, kind):
            self.kind, self.base, self.size, self.at, self.step = kind, 0, model, 0, 0
            self.copy, self.back, self.done = None, False, False

        def reduce_send(self):
            mask = bits[self.step]
            half = self.size // 2
            out = pl.ds(pl.multiple_of(self.base + (1 - bit_of(mask)) * half, 16), half)
            slot = pl.ds(self.at, half)
            stage[self.kind, slot, :] = acc[self.kind, out, :].astype(BF)
            self.copy = remote(stage.at[self.kind, slot, :], arrived.at[self.kind, slot, :], dp_peer(mask))
            self.base, self.size = self.base + bit_of(mask) * half, half

        def reduce_wait(self):
            self.copy.wait_recv()
            mine = pl.ds(pl.multiple_of(self.base, 16), self.size)
            total = acc[self.kind, mine, :] + arrived[self.kind, pl.ds(self.at, self.size), :].astype(F32)
            self.at += self.size
            self.step += 1
            if self.step < len(bits):
                acc[self.kind, mine, :] = total
            else:
                res[self.kind, mine, :] = total.astype(BF)

        def gather_send(self):
            self.step -= 1
            mask = bits[self.step]
            mine = pl.ds(pl.multiple_of(self.base, 16), self.size)
            self.copy = remote(res.at[self.kind, mine, :], res.at[self.kind, mine, :], dp_peer(mask))
            self.base, self.size = self.base - bit_of(mask) * self.size, 2 * self.size

        def go(self):
            if self.back:
                self.copy.wait_recv()
                if self.step:
                    self.gather_send()
                else:
                    self.done = True
            else:
                self.reduce_wait()
                if self.step < len(bits):
                    self.reduce_send()
                else:
                    self.back = True
                    self.gather_send()

    small[...] = jnp.zeros_like(small)
    small[1:4] = mid_gains[...].reshape(3, 8, model)
    contrib_k[4 * slots] = jnp.zeros((SEG, width), BF)
    contrib_v[4 * slots] = jnp.zeros((SEG, width), BF)
    for copy, part in zip(in_share, gathers[0]):
        copy.wait()
        part.start()
    in_du.wait()
    query, mixer, key, value = [Chain(kind) for kind in (0, 3, 1, 2)]
    each(model // SEG, out_rows)
    mixer.reduce_send()
    in_full = fetch(full_hbm, big)
    in_rest = [fetch(x_hbm, x), fetch(dr1_hbm, dr1)]
    for copy in in_tree:
        copy.wait()

    each(4, lambda step: attend_back(0, step))
    in_tree = fetch_tree(1)
    first0 = first_sends(0)
    second0 = second_pair(0)
    mixer.go()
    for copy in in_tree:
        copy.wait()

    def back1(step):
        attend_back(1, step)

        @pl.when(step == 1)
        def _():
            second_sends(0, first0, second0)

    each(4, back1)
    first1 = first_sends(1)
    second1 = second_pair(1)
    mixer.go()
    in_full.wait()
    weight_rows(0, 0)
    weight_rows(1, 0)
    query.reduce_send()
    own_key(0, first0, second0)
    own_value(0, first0, second0)
    for copy in in_rest:
        copy.wait()
    hops0 = input_rows(0, ())
    second_sends(1, first1, second1)
    weight_rows(0, 1)
    weight_rows(0, 2)
    query.go()
    mixer.go()
    input_norms(0, hops0)
    query.go()
    own_key(1, first1, second1)
    weight_rows(1, 1)
    key.reduce_send()
    own_value(1, first1, second1)
    weight_rows(1, 2)
    value.reduce_send()
    query.go()
    mixer.go()
    hops1 = input_rows(1, hops0)
    key.go()
    value.go()
    query.go()
    mixer.go()
    input_norms(1, hops1)
    totals = jnp.zeros((8, model), F32)
    place_row = lax.broadcasted_iota(jnp.int32, (8, model), 0)
    for i in range(5):
        totals = jnp.where(place_row == i, jnp.sum(small[i], axis=0, keepdims=True), totals)
    small[0] = totals
    small_copy = remote(small.at[0], small_in.at[0], {"tensor": near})
    key.go()
    value.go()
    query.go()
    mixer.go()
    small_copy.wait_recv()
    small[1] = small[0] + jnp.where(place_row < 3, small_in[0], 0.0)
    small_copy = remote(small.at[1], small_in.at[1], {"tensor": far})
    key.go()
    value.go()
    small_copy.wait_recv()
    small[2] = small[1] + jnp.where(place_row < 3, small_in[1], 0.0)
    for step, mask in enumerate(bits):
        small_copy = remote(small.at[2 + step], small_in.at[2 + step], dp_peer(mask))
        for chain in (key, value, query, mixer):
            if not chain.done:
                chain.go()
        small_copy.wait_recv()
        small[3 + step] = small[2 + step] + small_in[2 + step]
    while not (key.done and value.done and query.done and mixer.done):
        for chain in (key, value, query, mixer):
            if not chain.done:
                chain.go()
    small_out[...] = small[2 + len(bits)]

    for copy in gathers[-1]:
        copy.wait_recv()
    for copy in pending:
        copy.wait_send()


def closing_call(parents, qs, os_pair, lses, scale_row, weight, pre, mid_gains, kt, vt, dos, outs, full, du, x, dr1, shares):
    micro, rows, model = x.shape
    tokens, width = qs[0].shape
    size = lax.axis_size("dp")
    bits = tuple(2**b for b in range(size.bit_length() - 1))
    vmem = pl.BlockSpec(memory_space=pltpu.VMEM)
    count, lines = shares.shape[0], shares.shape[1]
    slots = DEPTH + 1
    segs = pltpu.VMEM((4 * tokens // SEG, SEG, width), BF)
    return pl.pallas_call(
        partial(closing, bits),
        out_shape=(
            jax.ShapeDtypeStruct((micro, rows, model), F32),
            jax.ShapeDtypeStruct((4, model, width), BF),
            jax.ShapeDtypeStruct((8, model), F32),
            jax.ShapeDtypeStruct((2, count // 2, lines * size, model), BF),
        ),
        in_specs=[pl.BlockSpec(memory_space=pltpu.SMEM)] + [vmem] * 11 + [HBM] * 9,
        out_specs=(vmem, vmem, vmem, HBM),
        scratch_shapes=[
            segs,
            segs,
            pltpu.VMEM((tokens, width), F32),
            pltpu.VMEM((tokens, width), F32),
            pltpu.VMEM((SEG, SEG), F32),
            pltpu.VMEM((width, SEG), F32),
            pltpu.VMEM((4 * slots + 1, SEG, width), BF),
            pltpu.VMEM((4 * slots + 1, SEG, width), BF),
            segs,
            segs,
            segs,
            segs,
            pltpu.VMEM((micro, 6, tokens // SEG, SEG, width), BF),
            pltpu.VMEM((micro, 2, tokens // SEG, SEG, width), BF),
            pltpu.VMEM((micro, tokens, 3 * width), BF),
            pltpu.VMEM((4, model, width), F32),
            pltpu.VMEM((4, model, width), BF),
            pltpu.VMEM((4, model, width), BF),
            pltpu.VMEM((2, rows, model), BF),
            pltpu.VMEM((micro, 2, rows, model), BF),
            pltpu.VMEM((rows, model), BF),
            pltpu.VMEM((micro, rows, model), BF),
            pltpu.VMEM((3 + len(bits) + 2, 8, model), F32),
            pltpu.VMEM((2 + len(bits), 8, model), F32),
            pltpu.VMEM((micro, tokens, model), BF),
            pltpu.VMEM((micro, rows, model), BF),
            pltpu.VMEM((micro, rows, model), F32),
            pltpu.SemaphoreType.DMA((28 + 14 * len(bits),)),
            pltpu.SemaphoreType.DMA((28 + 14 * len(bits),)),
            pltpu.SemaphoreType.DMA((20,)),
        ],
        compiler_params=pltpu.CompilerParams(
            collective_id=1, has_side_effects=True, vmem_limit_bytes=62 << 20
        ),
        cost_estimate=pl.CostEstimate(flops=120 * 10**9, transcendentals=0, bytes_accessed=30 << 20),
        name="closing",
    )(
        parents, *qs, *os_pair, *lses, scale_row, weight, pre, mid_gains, shares, kt, vt, dos, *outs, full, du, x, dr1
    )


def body(
    block_input,
    cotangent,
    parent,
    pre_attn_gain,
    qkv_weight,
    head_scale,
    out_weight,
    post_attn_gain,
    pre_ffn_gain,
    fc1_weight,
    ffn_norm_gain,
    fc2_weight,
):
    tokens = cotangent.shape[1]
    width = qkv_weight.shape[2]
    parents = parent.reshape(-1)
    scale_row = jnp.repeat(head_scale, HEAD_DIM)[None, :]

    q0, q1, o0, o1, os0, os1, lse0, lse1, mixed, full1, keys, values = opening_call(
        parents, block_input, pre_attn_gain[None], qkv_weight, scale_row, out_weight
    )
    full1 = full1.reshape(MICRO, tokens, -1)
    du, dos, dr1, f_own, f_far, mid_gains, shares = middle_call(
        (os0, os1),
        mixed,
        block_input,
        cotangent,
        fc1_weight,
        fc2_weight,
        out_weight,
        post_attn_gain[None],
        pre_ffn_gain[None],
        ffn_norm_gain[None],
    )
    f_got = swap(f_far, "tensor", 2)
    outputs = (f_own + f_got.astype(F32)).astype(BF)
    din, narrow, small, whole = closing_call(
        parents,
        (q0, q1),
        (os0, os1),
        (lse0, lse1),
        scale_row,
        qkv_weight,
        pre_attn_gain[None],
        mid_gains,
        keys,
        values,
        dos,
        (o0, o1),
        full1,
        du,
        block_input,
        dr1,
        shares,
    )
    head_grad = small[4, 0:width].reshape(-1, HEAD_DIM).sum(-1)
    whole = whole.reshape(2, -1, whole.shape[-1])
    return (
        outputs,
        din,
        small[0],
        narrow[0:3].astype(F32),
        head_grad,
        narrow[3].T.astype(F32),
        small[1],
        small[2],
        whole[0].astype(F32),
        small[3],
        whole[1].astype(F32),
    )


def solution(mesh):
    in_specs = (
        P(None, ("dp", "tensor"), None),
        P(None, "dp", None),
        P(),
        P(),
        P(None, None, "tensor"),
        P("tensor"),
        P("tensor", None),
        P(),
        P(),
        P(None, "tensor"),
        P("tensor"),
        P("tensor", None),
    )
    out_specs = (
        P(None, ("dp", "tensor"), None),
        P(None, ("dp", "tensor"), None),
        P(),
        P(None, None, "tensor"),
        P("tensor"),
        P("tensor", None),
        P(),
        P(),
        P(None, "tensor"),
        P("tensor"),
        P("tensor", None),
    )
    return jax.shard_map(body, mesh=mesh, in_specs=in_specs, out_specs=out_specs, check_vma=False)
```

```python
from functools import partial

import jax
import jax.numpy as jnp
from jax import lax
from jax.experimental import pallas as pl
from jax.experimental.pallas import tpu as pltpu
from jax.sharding import PartitionSpec as P

HEAD_DIM = 64
FFN = 4096
SEG = 256
SEGS = 16
DEPTH = 5
MICRO = 2

EPSILON = 1e-05
NEGATIVE = -1e30
F32 = jnp.float32
BF = jnp.bfloat16
NN = (((1,), (0,)), ((), ()))
NT = (((1,), (1,)), ((), ()))
TN = (((0,), (0,)), ((), ()))


def mm(a, b, dims=NN):
    return lax.dot_general(a, b, dims, preferred_element_type=F32)


def swap(value, axis, mask):
    return lax.ppermute(value, axis, [(i, i ^ mask) for i in range(lax.axis_size(axis))])


def normalize(values):
    center = values - jnp.mean(values, axis=-1, keepdims=True)
    inverse = lax.rsqrt(jnp.mean(center * center, axis=-1, keepdims=True) + EPSILON)
    return (center * inverse, inverse)


def norm_backward(grad_hat, normed, inverse):
    mean_grad = jnp.mean(grad_hat, axis=-1, keepdims=True)
    mean_cross = jnp.mean(grad_hat * normed, axis=-1, keepdims=True)
    return inverse * (grad_hat - mean_grad - normed * mean_cross)


def climb(parents, base, seg):
    found = []
    current = seg
    count = jnp.int32(0)
    for _ in range(DEPTH):
        up = parents[base + current]
        valid = up >= 0
        count = count + valid.astype(jnp.int32)
        current = jnp.where(valid, up, current)
        found.append(current)
    return count, found


HBM = pl.BlockSpec(memory_space=pl.ANY)


def gelu_parts(c):
    root = 0.7978845608028654
    square = c * c
    tanh = jnp.tanh(root * (c + 0.044715 * (square * c)))
    act = 0.5 * c * (1.0 + tanh)
    slope = 0.5 * (1.0 + tanh) + 0.5 * c * (1.0 - tanh * tanh) * (root * (1.0 + 3 * 0.044715 * square))
    return act, slope


def other(shard, mask):
    near = shard + 1 - 2 * (shard % 2)
    return {0: shard, 1: near, 2: (shard + 2) % 4, 3: (near + 2) % 4}[mask]


def xor4(a, b):
    return 2 * lax.rem(lax.div(a, 2) + lax.div(b, 2), 2) + lax.rem(a + b, 2)


def opening(
    parents, x, gain, weight, scale_ref, out_w,
    q0, q1, o0, o1, os0, os1, lse0, lse1, mixed, full_hbm, kt_hbm, vt_hbm,
    full, kt0, kt1, vt0, vt1, picked_k, picked_v, core_out, core_in, y_out, y_in, send, recv, local,
):
    shard = lax.axis_index("tensor")
    index = lax.axis_index("dp")
    near, far = {"tensor": other(shard, 1)}, {"tensor": other(shard, 2)}
    beside, beyond = [{"dp": index + mask - 2 * mask * ((index // mask) % 2)} for mask in (1, 2)]
    rows, model = x.shape[1], x.shape[2]
    width = q0.shape[1]
    heads = width // HEAD_DIM
    tokens = 4 * rows
    per = tokens // SEG
    member, tree = index % 4, index // 4
    trees = parents.shape[0] // (MICRO * SEGS)
    qs, os_, oss, lses = (q0, q1), (o0, o1), (os0, os1), (lse0, lse1)
    kts, vts = (kt0, kt1), (vt0, vt1)
    used = [0]
    pending = []

    def remote(src, dst, target):
        i = used[0]
        used[0] += 1
        copy = pltpu.make_async_remote_copy(
            src_ref=src, dst_ref=dst, send_sem=send.at[i], recv_sem=recv.at[i],
            device_id=target, device_id_type=pl.DeviceIdType.MESH,
        )
        copy.start()
        pending.append(copy)
        return copy

    stores = []

    def store(src, dst):
        copy = pltpu.make_async_copy(src, dst, local.at[len(stores)])
        copy.start()
        stores.append(copy)

    def each(count, fn):
        lax.fori_loop(0, count, lambda i, c: (fn(i), c)[1], 0)

    barrier = pltpu.get_barrier_semaphore()
    for target in (near, far, beside, beyond):
        pl.semaphore_signal(barrier, inc=1, device_id=target, device_id_type=pl.DeviceIdType.MESH)

    chunk = 32

    def norms(m):
        def one(i):
            at = pl.ds(pl.multiple_of(i * chunk, chunk), chunk)
            values = x[m, at].astype(F32)
            center = values - jnp.mean(values, axis=-1, keepdims=True)
            inverse = lax.rsqrt(jnp.mean(center * center, axis=-1, keepdims=True) + EPSILON)
            full[m, 0, at] = (center * inverse * gain[...]).astype(BF)

        each(rows // chunk, one)

    def spread(m):
        return remote(full.at[m, 0], full.at[m, 2], far), remote(full.at[m, 0], full.at[m, 1], near)

    def project(m, first):
        for r in (first, first + 1):
            kts[m][r] = mm(full[m, r], weight[1]).astype(BF)
            vts[m][r] = mm(full[m, r], weight[2]).astype(BF)

    def queries(m):
        for r in range(4):
            qs[m][r * rows:(r + 1) * rows, :] = mm(full[m, r], weight[0]).astype(BF)

    def piece(ref, r, half):
        return ref.at[pl.ds(4 * r + 2 * half, 2)]

    def share(m, half):
        k, v = kts[m], vts[m]
        return [
            remote(piece(k, 0, half), piece(k, 1, half), beside),
            remote(piece(v, 0, half), piece(v, 2, half), beyond),
            remote(piece(k, 0, half), piece(k, 2, half), beyond),
            remote(piece(v, 0, half), piece(v, 1, half), beside),
        ]

    def forward(m, half, copies):
        copies[0].wait_recv()
        one = remote(piece(kts[m], 1, half), piece(kts[m], 3, half), beyond)
        copies[1].wait_recv()
        return copies[2:] + [one, remote(piece(vts[m], 2, half), piece(vts[m], 3, half), beside)]

    def settle(*groups):
        for copies in groups:
            for copy in copies:
                copy.wait_recv()

    def attend(m, step):
        seg = member * per + xor4(step, shard)
        count, found = climb(parents, (m * trees + tree) * SEGS, seg)
        past = DEPTH * SEG
        for slot in range(DEPTH):
            s = found[slot]
            at = 4 * xor4(lax.div(s, 4), member) + xor4(lax.rem(s, 4), shard)
            picked_k[slot * SEG:(slot + 1) * SEG, :] = kts[m][at]
            picked_v[slot * SEG:(slot + 1) * SEG, :] = vts[m][at]
        here = pl.ds(pl.multiple_of(step * SEG, SEG), SEG)
        picked_k[past:past + SEG, :] = kts[m][step]
        picked_v[past:past + SEG, :] = vts[m][step]
        lane = lax.broadcasted_iota(jnp.int32, (SEG, width), 1) // HEAD_DIM
        row = lax.broadcasted_iota(jnp.int32, (SEG, SEG), 0)
        col = lax.broadcasted_iota(jnp.int32, (SEG, SEG), 1)
        slot_of = lax.broadcasted_iota(jnp.int32, (1, past), 1) // SEG
        bias = jnp.where(slot_of < count, 0.0, NEGATIVE).astype(F32)
        q = qs[m][here, :] * BF(HEAD_DIM ** -0.5)
        lse_lane = lax.broadcasted_iota(jnp.int32, (SEG, 128), 1)
        lse_all = jnp.zeros((SEG, 128), F32)
        out = jnp.zeros((SEG, width), F32)
        for head in range(heads):
            qh = jnp.where(lane == head, q, jnp.zeros_like(q))
            s_past = mm(qh, picked_k[0:past, :], NT) + bias
            s_own = jnp.where(col <= row, mm(qh, picked_k[past:past + SEG, :], NT), NEGATIVE)
            top = jnp.maximum(
                jnp.max(s_past, axis=1, keepdims=True), jnp.max(s_own, axis=1, keepdims=True)
            )
            p_past = jnp.exp(s_past - top)
            p_own = jnp.exp(s_own - top)
            total = jnp.sum(p_past, axis=1, keepdims=True) + jnp.sum(p_own, axis=1, keepdims=True)
            got = mm(p_past.astype(BF), picked_v[0:past, :]) + mm(p_own.astype(BF), picked_v[past:past + SEG, :])
            out = jnp.where(lane == head, got / total, out)
            lse_all = jnp.where(lse_lane == head, top + jnp.log(total), lse_all)
        os_[m][here, :] = out
        oss[m][here, :] = (out * scale_ref[...]).astype(BF)
        lses[m][pl.ds(step, 1)] = jnp.transpose(lse_all)[0:8].reshape(1, 8, SEG)

    norms(0)
    pl.semaphore_wait(barrier, 4)
    far0, near0 = spread(0)
    norms(1)
    far1, near1 = spread(1)
    near0.wait_recv()
    project(0, 0)
    a0 = share(0, 0)
    near1.wait_recv()
    project(1, 0)
    far0.wait_recv()
    cross0 = remote(full.at[0, 2], full.at[0, 3], near)
    cross0.wait_recv()
    project(0, 2)
    b0 = share(0, 1)
    a0 = forward(0, 0, a0)
    queries(0)
    far1.wait_recv()
    cross1 = remote(full.at[1, 2], full.at[1, 3], near)
    b0 = forward(0, 1, b0)
    a1 = share(1, 0)
    cross1.wait_recv()
    project(1, 2)
    b1 = share(1, 1)
    queries(1)
    for m in range(MICRO):
        store(full.at[m], full_hbm.at[m])
    settle(a0, b0)
    lax.fori_loop(0, 2, lambda i, c: (attend(0, i), c)[1], 0)
    a1 = forward(1, 0, a1)
    lax.fori_loop(2, 4, lambda i, c: (attend(0, i), c)[1], 0)
    b1 = forward(1, 1, b1)

    def mix(r):
        return mm(os0[r * rows:(r + 1) * rows, :], out_w[...])

    core_out[0] = mix(3).astype(BF)
    hop3 = remote(core_out.at[0], core_in.at[0], near)
    core_out[1] = mix(1).astype(BF)
    hop1 = remote(core_out.at[1], core_in.at[1], near)
    mixed[...] = mix(2)
    hop3.wait_recv()
    y_out[...] = (mixed[...] + core_in[0].astype(F32)).astype(BF)
    hop2 = remote(y_out, y_in, far)
    hop1.wait_recv()
    mixed[...] = mix(0) + core_in[1].astype(F32)
    store(kt0, kt_hbm.at[0])
    store(vt0, vt_hbm.at[0])
    settle(a1, b1)
    store(kt1, kt_hbm.at[1])
    store(vt1, vt_hbm.at[1])
    lax.fori_loop(0, 4, lambda i, c: (attend(1, i), c)[1], 0)
    hop2.wait_recv()
    mixed[...] = mixed[...] + y_in[...].astype(F32)
    for copy in pending:
        copy.wait_send()
    for copy in stores:
        copy.wait()


def opening_call(parents, x, gain, weight, scale_row, out_w):
    micro, rows, model = x.shape
    width = weight.shape[2]
    tokens = 4 * rows
    vmem = pl.BlockSpec(memory_space=pltpu.VMEM)
    narrow = jax.ShapeDtypeStruct((tokens, width), BF)
    narrow_wide = jax.ShapeDtypeStruct((tokens, width), F32)
    tops = jax.ShapeDtypeStruct((tokens // SEG, 8, SEG), F32)
    trees = jax.ShapeDtypeStruct((micro, 4 * tokens // SEG, SEG, width), BF)
    return pl.pallas_call(
        opening,
        out_shape=(
            narrow, narrow, narrow_wide, narrow_wide, narrow, narrow, tops, tops,
            jax.ShapeDtypeStruct((rows, model), F32),
            jax.ShapeDtypeStruct((micro, 4, rows, model), BF),
            trees, trees,
        ),
        in_specs=[pl.BlockSpec(memory_space=pltpu.SMEM)] + [vmem] * 5,
        out_specs=(vmem,) * 9 + (HBM,) * 3,
        scratch_shapes=[pltpu.VMEM((micro, 4, rows, model), BF)]
        + [pltpu.VMEM((4 * tokens // SEG, SEG, width), BF)] * 4
        + [pltpu.VMEM(((DEPTH + 1) * SEG, width), BF)] * 2
        + [pltpu.VMEM((2, rows, model), BF)] * 2
        + [pltpu.VMEM((rows, model), BF)] * 2
        + [
            pltpu.SemaphoreType.DMA((36,)),
            pltpu.SemaphoreType.DMA((36,)),
            pltpu.SemaphoreType.DMA((8,)),
        ],
        compiler_params=pltpu.CompilerParams(
            collective_id=2, has_side_effects=True, vmem_limit_bytes=61 << 20
        ),
        cost_estimate=pl.CostEstimate(flops=60 * 10**9, transcendentals=0, bytes_accessed=20 << 20),
        name="opening",
    )(parents, x, gain, weight, scale_row, out_w)


def middle(
    bits, os0, os1, mixed0, x, g_hbm, fc1_hbm, fc2_hbm, out_w, post, pre, wide,
    du_hbm, dos, dr1, f_own, f_far, gains, shares,
    fc1, fc2, gd, du, act, slz, dzc, full, core_out, core_in, y_out, y_in, nu, inv, st_out, st_in, sums, cols,
    arrived, send, recv, local,
):
    shard = lax.axis_index("tensor")
    index = lax.axis_index("dp")

    def bit_of(mask):
        return (index // mask) % 2

    def dp_peer(mask):
        return {"dp": index + mask - 2 * mask * bit_of(mask)}

    peers = [other(shard, k) for k in range(4)]
    rows = x.shape[1]
    model = x.shape[2]
    hidden = fc1.shape[1]
    parts = hidden // SEG
    used = [0]
    pending = []

    def remote(src, dst, target):
        i = used[0]
        used[0] += 1
        if not isinstance(target, dict):
            target = {"tensor": peers[target]}
        copy = pltpu.make_async_remote_copy(
            src_ref=src, dst_ref=dst, send_sem=send.at[i], recv_sem=recv.at[i],
            device_id=target, device_id_type=pl.DeviceIdType.MESH,
        )
        copy.start()
        pending.append(copy)
        return copy

    stored = [0]
    stores = []

    def store(src, dst):
        i = stored[0]
        stored[0] += 1
        copy = pltpu.make_async_copy(src, dst, local.at[i])
        copy.start()
        stores.append(copy)

    def fetch(src, dst):
        i = stored[0]
        stored[0] += 1
        copy = pltpu.make_async_copy(src, dst, local.at[i])
        copy.start()
        return copy

    got_fc2 = fetch(fc2_hbm, fc2)
    got_g = [
        [fetch(g_hbm.at[m, pl.ds(peers[r] * rows, rows), :], gd.at[m, r]) for r in range(4)] for m in range(MICRO)
    ]
    got_fc1 = fetch(fc1_hbm, fc1)
    barrier = pltpu.get_barrier_semaphore()
    targets = [{"tensor": peers[mask]} for mask in (1, 2, 3)] + [dp_peer(mask) for mask in bits]
    for target in targets:
        pl.semaphore_signal(barrier, inc=1, device_id=target, device_id_type=pl.DeviceIdType.MESH)
    pl.semaphore_wait(barrier, len(targets))
    gains[...] = jnp.zeros_like(gains)

    def each(count, fn):
        lax.fori_loop(0, count, lambda i, c: (fn(i), c)[1], 0)

    def tile(n):
        return pl.ds(pl.multiple_of(n * SEG, SEG), SEG)

    def merge(value):
        return value.reshape((-1,) + value.shape[2:])

    def reuse(*groups):
        for copies in groups:
            for copy in copies if isinstance(copies, tuple) else (copies,):
                copy.wait_send()
                pending[:] = [other_copy for other_copy in pending if other_copy is not copy]

    def first_hop(kind, m, block, out):
        block(3, core_out.at[m, 0])
        hop3 = remote(core_out.at[m, 0], core_in.at[kind, m, 0], 1)
        block(2, None)
        hop3.wait_recv()
        add_far(kind, m)
        far_hop = remote(y_out.at[m], y_in.at[kind, m], 2)
        block(1, core_out.at[m, 1])
        hop1 = remote(core_out.at[m, 1], core_in.at[kind, m, 1], 1)
        block(0, out)
        return hop3, hop1, far_hop

    chunk = 32

    def chunks(fn):
        each(rows // chunk, lambda i: fn(pl.ds(pl.multiple_of(i * chunk, chunk), chunk)))

    def add_far(kind, m):
        def one(at):
            y_out[m, at] = (sums_far[m][at] + core_in[kind, m, 0, at].astype(F32)).astype(BF)

        chunks(one)

    sums_far = [f_own.at[m] for m in range(MICRO)]
    def mixed_block():
        def block(r, out):
            part = mm(os1[r * rows:(r + 1) * rows, :], out_w[...])
            if r == 2:
                sums_far[1][...] = part
            else:
                out[...] = part.astype(out.dtype)

        return block

    def project_grad(m):
        for r in range(4):
            got_g[m][r].wait()

        def one(i):
            r, n = i // parts, i % parts
            dzc[m, pl.ds(pl.multiple_of(r * rows, rows), rows), tile(n)] = mm(gd[m, r], fc2[tile(n), :], NT).astype(BF)

        each(4 * parts, one)

    def own_sum(kind, m, base, at):
        return base + core_in[kind, m, 1, at].astype(F32) + y_in[kind, m, at].astype(F32)

    def norm_two(m, at, residual):
        center = residual - jnp.mean(residual, axis=-1, keepdims=True)
        inverse = lax.rsqrt(jnp.mean(center * center, axis=-1, keepdims=True) + EPSILON)
        return center * inverse, inverse

    def forward_norms(m, hops=None):
        if m:
            hops[1].wait_recv()
            hops[2].wait_recv()

        def one(at):
            mixed, inverse = norm_two(m, at, own_sum(0, m, nu[m, at], at) if m else mixed0[at, :])
            nu[m, at] = mixed
            inv[m, at] = jnp.broadcast_to(inverse, (chunk, 128))
            residual = x[m, at].astype(F32) + mixed * post[...]
            normed, _ = norm_two(m, at, residual)
            full[m, 0, at] = (normed * pre[...]).astype(BF)

        chunks(one)

    def spread(m, buf):
        return remote(buf.at[m, 0], buf.at[m, 2], 2), remote(buf.at[m, 0], buf.at[m, 1], 1)

    def ffn_forward(m, r):
        sums[...] = jnp.zeros_like(sums)

        def one(n):
            value, slope = gelu_parts(mm(full[m, r], fc1[:, tile(n)]))
            act[m, r * rows:(r + 1) * rows, tile(n)] = value
            slz[m, r, :, tile(n)] = slope.astype(BF)
            dna = dzc[m, pl.ds(pl.multiple_of(r * rows, rows), rows), tile(n)].astype(F32) * wide[:, tile(n)]
            for i, term in enumerate((value, value * value, dna, dna * value)):
                sums[i] += term[:, 0:128] + term[:, 128:256]

        each(parts, one)
        lane = lax.broadcasted_iota(jnp.int32, (rows, 128), 1)
        merged = jnp.zeros((rows, 128), F32)
        for i in range(4):
            merged = jnp.where(lane == i, jnp.sum(sums[i], axis=-1, keepdims=True), merged)
        st_out[m, :, r * rows:(r + 1) * rows] = jnp.transpose(merged)[0:8]

    def send_stats(m):
        return [remote(st_out.at[m], st_in.at[m, mask - 1], mask) for mask in (1, 2, 3)]

    def ffn_backward_rows(m, r):
        total = st_out[m, :, r * rows:(r + 1) * rows]
        for mask in (1, 2, 3):
            b = r ^ mask
            total = total + st_in[m, mask - 1, :, b * rows:(b + 1) * rows]
        cols[0:8, :] = total * (1.0 / FFN)
        flipped = jnp.transpose(cols[...])
        mu, square, m_dna, m_cross = [flipped[:, i:i + 1] for i in range(4)]
        rw = lax.rsqrt(square - mu * mu + EPSILON)
        m_both = (m_cross - mu * m_dna) * rw

        def one(n):
            gain = wide[:, tile(n)]
            dz = dzc[m, pl.ds(pl.multiple_of(r * rows, rows), rows), tile(n)].astype(F32)
            na = (act[m, r * rows:(r + 1) * rows, tile(n)] - mu) * rw
            slope = slz[m, r, :, tile(n)].astype(F32)
            slz[m, r, :, tile(n)] = (na * gain).astype(BF)
            gains[16:24, tile(n)] += jnp.sum((dz * na).reshape(rows // 8, 8, SEG), axis=0)
            dzc[m, pl.ds(pl.multiple_of(r * rows, rows), rows), tile(n)] = (rw * (dz * gain - m_dna - na * m_both) * slope).astype(BF)

        each(parts, one)

    def grad_block(m):
        def block(r, out):
            ffn_backward_rows(m, r)
            if r == 2:
                out = sums_far[m]

            def one(n):
                out[:, tile(n)] = mm(dzc[m, r * rows:(r + 1) * rows, :], fc1[tile(n), :], NT).astype(out.dtype)

            each(model // SEG, one)

        return block

    def ffn_out_block(m):
        def block(r, out):
            def one(n):
                out[:, tile(n)] = mm(slz[m, r], fc2[:, tile(n)]).astype(out.dtype)

            each(model // SEG, one)

        return block

    def backward_norms(m, hop1, far_hop):
        hop1.wait_recv()
        far_hop.wait_recv()

        def one(at):
            dh2 = own_sum(1, m, dr1[m, at], at)
            mixed = nu[m, at]
            residual = x[m, at].astype(F32) + mixed * post[...]
            normed, inverse = norm_two(m, at, residual)
            gains[8:16, :] += jnp.sum((dh2 * normed).reshape(chunk // 8, 8, model), axis=0)
            grad = gd[m, 0, at].astype(F32) + norm_backward(dh2 * pre[...], normed, inverse)
            gains[0:8, :] += jnp.sum((grad * mixed).reshape(chunk // 8, 8, model), axis=0)
            dr1[m, at] = grad
            back = norm_backward(grad * post[...], mixed, inv[m, at][:, 0:1])
            du[m, 0, at] = back.astype(BF)

        chunks(one)

    def unmix(m, r):
        dos[m, r * rows:(r + 1) * rows, :] = mm(du[m, r], out_w[...], NT)

    forward_norms(0)
    far0, near0 = spread(0, full)
    hops = first_hop(0, 1, mixed_block(), nu.at[1])
    got_fc2.wait()
    project_grad(0)
    got_fc1.wait()
    ffn_forward(0, 0)
    near0.wait_recv()
    ffn_forward(0, 1)
    project_grad(1)
    far0.wait_recv()
    cross0 = remote(full.at[0, 2], full.at[0, 3], 1)
    ffn_forward(0, 2)
    cross0.wait_recv()
    ffn_forward(0, 3)
    stats0 = send_stats(0)
    forward_norms(1, hops)
    far1, near1 = spread(1, full)
    ffn_forward(1, 0)
    near1.wait_recv()
    ffn_forward(1, 1)
    for copy in stats0:
        copy.wait_recv()
    hop_a = first_hop(1, 0, grad_block(0), dr1.at[0])
    far1.wait_recv()
    cross1 = remote(full.at[1, 2], full.at[1, 3], 1)
    ffn_forward(1, 2)
    cross1.wait_recv()
    ffn_forward(1, 3)
    stats1 = send_stats(1)

    def first_grad(m):
        def one(n):
            part = mm(merge(full[m, :, :, tile(n)]), dzc[m], TN)
            act[0, tile(n), :] = part if m == 0 else act[0, tile(n), :] + part

        each(parts, one)

    def second_grad(n):
        part = mm(merge(slz[0, :, :, tile(n)]), merge(gd[0]), TN)
        act[1, tile(n), :] = part + mm(merge(slz[1, :, :, tile(n)]), merge(gd[1]), TN)

    first_grad(0)
    for copy in stats1:
        copy.wait_recv()
    reuse(hops)
    hop_b = first_hop(1, 1, grad_block(1), dr1.at[1])
    backward_norms(0, hop_a[1], hop_a[2])
    du_far0, du_near0 = spread(0, du)
    first_grad(1)
    group = hidden // (shares.shape[0] // 2)

    class Chain:
        def __init__(self, number):
            self.number, self.which = number, number // (hidden // group)
            self.start = (number % (hidden // group)) * group
            self.base, self.size, self.at, self.step = self.start, group, self.start, 0
            self.back = False

        def send(self):
            mask = bits[self.step]
            half = self.size // 2
            away = self.base + (1 - bit_of(mask)) * half
            where = self.at

            def one(i):
                src = pl.ds(pl.multiple_of(away + i * 16, 16), 16)
                staged[self.which, pl.ds(pl.multiple_of(where + i * 16, 16), 16), :] = act[
                    self.which, src, :
                ].astype(BF)

            each(half // 16, one)
            slot = pl.ds(where, half)
            self.copy = remote(
                staged.at[self.which, slot, :], arrived.at[self.which, slot, :], dp_peer(mask)
            )
            self.base, self.size = self.base + bit_of(mask) * half, half

        def wait(self):
            self.copy.wait_recv()
            self.step += 1
            base, where, last = self.base, self.at, self.step == len(bits)

            def one(i):
                mine = pl.ds(pl.multiple_of(base + i * 16, 16), 16)
                total = act[self.which, mine, :] + arrived[
                    self.which, pl.ds(pl.multiple_of(where + i * 16, 16), 16), :
                ].astype(F32)
                if last:
                    at = self.start + base - self.first + i * 16
                    staged[self.which, pl.ds(pl.multiple_of(at, 16), 16), :] = total.astype(BF)
                else:
                    act[self.which, mine, :] = total

            each(self.size // 16, one)
            self.at += self.size
            if self.step == 1:
                self.first = base

        def gather(self):
            self.step -= 1
            mask = bits[self.step]
            at = pl.ds(pl.multiple_of(self.start + self.base - self.first, 16), self.size)
            self.copy = remote(staged.at[self.which, at, :], staged.at[self.which, at, :], dp_peer(mask))
            self.base, self.size = self.base - bit_of(mask) * self.size, 2 * self.size

        def go(self):
            if self.back:
                self.copy.wait_recv()
            else:
                self.wait()
                self.back = self.step == len(bits)
            if not self.back:
                reuse(self.copy)
                self.send()
            elif self.which == 0 and self.step > 1:
                self.gather()
            else:
                half = group // 2
                store(staged.at[self.which, pl.ds(self.start, half), :], shares.at[self.number])

    chains = [Chain(i) for i in range(shares.shape[0])]
    half_chains = len(chains) // 2
    staged = dzc
    for chain in chains[:half_chains]:
        chain.send()
    per_chain = parts // half_chains
    for i, chain in enumerate(chains[half_chains:]):
        each(per_chain, lambda n: second_grad(n + i * per_chain))
        chain.send()
    backward_norms(1, hop_b[1], hop_b[2])
    du_far1, du_near1 = spread(1, du)

    def ffn_out(m, hop_old):
        reuse(hop_old, ())
        block = ffn_out_block(m)
        block(3, core_out.at[m, 0])
        hop3 = remote(core_out.at[m, 0], core_in.at[0, m, 0], 1)
        block(1, core_out.at[m, 1])
        hop1 = remote(core_out.at[m, 1], core_in.at[0, m, 1], 1)
        block(2, f_own.at[m])
        hop3.wait_recv()

        def one(at):
            f_far[m, at] = (f_own[m, at] + core_in[0, m, 0, at].astype(F32)).astype(BF)

        chunks(one)
        block(0, f_own.at[m])
        hop1.wait_recv()

        def two(at):
            residual = x[m, at].astype(F32) + nu[m, at] * post[...]
            f_own[m, at] = residual + f_own[m, at] + core_in[0, m, 1, at].astype(F32)

        chunks(two)

    todo = [
        chains[turn - level]
        for turn in range(len(chains) + 2 * len(bits) - 2)
        for level in range(2 * len(bits) - 1)
        if 0 <= turn - level < (half_chains if level >= len(bits) else len(chains))
    ]

    def advance(count):
        for _ in range(min(count, len(todo))):
            todo.pop(0).go()

    slice_of = -(-len(todo) // 5)
    ffn_out(0, hop_a)
    unmix(0, 0)
    du_near0.wait_recv()
    unmix(0, 1)
    du_far0.wait_recv()
    du_cross0 = remote(du.at[0, 2], du.at[0, 3], 1)
    unmix(0, 2)
    advance(slice_of)
    du_cross0.wait_recv()
    unmix(0, 3)
    ffn_out(1, hop_b)
    advance(slice_of)
    unmix(1, 0)
    du_near1.wait_recv()
    unmix(1, 1)
    for r in range(4):
        store(du.at[0, r], du_hbm.at[0, pl.ds(r * rows, rows), :])
    du_far1.wait_recv()
    du_cross1 = remote(du.at[1, 2], du.at[1, 3], 1)
    unmix(1, 2)
    advance(slice_of)
    du_cross1.wait_recv()
    unmix(1, 3)
    for r in range(4):
        store(du.at[1, r], du_hbm.at[1, pl.ds(r * rows, rows), :])
    advance(len(todo))
    for copy in pending:
        copy.wait_send()
    for copy in stores:
        copy.wait()


def middle_call(os_pair, mixed, x, g, fc1, fc2, out_w, post, pre, wide):
    micro, rows, model = x.shape
    hidden = fc1.shape[1]
    width = out_w.shape[0]
    tokens = 4 * rows
    vmem = pl.BlockSpec(memory_space=pltpu.VMEM)
    wide_rows = jax.ShapeDtypeStruct((micro, tokens, model), BF)
    own = jax.ShapeDtypeStruct((micro, rows, model), F32)
    size = lax.axis_size("dp")
    bits = tuple(2**b for b in range(size.bit_length() - 1))
    group = max(SEG, 16 * size)
    count = 2 * hidden // group
    return pl.pallas_call(
        partial(middle, bits),
        out_shape=(
            wide_rows,
            jax.ShapeDtypeStruct((micro, tokens, width), F32),
            own, own,
            jax.ShapeDtypeStruct((micro, rows, model), BF),
            jax.ShapeDtypeStruct((24, model), F32),
            jax.ShapeDtypeStruct((count, group // 2, model), BF),
        ),
        in_specs=[vmem, vmem, vmem, vmem, HBM, HBM, HBM, vmem, vmem, vmem, vmem],
        out_specs=(HBM, vmem, vmem, vmem, vmem, vmem, HBM),
        scratch_shapes=[
            pltpu.VMEM((model, hidden), BF),
            pltpu.VMEM((hidden, model), BF),
            pltpu.VMEM((micro, 4, rows, model), BF),
            pltpu.VMEM((micro, 4, rows, model), BF),
            pltpu.VMEM((micro, tokens, hidden), F32),
            pltpu.VMEM((micro, 4, rows, hidden), BF),
            pltpu.VMEM((micro, tokens, hidden), BF),
            pltpu.VMEM((micro, 4, rows, model), BF),
            pltpu.VMEM((micro, 2, rows, model), BF),
            pltpu.VMEM((2, micro, 2, rows, model), BF),
            pltpu.VMEM((micro, rows, model), BF),
            pltpu.VMEM((2, micro, rows, model), BF),
            pltpu.VMEM((micro, rows, model), F32),
            pltpu.VMEM((micro, rows, 128), F32),
            pltpu.VMEM((micro, 8, tokens), F32),
            pltpu.VMEM((micro, 3, 8, tokens), F32),
            pltpu.VMEM((4, rows, 128), F32),
            pltpu.VMEM((128, rows), F32),
            pltpu.VMEM((2, hidden, model), BF),
            pltpu.SemaphoreType.DMA((40 + 2 * count * len(bits),)),
            pltpu.SemaphoreType.DMA((40 + 2 * count * len(bits),)),
            pltpu.SemaphoreType.DMA((20 + count,)),
        ],
        compiler_params=pltpu.CompilerParams(
            collective_id=0, has_side_effects=True, vmem_limit_bytes=61 << 20
        ),
        cost_estimate=pl.CostEstimate(flops=100 * 10**9, transcendentals=0, bytes_accessed=40 << 20),
        name="middle",
    )(*os_pair, mixed, x, g, fc1, fc2, out_w, post, pre, wide)


def closing(bits, parents, *refs):
    q0, q1, os0, os1, lse0, lse1, scale_ref, weight, pre, mid_gains = refs[0:10]
    shares, kt_hbm, vt_hbm, dos_hbm, o0_hbm, o1_hbm, full_hbm, du_hbm, x_hbm, dr1_hbm = refs[10:20]
    din, res, small_out, ffn = refs[20:24]
    (
        kt, vt, dos, o, bias, dqt, contrib_k, contrib_v, dkp0, dkp1, dvp0, dvp1, inbox, inner, grads, acc, stage,
        arrived, core_out, core_in, y_out, y_in, small, small_in, big, x, dr1, send, recv, local,
    ) = refs[24:]
    shard = lax.axis_index("tensor")
    index = lax.axis_index("dp")
    near, far = other(shard, 1), other(shard, 2)
    rows, model = x.shape[1], x.shape[2]
    tokens, width = q0.shape
    heads = width // HEAD_DIM
    per = tokens // SEG
    member, tree = index % 4, index // 4
    trees = parents.shape[0] // (MICRO * SEGS)
    qs, lses, os_hbm = (q0, q1), (lse0, lse1), (o0_hbm, o1_hbm)
    dkp, dvp = (dkp0, dkp1), (dvp0, dvp1)
    slots = DEPTH + 1

    def bit_of(mask):
        return (index // mask) % 2

    def dp_peer(mask):
        return {"dp": index + mask - 2 * mask * bit_of(mask)}

    used = [0]
    pending = []

    def prepare(src, dst, target):
        i = used[0]
        used[0] += 1
        copy = pltpu.make_async_remote_copy(
            src_ref=src, dst_ref=dst, send_sem=send.at[i], recv_sem=recv.at[i],
            device_id=target, device_id_type=pl.DeviceIdType.MESH,
        )
        pending.append(copy)
        return copy

    def remote(src, dst, target):
        copy = prepare(src, dst, target)
        copy.start()
        return copy

    fetched = [0]

    def fetch(src, dst):
        i = fetched[0]
        fetched[0] += 1
        copy = pltpu.make_async_copy(src, dst, local.at[i])
        copy.start()
        return copy

    def each(count, fn):
        lax.fori_loop(0, count, lambda i, c: (fn(i), c)[1], 0)

    def tile(n):
        return pl.ds(pl.multiple_of(n * SEG, SEG), SEG)

    barrier = pltpu.get_barrier_semaphore()
    targets = [{"tensor": near}, {"tensor": far}] + [dp_peer(mask) for mask in bits]
    for target in targets:
        pl.semaphore_signal(barrier, inc=1, device_id=target, device_id_type=pl.DeviceIdType.MESH)

    def fetch_tree(m):
        return [
            fetch(kt_hbm.at[m], kt), fetch(vt_hbm.at[m], vt), fetch(dos_hbm.at[m], dos), fetch(os_hbm[m], o)
        ]

    count, half = shares.shape[0] // 2, shares.shape[1]
    lines = 2 * half // 2 ** len(bits)
    base = bit_of(bits[0]) * half
    inside = 0
    for step, mask in enumerate(bits[1:]):
        inside = inside + bit_of(mask) * (half // 2 ** (step + 1))
    cut = max(1, count // 2)
    parts = list(range(0, count, cut))
    whole_half = pl.ds(pl.multiple_of(base, 16), half)
    own_lines = pl.ds(pl.multiple_of(base + inside, 16), lines)
    inside_lines = pl.ds(pl.multiple_of(inside, 16), lines)
    in_share = [
        fetch(shares.at[pl.ds(count + at, cut), inside_lines, :], ffn.at[1, pl.ds(at, cut), own_lines, :])
        for at in parts
    ]
    in_tree = fetch_tree(0)
    in_du = fetch(du_hbm, big)
    in_share.append(fetch(shares.at[pl.ds(0, count)], ffn.at[0, :, whole_half, :]))
    pl.semaphore_wait(barrier, len(targets))
    ready = [
        remote(shares.at[pl.ds(at, cut)], ffn.at[0, pl.ds(at, cut), whole_half, :], dp_peer(bits[0]))
        for at in parts
    ]
    gathers = []
    size, base = lines, base + inside
    for mask in bits[::-1]:
        rows_at = pl.ds(pl.multiple_of(base, 16), size)
        level = []
        for at in parts:
            where = ffn.at[1, pl.ds(at, cut), rows_at, :]
            source = where if gathers else shares.at[pl.ds(count + at, cut), inside_lines, :]
            level.append(prepare(source, where, dp_peer(mask)))
        if not gathers:
            for copy in level:
                copy.start()
        gathers.append(level)
        base, size = base - bit_of(mask) * size, 2 * size

    events = {}
    for level in range(1, len(bits)):
        for part in range(len(parts)):
            turn = (2, 6)[part] if level < len(bits) - 1 else (8, 13)[part]
            events.setdefault(min(23, turn), []).append((level, part))

    def gather_turn(step, slot):
        for turn, moves in sorted(events.items()):

            @pl.when(step * 6 + slot == turn)
            def _():
                for level, part in moves:
                    if level == 1:
                        in_share[part].wait()
                    gathers[level - 1][part].wait_recv()
                    gathers[level][part].start()

    def attend_back(m, step):
        seg = member * per + xor4(step, shard)
        steps_up, found = climb(parents, (m * trees + tree) * SEGS, seg)
        here = pl.ds(pl.multiple_of(step * SEG, SEG), SEG)
        grad_out = dos[here, :]
        cross = grad_out * o[here, :]
        small[4, :, 0:width] += jnp.sum(cross.reshape(SEG // 8, 8, width), axis=0)
        scale = scale_ref[...]
        go = (grad_out * scale).astype(BF)
        cross_t = jnp.transpose(cross * scale)
        lane = lax.broadcasted_iota(jnp.int32, (SEG, width), 1) // HEAD_DIM
        q = qs[m][here, :] * BF(HEAD_DIM ** -0.5)
        zero = jnp.zeros_like(q)
        q_heads = [jnp.where(lane == h, q, zero) for h in range(heads)]
        g_heads = [jnp.where(lane == h, go, zero) for h in range(heads)]
        deltas = [
            jnp.sum(cross_t[h * HEAD_DIM:(h + 1) * HEAD_DIM], axis=0, keepdims=True) for h in range(heads)
        ]
        tops = lses[m][step]
        dqt[...] = jnp.zeros_like(dqt)

        def slot_block(slot):
            here_slot = slot == DEPTH
            source = seg
            for j in range(DEPTH):
                source = jnp.where(slot == j, found[j], source)
            at = 4 * xor4(lax.div(source, 4), member) + xor4(lax.rem(source, 4), shard)
            key_row = lax.broadcasted_iota(jnp.int32, (SEG, SEG), 0)
            query_col = lax.broadcasted_iota(jnp.int32, (SEG, SEG), 1)
            last = jnp.where(here_slot, 0, jnp.where(slot < steps_up, SEG, -SEG))
            bias[...] = jnp.where(key_row <= query_col + last, 0.0, NEGATIVE)
            k = kt[at]
            v = vt[at]
            k_t = jnp.transpose(k)
            dk = jnp.zeros((SEG, width), F32)
            dv = jnp.zeros((SEG, width), F32)
            for h in range(heads):
                p = jnp.exp(mm(k, q_heads[h], NT) + bias[...] - tops[h:h + 1, :])
                dv += mm(p.astype(BF), g_heads[h])
                dp = mm(v, g_heads[h], NT)
                ds = (p * (dp - deltas[h])).astype(BF)
                dk += mm(ds, q_heads[h])
                dqt[pl.ds(h * HEAD_DIM, HEAD_DIM), :] += mm(k_t[h * HEAD_DIM:(h + 1) * HEAD_DIM], ds)
            contrib_k[step * slots + slot] = dk.astype(BF)
            contrib_v[step * slots + slot] = dv.astype(BF)
            if m == 0:
                gather_turn(step, slot)

        each(slots, slot_block)
        grads[m, here, 0:width] = (jnp.transpose(dqt[...]) * HEAD_DIM ** -0.5).astype(BF)

    def combine(m, r):
        def one(line):
            seg = xor4(jnp.int32(r), member) * per + xor4(line, shard)
            dk = jnp.zeros((SEG, width), F32)
            dv = jnp.zeros((SEG, width), F32)
            for step in range(4):
                own = member * per + other(shard, step)
                steps_up, found = climb(parents, (m * trees + tree) * SEGS, own)
                at = jnp.where(seg == own, step * slots + DEPTH, 4 * slots)
                for j in range(DEPTH):
                    hit = jnp.logical_and(found[j] == seg, j < steps_up)
                    at = jnp.where(hit, step * slots + j, at)
                dk = dk + contrib_k[at].astype(F32)
                dv = dv + contrib_v[at].astype(F32)
            dkp[m][4 * r + line] = dk.astype(BF)
            dvp[m][4 * r + line] = dv.astype(BF)

        each(4, one)

    def piece(ref, r):
        return ref.at[pl.ds(4 * r, 4)]

    def first_sends(m):
        combine(m, 3)
        copies = [
            remote(piece(dkp[m], 3), inbox.at[m, 0], dp_peer(2)),
            remote(piece(dvp[m], 3), inbox.at[m, 1], dp_peer(1)),
        ]
        combine(m, 2)
        copies.append(remote(piece(dkp[m], 2), inbox.at[m, 2], dp_peer(2)))
        combine(m, 1)
        copies.append(remote(piece(dvp[m], 1), inbox.at[m, 3], dp_peer(1)))
        combine(m, 0)
        return copies

    def second_pair(m):
        return [
            prepare(inner.at[m, 0], inbox.at[m, 4], dp_peer(1)),
            prepare(inner.at[m, 1], inbox.at[m, 5], dp_peer(2)),
        ]

    def second_sends(m, first, second):
        for i, own in enumerate((piece(dkp[m], 1), piece(dvp[m], 2))):
            first[i].wait_recv()

            def one(n):
                inner[m, i, n] = (own[n].astype(F32) + inbox[m, i, n].astype(F32)).astype(BF)

            each(4, one)
            second[i].start()

    def own_rows(m, kind, own, slots_in):
        def one(n):
            total = own[n].astype(F32)
            for i in slots_in:
                total = total + inbox[m, i, n].astype(F32)
            grads[m, tile(n), kind * width:(kind + 1) * width] = total.astype(BF)

        each(4, one)

    def own_key(m, first, second):
        first[2].wait_recv()
        second[0].wait_recv()
        own_rows(m, 1, piece(dkp[m], 0), (2, 4))

    def own_value(m, first, second):
        first[3].wait_recv()
        second[1].wait_recv()
        own_rows(m, 2, piece(dvp[m], 0), (3, 5))

    def out_rows(n):
        acc[3, tile(n), :] = mm(big[0, :, tile(n)], os0[...], TN) + mm(big[1, :, tile(n)], os1[...], TN)

    def weight_rows(m, kind):
        cols = slice(kind * width, (kind + 1) * width)

        def one(n):
            part = mm(big[m, :, tile(n)], grads[m, :, cols], TN)
            acc[kind, tile(n), :] = part if m == 0 else acc[kind, tile(n), :] + part

        each(model // SEG, one)

    def input_rows(m, old):
        def block(r, out):
            def one(n):
                part = jnp.zeros((rows, SEG), F32)
                for kind in range(3):
                    part += mm(
                        grads[m, r * rows:(r + 1) * rows, kind * width:(kind + 1) * width],
                        weight[kind, tile(n), :],
                        NT,
                    )
                out[:, tile(n)] = part.astype(out.dtype)

            each(model // SEG, one)

        for copy in old:
            copy.wait_send()
            pending[:] = [kept for kept in pending if kept is not copy]
        block(3, core_out.at[0])
        hop3 = remote(core_out.at[0], core_in.at[m, 0], {"tensor": near})
        block(2, din.at[m])
        hop3.wait_recv()
        y_out[...] = (din[m] + core_in[m, 0].astype(F32)).astype(BF)
        hop = remote(y_out, y_in.at[m], {"tensor": far})
        block(1, core_out.at[1])
        hop1 = remote(core_out.at[1], core_in.at[m, 1], {"tensor": near})
        block(0, din.at[m])
        return hop1, hop, hop3

    chunk = 32

    def input_norms(m, hops):
        hops[0].wait_recv()
        hops[1].wait_recv()

        def one(i):
            at = pl.ds(pl.multiple_of(i * chunk, chunk), chunk)
            dh1 = din[m, at] + core_in[m, 1, at].astype(F32) + y_in[m, at].astype(F32)
            values = x[m, at].astype(F32)
            center = values - jnp.mean(values, axis=-1, keepdims=True)
            inverse = lax.rsqrt(jnp.mean(center * center, axis=-1, keepdims=True) + EPSILON)
            normed = center * inverse
            small[0] += jnp.sum((dh1 * normed).reshape(chunk // 8, 8, model), axis=0)
            din[m, at] = dr1[m, at] + norm_backward(dh1 * pre[...], normed, inverse)

        each(rows // chunk, one)

    class Chain:
        def __init__(self, kind, order):
            self.order = order
            self.kind, self.base, self.size, self.at, self.step = kind, 0, model, 0, 0
            self.copy, self.back, self.done = None, False, False

        def reduce_send(self):
            mask = self.order[self.step]
            half = self.size // 2
            out = pl.ds(pl.multiple_of(self.base + (1 - bit_of(mask)) * half, 16), half)
            slot = pl.ds(self.at, half)
            stage[self.kind, slot, :] = acc[self.kind, out, :].astype(BF)
            self.copy = remote(stage.at[self.kind, slot, :], arrived.at[self.kind, slot, :], dp_peer(mask))
            self.base, self.size = self.base + bit_of(mask) * half, half

        def reduce_wait(self):
            self.copy.wait_recv()
            mine = pl.ds(pl.multiple_of(self.base, 16), self.size)
            total = acc[self.kind, mine, :] + arrived[self.kind, pl.ds(self.at, self.size), :].astype(F32)
            self.at += self.size
            self.step += 1
            if self.step < len(bits):
                acc[self.kind, mine, :] = total
            else:
                res[self.kind, mine, :] = total.astype(BF)

        def gather_send(self):
            self.step -= 1
            mask = self.order[self.step]
            mine = pl.ds(pl.multiple_of(self.base, 16), self.size)
            self.copy = remote(res.at[self.kind, mine, :], res.at[self.kind, mine, :], dp_peer(mask))
            self.base, self.size = self.base - bit_of(mask) * self.size, 2 * self.size

        def go(self):
            if self.back:
                self.copy.wait_recv()
                if self.step:
                    self.gather_send()
                else:
                    self.done = True
            else:
                self.reduce_wait()
                if self.step < len(bits):
                    self.reduce_send()
                else:
                    self.back = True
                    self.gather_send()

    small[...] = jnp.zeros_like(small)
    small[1:4] = mid_gains[...].reshape(3, 8, model)
    contrib_k[4 * slots] = jnp.zeros((SEG, width), BF)
    contrib_v[4 * slots] = jnp.zeros((SEG, width), BF)
    in_du.wait()
    turned = bits[1:] + bits[:1]
    query, mixer, key, value = [Chain(*a) for a in ((0, bits), (3, turned), (1, bits), (2, turned))]
    each(model // SEG, out_rows)
    mixer.reduce_send()
    in_full = fetch(full_hbm, big)
    in_rest = [fetch(x_hbm, x), fetch(dr1_hbm, dr1)]
    for copy in in_tree:
        copy.wait()

    each(4, lambda step: attend_back(0, step))
    in_tree = fetch_tree(1)
    first0 = first_sends(0)
    second0 = second_pair(0)
    mixer.go()
    for copy in in_tree:
        copy.wait()

    def back1(step):
        attend_back(1, step)

        @pl.when(step == 1)
        def _():
            second_sends(0, first0, second0)

    each(4, back1)
    first1 = first_sends(1)
    second1 = second_pair(1)
    mixer.go()
    in_full.wait()
    weight_rows(0, 0)
    weight_rows(1, 0)
    query.reduce_send()
    own_key(0, first0, second0)
    own_value(0, first0, second0)
    for copy in in_rest:
        copy.wait()
    hops0 = input_rows(0, ())
    second_sends(1, first1, second1)
    weight_rows(0, 1)
    weight_rows(0, 2)
    query.go()
    mixer.go()
    input_norms(0, hops0)
    query.go()
    own_key(1, first1, second1)
    weight_rows(1, 1)
    key.reduce_send()
    own_value(1, first1, second1)
    weight_rows(1, 2)
    value.reduce_send()
    query.go()
    mixer.go()
    hops1 = input_rows(1, hops0)
    key.go()
    value.go()
    query.go()
    mixer.go()
    input_norms(1, hops1)
    totals = jnp.zeros((8, model), F32)
    place_row = lax.broadcasted_iota(jnp.int32, (8, model), 0)
    for i in range(5):
        totals = jnp.where(place_row == i, jnp.sum(small[i], axis=0, keepdims=True), totals)
    small[0] = totals
    small_copy = remote(small.at[0], small_in.at[0], {"tensor": near})
    key.go()
    value.go()
    query.go()
    mixer.go()
    small_copy.wait_recv()
    small[1] = small[0] + jnp.where(place_row < 3, small_in[0], 0.0)
    small_copy = remote(small.at[1], small_in.at[1], {"tensor": far})
    key.go()
    value.go()
    small_copy.wait_recv()
    small[2] = small[1] + jnp.where(place_row < 3, small_in[1], 0.0)
    for step, mask in enumerate(bits):
        small_copy = remote(small.at[2 + step], small_in.at[2 + step], dp_peer(mask))
        for chain in (key, value, query, mixer):
            if not chain.done:
                chain.go()
        small_copy.wait_recv()
        small[3 + step] = small[2 + step] + small_in[2 + step]
    while not (key.done and value.done and query.done and mixer.done):
        for chain in (key, value, query, mixer):
            if not chain.done:
                chain.go()
    small_out[...] = small[2 + len(bits)]

    for copy in ready + gathers[-1]:
        copy.wait_recv()
    in_share[-1].wait()
    for copy in pending:
        copy.wait_send()


def closing_call(parents, qs, os_pair, lses, scale_row, weight, pre, mid_gains, kt, vt, dos, outs, full, du, x, dr1, shares):
    micro, rows, model = x.shape
    tokens, width = qs[0].shape
    size = lax.axis_size("dp")
    bits = tuple(2**b for b in range(size.bit_length() - 1))
    vmem = pl.BlockSpec(memory_space=pltpu.VMEM)
    count, half = shares.shape[0], shares.shape[1]
    slots = DEPTH + 1
    segs = pltpu.VMEM((4 * tokens // SEG, SEG, width), BF)
    return pl.pallas_call(
        partial(closing, bits),
        out_shape=(
            jax.ShapeDtypeStruct((micro, rows, model), F32),
            jax.ShapeDtypeStruct((4, model, width), BF),
            jax.ShapeDtypeStruct((8, model), F32),
            jax.ShapeDtypeStruct((2, count // 2, 2 * half, model), BF),
        ),
        in_specs=[pl.BlockSpec(memory_space=pltpu.SMEM)] + [vmem] * 10 + [HBM] * 10,
        out_specs=(vmem, vmem, vmem, HBM),
        scratch_shapes=[
            segs,
            segs,
            pltpu.VMEM((tokens, width), F32),
            pltpu.VMEM((tokens, width), F32),
            pltpu.VMEM((SEG, SEG), F32),
            pltpu.VMEM((width, SEG), F32),
            pltpu.VMEM((4 * slots + 1, SEG, width), BF),
            pltpu.VMEM((4 * slots + 1, SEG, width), BF),
            segs,
            segs,
            segs,
            segs,
            pltpu.VMEM((micro, 6, tokens // SEG, SEG, width), BF),
            pltpu.VMEM((micro, 2, tokens // SEG, SEG, width), BF),
            pltpu.VMEM((micro, tokens, 3 * width), BF),
            pltpu.VMEM((4, model, width), F32),
            pltpu.VMEM((4, model, width), BF),
            pltpu.VMEM((4, model, width), BF),
            pltpu.VMEM((2, rows, model), BF),
            pltpu.VMEM((micro, 2, rows, model), BF),
            pltpu.VMEM((rows, model), BF),
            pltpu.VMEM((micro, rows, model), BF),
            pltpu.VMEM((3 + len(bits) + 2, 8, model), F32),
            pltpu.VMEM((2 + len(bits), 8, model), F32),
            pltpu.VMEM((micro, tokens, model), BF),
            pltpu.VMEM((micro, rows, model), BF),
            pltpu.VMEM((micro, rows, model), F32),
            pltpu.SemaphoreType.DMA((28 + 14 * len(bits),)),
            pltpu.SemaphoreType.DMA((28 + 14 * len(bits),)),
            pltpu.SemaphoreType.DMA((20,)),
        ],
        compiler_params=pltpu.CompilerParams(
            collective_id=1, has_side_effects=True, vmem_limit_bytes=62 << 20
        ),
        cost_estimate=pl.CostEstimate(flops=120 * 10**9, transcendentals=0, bytes_accessed=30 << 20),
        name="closing",
    )(
        parents, *qs, *os_pair, *lses, scale_row, weight, pre, mid_gains, shares, kt, vt, dos, *outs, full, du, x, dr1
    )


def body(
    block_input,
    cotangent,
    parent,
    pre_attn_gain,
    qkv_weight,
    head_scale,
    out_weight,
    post_attn_gain,
    pre_ffn_gain,
    fc1_weight,
    ffn_norm_gain,
    fc2_weight,
):
    tokens = cotangent.shape[1]
    width = qkv_weight.shape[2]
    parents = parent.reshape(-1)
    scale_row = jnp.repeat(head_scale, HEAD_DIM)[None, :]

    q0, q1, o0, o1, os0, os1, lse0, lse1, mixed, full1, keys, values = opening_call(
        parents, block_input, pre_attn_gain[None], qkv_weight, scale_row, out_weight
    )
    full1 = full1.reshape(MICRO, tokens, -1)
    du, dos, dr1, f_own, f_far, mid_gains, shares = middle_call(
        (os0, os1),
        mixed,
        block_input,
        cotangent,
        fc1_weight,
        fc2_weight,
        out_weight,
        post_attn_gain[None],
        pre_ffn_gain[None],
        ffn_norm_gain[None],
    )
    f_got = swap(f_far, "tensor", 2)
    outputs = (f_own + f_got.astype(F32)).astype(BF)
    din, narrow, small, whole = closing_call(
        parents,
        (q0, q1),
        (os0, os1),
        (lse0, lse1),
        scale_row,
        qkv_weight,
        pre_attn_gain[None],
        mid_gains,
        keys,
        values,
        dos,
        (o0, o1),
        full1,
        du,
        block_input,
        dr1,
        shares,
    )
    head_grad = small[4, 0:width].reshape(-1, HEAD_DIM).sum(-1)
    whole = whole.reshape(2, -1, whole.shape[-1])
    return (
        outputs,
        din,
        small[0],
        narrow[0:3].astype(F32),
        head_grad,
        narrow[3].T.astype(F32),
        small[1],
        small[2],
        whole[0].astype(F32),
        small[3],
        whole[1].astype(F32),
    )


def solution(mesh):
    in_specs = (
        P(None, ("dp", "tensor"), None),
        P(None, "dp", None),
        P(),
        P(),
        P(None, None, "tensor"),
        P("tensor"),
        P("tensor", None),
        P(),
        P(),
        P(None, "tensor"),
        P("tensor"),
        P("tensor", None),
    )
    out_specs = (
        P(None, ("dp", "tensor"), None),
        P(None, ("dp", "tensor"), None),
        P(),
        P(None, None, "tensor"),
        P("tensor"),
        P("tensor", None),
        P(),
        P(),
        P(None, "tensor"),
        P("tensor"),
        P("tensor", None),
    )
    return jax.shard_map(body, mesh=mesh, in_specs=in_specs, out_specs=out_specs, check_vma=False)
```

```python
from functools import partial

import jax
import jax.numpy as jnp
from jax import lax
from jax.experimental import pallas as pl
from jax.experimental.pallas import tpu as pltpu
from jax.sharding import PartitionSpec as P

HEAD_DIM = 64
FFN = 4096
SEG = 256
SEGS = 16
DEPTH = 5
MICRO = 2

EPSILON = 1e-05
NEGATIVE = -1e30
F32 = jnp.float32
BF = jnp.bfloat16
NN = (((1,), (0,)), ((), ()))
NT = (((1,), (1,)), ((), ()))
TN = (((0,), (0,)), ((), ()))


def mm(a, b, dims=NN):
    return lax.dot_general(a, b, dims, preferred_element_type=F32)


def swap(value, axis, mask):
    return lax.ppermute(value, axis, [(i, i ^ mask) for i in range(lax.axis_size(axis))])


def normalize(values):
    center = values - jnp.mean(values, axis=-1, keepdims=True)
    inverse = lax.rsqrt(jnp.mean(center * center, axis=-1, keepdims=True) + EPSILON)
    return (center * inverse, inverse)


def norm_backward(grad_hat, normed, inverse):
    mean_grad = jnp.mean(grad_hat, axis=-1, keepdims=True)
    mean_cross = jnp.mean(grad_hat * normed, axis=-1, keepdims=True)
    return inverse * (grad_hat - mean_grad - normed * mean_cross)


def climb(parents, base, seg):
    found = []
    current = seg
    count = jnp.int32(0)
    for _ in range(DEPTH):
        up = parents[base + current]
        valid = up >= 0
        count = count + valid.astype(jnp.int32)
        current = jnp.where(valid, up, current)
        found.append(current)
    return count, found


HBM = pl.BlockSpec(memory_space=pl.ANY)


def gelu_parts(c):
    root = 0.7978845608028654
    square = c * c
    tanh = jnp.tanh(root * (c + 0.044715 * (square * c)))
    act = 0.5 * c * (1.0 + tanh)
    slope = 0.5 * (1.0 + tanh) + 0.5 * c * (1.0 - tanh * tanh) * (root * (1.0 + 3 * 0.044715 * square))
    return act, slope


def other(shard, mask):
    near = shard + 1 - 2 * (shard % 2)
    return {0: shard, 1: near, 2: (shard + 2) % 4, 3: (near + 2) % 4}[mask]


def xor4(a, b):
    return 2 * lax.rem(lax.div(a, 2) + lax.div(b, 2), 2) + lax.rem(a + b, 2)


def opening(
    parents, x, gain, weight, scale_ref, out_w,
    q0, q1, o0, o1, os0, os1, lse0, lse1, mixed, full_hbm, kt_hbm, vt_hbm,
    full, kt0, kt1, vt0, vt1, picked_k, picked_v, core_out, core_in, y_out, y_in, send, recv, local,
):
    shard = lax.axis_index("tensor")
    index = lax.axis_index("dp")
    near, far = {"tensor": other(shard, 1)}, {"tensor": other(shard, 2)}
    beside, beyond = [{"dp": index + mask - 2 * mask * ((index // mask) % 2)} for mask in (1, 2)]
    rows, model = x.shape[1], x.shape[2]
    width = q0.shape[1]
    heads = width // HEAD_DIM
    tokens = 4 * rows
    per = tokens // SEG
    member, tree = index % 4, index // 4
    trees = parents.shape[0] // (MICRO * SEGS)
    qs, os_, oss, lses = (q0, q1), (o0, o1), (os0, os1), (lse0, lse1)
    kts, vts = (kt0, kt1), (vt0, vt1)
    used = [0]
    pending = []

    def remote(src, dst, target):
        i = used[0]
        used[0] += 1
        copy = pltpu.make_async_remote_copy(
            src_ref=src, dst_ref=dst, send_sem=send.at[i], recv_sem=recv.at[i],
            device_id=target, device_id_type=pl.DeviceIdType.MESH,
        )
        copy.start()
        pending.append(copy)
        return copy

    stores = []

    def store(src, dst):
        copy = pltpu.make_async_copy(src, dst, local.at[len(stores)])
        copy.start()
        stores.append(copy)

    def each(count, fn):
        lax.fori_loop(0, count, lambda i, c: (fn(i), c)[1], 0)

    barrier = pltpu.get_barrier_semaphore()
    for target in (near, far, beside, beyond):
        pl.semaphore_signal(barrier, inc=1, device_id=target, device_id_type=pl.DeviceIdType.MESH)

    chunk = 32

    def norms(m):
        def one(i):
            at = pl.ds(pl.multiple_of(i * chunk, chunk), chunk)
            values = x[m, at].astype(F32)
            center = values - jnp.mean(values, axis=-1, keepdims=True)
            inverse = lax.rsqrt(jnp.mean(center * center, axis=-1, keepdims=True) + EPSILON)
            full[m, 0, at] = (center * inverse * gain[...]).astype(BF)

        each(rows // chunk, one)

    def spread(m):
        return remote(full.at[m, 0], full.at[m, 2], far), remote(full.at[m, 0], full.at[m, 1], near)

    def project(m, first):
        for r in (first, first + 1):
            kts[m][r] = mm(full[m, r], weight[1]).astype(BF)
            vts[m][r] = mm(full[m, r], weight[2]).astype(BF)

    def queries(m):
        for r in range(4):
            qs[m][r * rows:(r + 1) * rows, :] = mm(full[m, r], weight[0]).astype(BF)

    def piece(ref, r, half):
        return ref.at[pl.ds(4 * r + 2 * half, 2)]

    def share(m, half):
        k, v = kts[m], vts[m]
        return [
            remote(piece(k, 0, half), piece(k, 1, half), beside),
            remote(piece(v, 0, half), piece(v, 2, half), beyond),
            remote(piece(k, 0, half), piece(k, 2, half), beyond),
            remote(piece(v, 0, half), piece(v, 1, half), beside),
        ]

    def forward(m, half, copies):
        copies[0].wait_recv()
        one = remote(piece(kts[m], 1, half), piece(kts[m], 3, half), beyond)
        copies[1].wait_recv()
        return copies[2:] + [one, remote(piece(vts[m], 2, half), piece(vts[m], 3, half), beside)]

    def settle(*groups):
        for copies in groups:
            for copy in copies:
                copy.wait_recv()

    def attend(m, step):
        seg = member * per + xor4(step, shard)
        count, found = climb(parents, (m * trees + tree) * SEGS, seg)
        past = DEPTH * SEG
        for slot in range(DEPTH):
            s = found[slot]
            at = 4 * xor4(lax.div(s, 4), member) + xor4(lax.rem(s, 4), shard)
            picked_k[slot * SEG:(slot + 1) * SEG, :] = kts[m][at]
            picked_v[slot * SEG:(slot + 1) * SEG, :] = vts[m][at]
        here = pl.ds(pl.multiple_of(step * SEG, SEG), SEG)
        picked_k[past:past + SEG, :] = kts[m][step]
        picked_v[past:past + SEG, :] = vts[m][step]
        lane = lax.broadcasted_iota(jnp.int32, (SEG, width), 1) // HEAD_DIM
        row = lax.broadcasted_iota(jnp.int32, (SEG, SEG), 0)
        col = lax.broadcasted_iota(jnp.int32, (SEG, SEG), 1)
        slot_of = lax.broadcasted_iota(jnp.int32, (1, past), 1) // SEG
        bias = jnp.where(slot_of < count, 0.0, NEGATIVE).astype(F32)
        q = qs[m][here, :] * BF(HEAD_DIM ** -0.5)
        lse_lane = lax.broadcasted_iota(jnp.int32, (SEG, 128), 1)
        lse_all = jnp.zeros((SEG, 128), F32)
        out = jnp.zeros((SEG, width), F32)
        for head in range(heads):
            qh = jnp.where(lane == head, q, jnp.zeros_like(q))
            s_past = mm(qh, picked_k[0:past, :], NT) + bias
            s_own = jnp.where(col <= row, mm(qh, picked_k[past:past + SEG, :], NT), NEGATIVE)
            top = jnp.maximum(
                jnp.max(s_past, axis=1, keepdims=True), jnp.max(s_own, axis=1, keepdims=True)
            )
            p_past = jnp.exp(s_past - top)
            p_own = jnp.exp(s_own - top)
            total = jnp.sum(p_past, axis=1, keepdims=True) + jnp.sum(p_own, axis=1, keepdims=True)
            got = mm(p_past.astype(BF), picked_v[0:past, :]) + mm(p_own.astype(BF), picked_v[past:past + SEG, :])
            out = jnp.where(lane == head, got / total, out)
            lse_all = jnp.where(lse_lane == head, top + jnp.log(total), lse_all)
        os_[m][here, :] = out
        oss[m][here, :] = (out * scale_ref[...]).astype(BF)
        lses[m][pl.ds(step, 1)] = jnp.transpose(lse_all)[0:8].reshape(1, 8, SEG)

    norms(0)
    pl.semaphore_wait(barrier, 4)
    far0, near0 = spread(0)
    norms(1)
    far1, near1 = spread(1)
    near0.wait_recv()
    project(0, 0)
    a0 = share(0, 0)
    near1.wait_recv()
    project(1, 0)
    far0.wait_recv()
    cross0 = remote(full.at[0, 2], full.at[0, 3], near)
    cross0.wait_recv()
    project(0, 2)
    b0 = share(0, 1)
    a0 = forward(0, 0, a0)
    queries(0)
    far1.wait_recv()
    cross1 = remote(full.at[1, 2], full.at[1, 3], near)
    b0 = forward(0, 1, b0)
    a1 = share(1, 0)
    cross1.wait_recv()
    project(1, 2)
    b1 = share(1, 1)
    queries(1)
    for m in range(MICRO):
        store(full.at[m], full_hbm.at[m])
    settle(a0, b0)
    lax.fori_loop(0, 2, lambda i, c: (attend(0, i), c)[1], 0)
    a1 = forward(1, 0, a1)
    lax.fori_loop(2, 4, lambda i, c: (attend(0, i), c)[1], 0)
    b1 = forward(1, 1, b1)

    def mix(r):
        return mm(os0[r * rows:(r + 1) * rows, :], out_w[...])

    core_out[0] = mix(3).astype(BF)
    hop3 = remote(core_out.at[0], core_in.at[0], near)
    core_out[1] = mix(1).astype(BF)
    hop1 = remote(core_out.at[1], core_in.at[1], near)
    mixed[...] = mix(2)
    hop3.wait_recv()
    y_out[...] = (mixed[...] + core_in[0].astype(F32)).astype(BF)
    hop2 = remote(y_out, y_in, far)
    hop1.wait_recv()
    mixed[...] = mix(0) + core_in[1].astype(F32)
    store(kt0, kt_hbm.at[0])
    store(vt0, vt_hbm.at[0])
    settle(a1, b1)
    store(kt1, kt_hbm.at[1])
    store(vt1, vt_hbm.at[1])
    lax.fori_loop(0, 4, lambda i, c: (attend(1, i), c)[1], 0)
    hop2.wait_recv()
    mixed[...] = mixed[...] + y_in[...].astype(F32)
    for copy in pending:
        copy.wait_send()
    for copy in stores:
        copy.wait()


def opening_call(parents, x, gain, weight, scale_row, out_w):
    micro, rows, model = x.shape
    width = weight.shape[2]
    tokens = 4 * rows
    vmem = pl.BlockSpec(memory_space=pltpu.VMEM)
    narrow = jax.ShapeDtypeStruct((tokens, width), BF)
    narrow_wide = jax.ShapeDtypeStruct((tokens, width), F32)
    tops = jax.ShapeDtypeStruct((tokens // SEG, 8, SEG), F32)
    trees = jax.ShapeDtypeStruct((micro, 4 * tokens // SEG, SEG, width), BF)
    return pl.pallas_call(
        opening,
        out_shape=(
            narrow, narrow, narrow_wide, narrow_wide, narrow, narrow, tops, tops,
            jax.ShapeDtypeStruct((rows, model), F32),
            jax.ShapeDtypeStruct((micro, 4, rows, model), BF),
            trees, trees,
        ),
        in_specs=[pl.BlockSpec(memory_space=pltpu.SMEM)] + [vmem] * 5,
        out_specs=(vmem,) * 9 + (HBM,) * 3,
        scratch_shapes=[pltpu.VMEM((micro, 4, rows, model), BF)]
        + [pltpu.VMEM((4 * tokens // SEG, SEG, width), BF)] * 4
        + [pltpu.VMEM(((DEPTH + 1) * SEG, width), BF)] * 2
        + [pltpu.VMEM((2, rows, model), BF)] * 2
        + [pltpu.VMEM((rows, model), BF)] * 2
        + [
            pltpu.SemaphoreType.DMA((36,)),
            pltpu.SemaphoreType.DMA((36,)),
            pltpu.SemaphoreType.DMA((8,)),
        ],
        compiler_params=pltpu.CompilerParams(
            collective_id=2, has_side_effects=True, vmem_limit_bytes=61 << 20
        ),
        cost_estimate=pl.CostEstimate(flops=60 * 10**9, transcendentals=0, bytes_accessed=20 << 20),
        name="opening",
    )(parents, x, gain, weight, scale_row, out_w)


def middle(
    bits, os0, os1, mixed0, x, g_hbm, fc1_hbm, fc2_hbm, out_w, post, pre, wide,
    du_hbm, dos, dr1, f_own, f_far, gains, shares,
    fc1, fc2, gd, du, act, slz, dzc, full, core_out, core_in, y_out, y_in, nu, inv, st_out, st_in, sums, cols,
    arrived, send, recv, local,
):
    shard = lax.axis_index("tensor")
    index = lax.axis_index("dp")

    def bit_of(mask):
        return (index // mask) % 2

    def dp_peer(mask):
        return {"dp": index + mask - 2 * mask * bit_of(mask)}

    peers = [other(shard, k) for k in range(4)]
    rows = x.shape[1]
    model = x.shape[2]
    hidden = fc1.shape[1]
    parts = hidden // SEG
    used = [0]
    pending = []

    def remote(src, dst, target):
        i = used[0]
        used[0] += 1
        if not isinstance(target, dict):
            target = {"tensor": peers[target]}
        copy = pltpu.make_async_remote_copy(
            src_ref=src, dst_ref=dst, send_sem=send.at[i], recv_sem=recv.at[i],
            device_id=target, device_id_type=pl.DeviceIdType.MESH,
        )
        copy.start()
        pending.append(copy)
        return copy

    stored = [0]
    stores = []

    def store(src, dst):
        i = stored[0]
        stored[0] += 1
        copy = pltpu.make_async_copy(src, dst, local.at[i])
        copy.start()
        stores.append(copy)

    def fetch(src, dst):
        i = stored[0]
        stored[0] += 1
        copy = pltpu.make_async_copy(src, dst, local.at[i])
        copy.start()
        return copy

    got_fc2 = fetch(fc2_hbm, fc2)
    got_g = [
        [fetch(g_hbm.at[m, pl.ds(peers[r] * rows, rows), :], gd.at[m, r]) for r in range(4)] for m in range(MICRO)
    ]
    got_fc1 = fetch(fc1_hbm, fc1)
    barrier = pltpu.get_barrier_semaphore()
    targets = [{"tensor": peers[mask]} for mask in (1, 2, 3)] + [dp_peer(mask) for mask in bits]
    for target in targets:
        pl.semaphore_signal(barrier, inc=1, device_id=target, device_id_type=pl.DeviceIdType.MESH)
    pl.semaphore_wait(barrier, len(targets))
    gains[...] = jnp.zeros_like(gains)

    def each(count, fn):
        lax.fori_loop(0, count, lambda i, c: (fn(i), c)[1], 0)

    def tile(n):
        return pl.ds(pl.multiple_of(n * SEG, SEG), SEG)

    def merge(value):
        return value.reshape((-1,) + value.shape[2:])

    def reuse(*groups):
        for copies in groups:
            for copy in copies if isinstance(copies, tuple) else (copies,):
                copy.wait_send()
                pending[:] = [other_copy for other_copy in pending if other_copy is not copy]

    def first_hop(kind, m, block, out):
        block(3, core_out.at[m, 0])
        hop3 = remote(core_out.at[m, 0], core_in.at[kind, m, 0], 1)
        block(2, None)
        hop3.wait_recv()
        add_far(kind, m)
        far_hop = remote(y_out.at[m], y_in.at[kind, m], 2)
        block(1, core_out.at[m, 1])
        hop1 = remote(core_out.at[m, 1], core_in.at[kind, m, 1], 1)
        block(0, out)
        return hop3, hop1, far_hop

    chunk = 32

    def chunks(fn):
        each(rows // chunk, lambda i: fn(pl.ds(pl.multiple_of(i * chunk, chunk), chunk)))

    def add_far(kind, m):
        def one(at):
            y_out[m, at] = (sums_far[m][at] + core_in[kind, m, 0, at].astype(F32)).astype(BF)

        chunks(one)

    sums_far = [f_own.at[m] for m in range(MICRO)]
    def mixed_block():
        def block(r, out):
            part = mm(os1[r * rows:(r + 1) * rows, :], out_w[...])
            if r == 2:
                sums_far[1][...] = part
            else:
                out[...] = part.astype(out.dtype)

        return block

    def project_grad(m):
        for r in range(4):
            got_g[m][r].wait()

        def one(i):
            r, n = i // parts, i % parts
            dzc[m, pl.ds(pl.multiple_of(r * rows, rows), rows), tile(n)] = mm(gd[m, r], fc2[tile(n), :], NT).astype(BF)

        each(4 * parts, one)

    def own_sum(kind, m, base, at):
        return base + core_in[kind, m, 1, at].astype(F32) + y_in[kind, m, at].astype(F32)

    def norm_two(m, at, residual):
        center = residual - jnp.mean(residual, axis=-1, keepdims=True)
        inverse = lax.rsqrt(jnp.mean(center * center, axis=-1, keepdims=True) + EPSILON)
        return center * inverse, inverse

    def forward_norms(m, hops=None):
        if m:
            hops[1].wait_recv()
            hops[2].wait_recv()

        def one(at):
            mixed, inverse = norm_two(m, at, own_sum(0, m, nu[m, at], at) if m else mixed0[at, :])
            nu[m, at] = mixed
            inv[m, at] = jnp.broadcast_to(inverse, (chunk, 128))
            residual = x[m, at].astype(F32) + mixed * post[...]
            normed, _ = norm_two(m, at, residual)
            full[m, 0, at] = (normed * pre[...]).astype(BF)

        chunks(one)

    def spread(m, buf):
        return remote(buf.at[m, 0], buf.at[m, 2], 2), remote(buf.at[m, 0], buf.at[m, 1], 1)

    def ffn_forward(m, r):
        sums[...] = jnp.zeros_like(sums)

        def one(n):
            value, slope = gelu_parts(mm(full[m, r], fc1[:, tile(n)]))
            act[m, r * rows:(r + 1) * rows, tile(n)] = value
            slz[m, r, :, tile(n)] = slope.astype(BF)
            dna = dzc[m, pl.ds(pl.multiple_of(r * rows, rows), rows), tile(n)].astype(F32) * wide[:, tile(n)]
            for i, term in enumerate((value, value * value, dna, dna * value)):
                sums[i] += term[:, 0:128] + term[:, 128:256]

        each(parts, one)
        lane = lax.broadcasted_iota(jnp.int32, (rows, 128), 1)
        merged = jnp.zeros((rows, 128), F32)
        for i in range(4):
            merged = jnp.where(lane == i, jnp.sum(sums[i], axis=-1, keepdims=True), merged)
        st_out[m, :, r * rows:(r + 1) * rows] = jnp.transpose(merged)[0:8]

    def send_stats(m):
        return [remote(st_out.at[m], st_in.at[m, mask - 1], mask) for mask in (1, 2, 3)]

    def ffn_backward_rows(m, r):
        total = st_out[m, :, r * rows:(r + 1) * rows]
        for mask in (1, 2, 3):
            b = r ^ mask
            total = total + st_in[m, mask - 1, :, b * rows:(b + 1) * rows]
        cols[0:8, :] = total * (1.0 / FFN)
        flipped = jnp.transpose(cols[...])
        mu, square, m_dna, m_cross = [flipped[:, i:i + 1] for i in range(4)]
        rw = lax.rsqrt(square - mu * mu + EPSILON)
        m_both = (m_cross - mu * m_dna) * rw

        def one(n):
            gain = wide[:, tile(n)]
            dz = dzc[m, pl.ds(pl.multiple_of(r * rows, rows), rows), tile(n)].astype(F32)
            na = (act[m, r * rows:(r + 1) * rows, tile(n)] - mu) * rw
            slope = slz[m, r, :, tile(n)].astype(F32)
            slz[m, r, :, tile(n)] = (na * gain).astype(BF)
            gains[16:24, tile(n)] += jnp.sum((dz * na).reshape(rows // 8, 8, SEG), axis=0)
            dzc[m, pl.ds(pl.multiple_of(r * rows, rows), rows), tile(n)] = (rw * (dz * gain - m_dna - na * m_both) * slope).astype(BF)

        each(parts, one)

    def grad_block(m):
        def block(r, out):
            ffn_backward_rows(m, r)
            if r == 2:
                out = sums_far[m]

            def one(n):
                out[:, tile(n)] = mm(dzc[m, r * rows:(r + 1) * rows, :], fc1[tile(n), :], NT).astype(out.dtype)

            each(model // SEG, one)

        return block

    def ffn_out_block(m):
        def block(r, out):
            def one(n):
                out[:, tile(n)] = mm(slz[m, r], fc2[:, tile(n)]).astype(out.dtype)

            each(model // SEG, one)

        return block

    def backward_norms(m, hop1, far_hop):
        hop1.wait_recv()
        far_hop.wait_recv()

        def one(at):
            dh2 = own_sum(1, m, dr1[m, at], at)
            mixed = nu[m, at]
            residual = x[m, at].astype(F32) + mixed * post[...]
            normed, inverse = norm_two(m, at, residual)
            gains[8:16, :] += jnp.sum((dh2 * normed).reshape(chunk // 8, 8, model), axis=0)
            grad = gd[m, 0, at].astype(F32) + norm_backward(dh2 * pre[...], normed, inverse)
            gains[0:8, :] += jnp.sum((grad * mixed).reshape(chunk // 8, 8, model), axis=0)
            dr1[m, at] = grad
            back = norm_backward(grad * post[...], mixed, inv[m, at][:, 0:1])
            du[m, 0, at] = back.astype(BF)

        chunks(one)

    def unmix(m, r):
        dos[m, r * rows:(r + 1) * rows, :] = mm(du[m, r], out_w[...], NT)

    forward_norms(0)
    far0, near0 = spread(0, full)
    hops = first_hop(0, 1, mixed_block(), nu.at[1])
    got_fc2.wait()
    project_grad(0)
    got_fc1.wait()
    ffn_forward(0, 0)
    near0.wait_recv()
    ffn_forward(0, 1)
    project_grad(1)
    far0.wait_recv()
    cross0 = remote(full.at[0, 2], full.at[0, 3], 1)
    ffn_forward(0, 2)
    cross0.wait_recv()
    ffn_forward(0, 3)
    stats0 = send_stats(0)
    forward_norms(1, hops)
    far1, near1 = spread(1, full)
    ffn_forward(1, 0)
    near1.wait_recv()
    ffn_forward(1, 1)
    for copy in stats0:
        copy.wait_recv()
    hop_a = first_hop(1, 0, grad_block(0), dr1.at[0])
    far1.wait_recv()
    cross1 = remote(full.at[1, 2], full.at[1, 3], 1)
    ffn_forward(1, 2)
    cross1.wait_recv()
    ffn_forward(1, 3)
    stats1 = send_stats(1)

    def first_grad(m):
        def one(n):
            part = mm(merge(full[m, :, :, tile(n)]), dzc[m], TN)
            act[0, tile(n), :] = part if m == 0 else act[0, tile(n), :] + part

        each(parts, one)

    def second_grad(n):
        part = mm(merge(slz[0, :, :, tile(n)]), merge(gd[0]), TN)
        act[1, tile(n), :] = part + mm(merge(slz[1, :, :, tile(n)]), merge(gd[1]), TN)

    first_grad(0)
    for copy in stats1:
        copy.wait_recv()
    reuse(hops)
    hop_b = first_hop(1, 1, grad_block(1), dr1.at[1])
    backward_norms(0, hop_a[1], hop_a[2])
    du_far0, du_near0 = spread(0, du)
    first_grad(1)
    group = hidden // (shares.shape[0] // 2)

    line = min(32, group // 2 ** len(bits))

    class Chain:
        def __init__(self, number):
            self.number, self.which = number, number // (hidden // group)
            self.start = (number % (hidden // group)) * group
            self.base, self.size, self.at, self.step = self.start, group, self.start, 0
            self.back = False

        def send(self):
            mask = bits[self.step]
            half = self.size // 2
            away = self.base + (1 - bit_of(mask)) * half
            where = self.at

            def one(i):
                src = pl.ds(pl.multiple_of(away + i * line, line), line)
                staged[self.which, pl.ds(pl.multiple_of(where + i * line, line), line), :] = act[
                    self.which, src, :
                ].astype(BF)

            each(half // line, one)
            slot = pl.ds(where, half)
            self.copy = remote(
                staged.at[self.which, slot, :], arrived.at[self.which, slot, :], dp_peer(mask)
            )
            self.base, self.size = self.base + bit_of(mask) * half, half

        def wait(self):
            self.copy.wait_recv()
            self.step += 1
            base, where, last = self.base, self.at, self.step == len(bits)

            def one(i):
                mine = pl.ds(pl.multiple_of(base + i * line, line), line)
                total = act[self.which, mine, :] + arrived[
                    self.which, pl.ds(pl.multiple_of(where + i * line, line), line), :
                ].astype(F32)
                if last:
                    at = self.start + base - self.first + i * line
                    staged[self.which, pl.ds(pl.multiple_of(at, line), line), :] = total.astype(BF)
                else:
                    act[self.which, mine, :] = total

            each(self.size // line, one)
            self.at += self.size
            if self.step == 1:
                self.first = base

        def gather(self):
            self.step -= 1
            mask = bits[self.step]
            at = pl.ds(pl.multiple_of(self.start + self.base - self.first, 16), self.size)
            self.copy = remote(staged.at[self.which, at, :], staged.at[self.which, at, :], dp_peer(mask))
            self.base, self.size = self.base - bit_of(mask) * self.size, 2 * self.size

        def go(self):
            if self.back:
                self.copy.wait_recv()
            else:
                self.wait()
                self.back = self.step == len(bits)
            if not self.back:
                reuse(self.copy)
                self.send()
            elif self.which == 0 and self.step > 1:
                self.gather()
            else:
                half = group // 2
                store(staged.at[self.which, pl.ds(self.start, half), :], shares.at[self.number])

    chains = [Chain(i) for i in range(shares.shape[0])]
    half_chains = len(chains) // 2
    staged = dzc
    for chain in chains[:half_chains]:
        chain.send()
    per_chain = parts // half_chains
    for i, chain in enumerate(chains[half_chains:]):
        each(per_chain, lambda n: second_grad(n + i * per_chain))
        chain.send()
    backward_norms(1, hop_b[1], hop_b[2])
    du_far1, du_near1 = spread(1, du)

    def ffn_out(m, hop_old):
        reuse(hop_old, ())
        block = ffn_out_block(m)
        block(3, core_out.at[m, 0])
        hop3 = remote(core_out.at[m, 0], core_in.at[0, m, 0], 1)
        block(1, core_out.at[m, 1])
        hop1 = remote(core_out.at[m, 1], core_in.at[0, m, 1], 1)
        block(2, f_own.at[m])
        hop3.wait_recv()

        def one(at):
            f_far[m, at] = (f_own[m, at] + core_in[0, m, 0, at].astype(F32)).astype(BF)

        chunks(one)
        block(0, f_own.at[m])
        hop1.wait_recv()

        def two(at):
            residual = x[m, at].astype(F32) + nu[m, at] * post[...]
            f_own[m, at] = residual + f_own[m, at] + core_in[0, m, 1, at].astype(F32)

        chunks(two)

    todo = [
        chains[turn - level]
        for turn in range(len(chains) + 2 * len(bits) - 2)
        for level in range(2 * len(bits) - 1)
        if 0 <= turn - level < (half_chains if level >= len(bits) else len(chains))
    ]

    def advance(count):
        for _ in range(min(count, len(todo))):
            todo.pop(0).go()

    slice_of = -(-len(todo) // 5)
    ffn_out(0, hop_a)
    unmix(0, 0)
    du_near0.wait_recv()
    unmix(0, 1)
    du_far0.wait_recv()
    du_cross0 = remote(du.at[0, 2], du.at[0, 3], 1)
    unmix(0, 2)
    advance(slice_of)
    du_cross0.wait_recv()
    unmix(0, 3)
    ffn_out(1, hop_b)
    advance(slice_of)
    unmix(1, 0)
    du_near1.wait_recv()
    unmix(1, 1)
    for r in range(4):
        store(du.at[0, r], du_hbm.at[0, pl.ds(r * rows, rows), :])
    du_far1.wait_recv()
    du_cross1 = remote(du.at[1, 2], du.at[1, 3], 1)
    unmix(1, 2)
    advance(slice_of)
    du_cross1.wait_recv()
    unmix(1, 3)
    for r in range(4):
        store(du.at[1, r], du_hbm.at[1, pl.ds(r * rows, rows), :])
    advance(len(todo))
    for copy in pending:
        copy.wait_send()
    for copy in stores:
        copy.wait()


def middle_call(os_pair, mixed, x, g, fc1, fc2, out_w, post, pre, wide):
    micro, rows, model = x.shape
    hidden = fc1.shape[1]
    width = out_w.shape[0]
    tokens = 4 * rows
    vmem = pl.BlockSpec(memory_space=pltpu.VMEM)
    wide_rows = jax.ShapeDtypeStruct((micro, tokens, model), BF)
    own = jax.ShapeDtypeStruct((micro, rows, model), F32)
    size = lax.axis_size("dp")
    bits = tuple(2**b for b in range(size.bit_length() - 1))
    group = max(SEG, 16 * size)
    count = 2 * hidden // group
    return pl.pallas_call(
        partial(middle, bits),
        out_shape=(
            wide_rows,
            jax.ShapeDtypeStruct((micro, tokens, width), F32),
            own, own,
            jax.ShapeDtypeStruct((micro, rows, model), BF),
            jax.ShapeDtypeStruct((24, model), F32),
            jax.ShapeDtypeStruct((count, group // 2, model), BF),
        ),
        in_specs=[vmem, vmem, vmem, vmem, HBM, HBM, HBM, vmem, vmem, vmem, vmem],
        out_specs=(HBM, vmem, vmem, vmem, vmem, vmem, HBM),
        scratch_shapes=[
            pltpu.VMEM((model, hidden), BF),
            pltpu.VMEM((hidden, model), BF),
            pltpu.VMEM((micro, 4, rows, model), BF),
            pltpu.VMEM((micro, 4, rows, model), BF),
            pltpu.VMEM((micro, tokens, hidden), F32),
            pltpu.VMEM((micro, 4, rows, hidden), BF),
            pltpu.VMEM((micro, tokens, hidden), BF),
            pltpu.VMEM((micro, 4, rows, model), BF),
            pltpu.VMEM((micro, 2, rows, model), BF),
            pltpu.VMEM((2, micro, 2, rows, model), BF),
            pltpu.VMEM((micro, rows, model), BF),
            pltpu.VMEM((2, micro, rows, model), BF),
            pltpu.VMEM((micro, rows, model), F32),
            pltpu.VMEM((micro, rows, 128), F32),
            pltpu.VMEM((micro, 8, tokens), F32),
            pltpu.VMEM((micro, 3, 8, tokens), F32),
            pltpu.VMEM((4, rows, 128), F32),
            pltpu.VMEM((128, rows), F32),
            pltpu.VMEM((2, hidden, model), BF),
            pltpu.SemaphoreType.DMA((40 + 2 * count * len(bits),)),
            pltpu.SemaphoreType.DMA((40 + 2 * count * len(bits),)),
            pltpu.SemaphoreType.DMA((20 + count,)),
        ],
        compiler_params=pltpu.CompilerParams(
            collective_id=0, has_side_effects=True, vmem_limit_bytes=61 << 20
        ),
        cost_estimate=pl.CostEstimate(flops=100 * 10**9, transcendentals=0, bytes_accessed=40 << 20),
        name="middle",
    )(*os_pair, mixed, x, g, fc1, fc2, out_w, post, pre, wide)


def closing(bits, parents, *refs):
    q0, q1, os0, os1, lse0, lse1, scale_ref, weight, pre, mid_gains = refs[0:10]
    shares, kt_hbm, vt_hbm, dos_hbm, o0_hbm, o1_hbm, full_hbm, du_hbm, x_hbm, dr1_hbm = refs[10:20]
    din, res, small_out, ffn = refs[20:24]
    (
        kt, vt, dos, o, bias, dqt, contrib_k, contrib_v, dkp0, dkp1, dvp0, dvp1, inbox, inner, grads, acc, stage,
        arrived, core_out, core_in, y_out, y_in, small, small_in, big, x, dr1, send, recv, local,
    ) = refs[24:]
    shard = lax.axis_index("tensor")
    index = lax.axis_index("dp")
    near, far = other(shard, 1), other(shard, 2)
    rows, model = x.shape[1], x.shape[2]
    tokens, width = q0.shape
    heads = width // HEAD_DIM
    per = tokens // SEG
    member, tree = index % 4, index // 4
    trees = parents.shape[0] // (MICRO * SEGS)
    qs, lses, os_hbm = (q0, q1), (lse0, lse1), (o0_hbm, o1_hbm)
    dkp, dvp = (dkp0, dkp1), (dvp0, dvp1)
    slots = DEPTH + 1

    def bit_of(mask):
        return (index // mask) % 2

    def dp_peer(mask):
        return {"dp": index + mask - 2 * mask * bit_of(mask)}

    used = [0]
    pending = []

    def prepare(src, dst, target):
        i = used[0]
        used[0] += 1
        copy = pltpu.make_async_remote_copy(
            src_ref=src, dst_ref=dst, send_sem=send.at[i], recv_sem=recv.at[i],
            device_id=target, device_id_type=pl.DeviceIdType.MESH,
        )
        pending.append(copy)
        return copy

    def remote(src, dst, target):
        copy = prepare(src, dst, target)
        copy.start()
        return copy

    fetched = [0]

    def fetch(src, dst):
        i = fetched[0]
        fetched[0] += 1
        copy = pltpu.make_async_copy(src, dst, local.at[i])
        copy.start()
        return copy

    def each(count, fn):
        lax.fori_loop(0, count, lambda i, c: (fn(i), c)[1], 0)

    def tile(n):
        return pl.ds(pl.multiple_of(n * SEG, SEG), SEG)

    barrier = pltpu.get_barrier_semaphore()
    targets = [{"tensor": near}, {"tensor": far}] + [dp_peer(mask) for mask in bits]
    for target in targets:
        pl.semaphore_signal(barrier, inc=1, device_id=target, device_id_type=pl.DeviceIdType.MESH)

    def fetch_tree(m):
        return [
            fetch(kt_hbm.at[m], kt), fetch(vt_hbm.at[m], vt), fetch(dos_hbm.at[m], dos), fetch(os_hbm[m], o)
        ]

    count, half = shares.shape[0] // 2, shares.shape[1]
    lines = 2 * half // 2 ** len(bits)
    base = bit_of(bits[0]) * half
    inside = 0
    for step, mask in enumerate(bits[1:]):
        inside = inside + bit_of(mask) * (half // 2 ** (step + 1))
    cut = max(1, count // 2)
    parts = list(range(0, count, cut))
    whole_half = pl.ds(pl.multiple_of(base, 16), half)
    own_lines = pl.ds(pl.multiple_of(base + inside, 16), lines)
    inside_lines = pl.ds(pl.multiple_of(inside, 16), lines)
    in_share = [
        fetch(shares.at[pl.ds(count + at, cut), inside_lines, :], ffn.at[1, pl.ds(at, cut), own_lines, :])
        for at in parts
    ]
    in_tree = fetch_tree(0)
    in_du = fetch(du_hbm, big)
    in_share.append(fetch(shares.at[pl.ds(0, count)], ffn.at[0, :, whole_half, :]))
    pl.semaphore_wait(barrier, len(targets))
    ready = [
        remote(shares.at[pl.ds(at, cut)], ffn.at[0, pl.ds(at, cut), whole_half, :], dp_peer(bits[0]))
        for at in parts
    ]
    gathers = []
    size, base = lines, base + inside
    for mask in bits[::-1]:
        rows_at = pl.ds(pl.multiple_of(base, 16), size)
        level = []
        for at in parts:
            where = ffn.at[1, pl.ds(at, cut), rows_at, :]
            source = where if gathers else shares.at[pl.ds(count + at, cut), inside_lines, :]
            level.append(prepare(source, where, dp_peer(mask)))
        if not gathers:
            for copy in level:
                copy.start()
        gathers.append(level)
        base, size = base - bit_of(mask) * size, 2 * size

    events = {}
    for level in range(1, len(bits)):
        for part in range(len(parts)):
            turn = (2, 6)[part] if level < len(bits) - 1 else (8, 13)[part]
            events.setdefault(min(23, turn), []).append((level, part))

    def gather_turn(step, slot):
        for turn, moves in sorted(events.items()):

            @pl.when(step * 6 + slot == turn)
            def _():
                for level, part in moves:
                    if level == 1:
                        in_share[part].wait()
                    gathers[level - 1][part].wait_recv()
                    gathers[level][part].start()

    def attend_back(m, step):
        seg = member * per + xor4(step, shard)
        steps_up, found = climb(parents, (m * trees + tree) * SEGS, seg)
        here = pl.ds(pl.multiple_of(step * SEG, SEG), SEG)
        grad_out = dos[here, :]
        cross = grad_out * o[here, :]
        small[4, :, 0:width] += jnp.sum(cross.reshape(SEG // 8, 8, width), axis=0)
        scale = scale_ref[...]
        go = (grad_out * scale).astype(BF)
        cross_t = jnp.transpose(cross * scale)
        lane = lax.broadcasted_iota(jnp.int32, (SEG, width), 1) // HEAD_DIM
        q = qs[m][here, :] * BF(HEAD_DIM ** -0.5)
        zero = jnp.zeros_like(q)
        q_heads = [jnp.where(lane == h, q, zero) for h in range(heads)]
        g_heads = [jnp.where(lane == h, go, zero) for h in range(heads)]
        deltas = [
            jnp.sum(cross_t[h * HEAD_DIM:(h + 1) * HEAD_DIM], axis=0, keepdims=True) for h in range(heads)
        ]
        tops = lses[m][step]
        dqt[...] = jnp.zeros_like(dqt)

        def slot_block(slot):
            here_slot = slot == DEPTH
            source = seg
            for j in range(DEPTH):
                source = jnp.where(slot == j, found[j], source)
            at = 4 * xor4(lax.div(source, 4), member) + xor4(lax.rem(source, 4), shard)
            key_row = lax.broadcasted_iota(jnp.int32, (SEG, SEG), 0)
            query_col = lax.broadcasted_iota(jnp.int32, (SEG, SEG), 1)
            last = jnp.where(here_slot, 0, jnp.where(slot < steps_up, SEG, -SEG))
            bias[...] = jnp.where(key_row <= query_col + last, 0.0, NEGATIVE)
            k = kt[at]
            v = vt[at]
            k_t = jnp.transpose(k)
            dk = jnp.zeros((SEG, width), F32)
            dv = jnp.zeros((SEG, width), F32)
            for h in range(heads):
                p = jnp.exp(mm(k, q_heads[h], NT) + bias[...] - tops[h:h + 1, :])
                dv += mm(p.astype(BF), g_heads[h])
                dp = mm(v, g_heads[h], NT)
                ds = (p * (dp - deltas[h])).astype(BF)
                dk += mm(ds, q_heads[h])
                dqt[pl.ds(h * HEAD_DIM, HEAD_DIM), :] += mm(k_t[h * HEAD_DIM:(h + 1) * HEAD_DIM], ds)
            contrib_k[step * slots + slot] = dk.astype(BF)
            contrib_v[step * slots + slot] = dv.astype(BF)
            if m == 0:
                gather_turn(step, slot)

        each(slots, slot_block)
        grads[m, here, 0:width] = (jnp.transpose(dqt[...]) * HEAD_DIM ** -0.5).astype(BF)

    def combine(m, r):
        def one(line):
            seg = xor4(jnp.int32(r), member) * per + xor4(line, shard)
            dk = jnp.zeros((SEG, width), F32)
            dv = jnp.zeros((SEG, width), F32)
            for step in range(4):
                own = member * per + other(shard, step)
                steps_up, found = climb(parents, (m * trees + tree) * SEGS, own)
                at = jnp.where(seg == own, step * slots + DEPTH, 4 * slots)
                for j in range(DEPTH):
                    hit = jnp.logical_and(found[j] == seg, j < steps_up)
                    at = jnp.where(hit, step * slots + j, at)
                dk = dk + contrib_k[at].astype(F32)
                dv = dv + contrib_v[at].astype(F32)
            dkp[m][4 * r + line] = dk.astype(BF)
            dvp[m][4 * r + line] = dv.astype(BF)

        each(4, one)

    def piece(ref, r):
        return ref.at[pl.ds(4 * r, 4)]

    def first_sends(m):
        combine(m, 3)
        copies = [
            remote(piece(dkp[m], 3), inbox.at[m, 0], dp_peer(2)),
            remote(piece(dvp[m], 3), inbox.at[m, 1], dp_peer(1)),
        ]
        combine(m, 2)
        copies.append(remote(piece(dkp[m], 2), inbox.at[m, 2], dp_peer(2)))
        combine(m, 1)
        copies.append(remote(piece(dvp[m], 1), inbox.at[m, 3], dp_peer(1)))
        combine(m, 0)
        return copies

    def second_pair(m):
        return [
            prepare(inner.at[m, 0], inbox.at[m, 4], dp_peer(1)),
            prepare(inner.at[m, 1], inbox.at[m, 5], dp_peer(2)),
        ]

    def second_sends(m, first, second):
        for i, own in enumerate((piece(dkp[m], 1), piece(dvp[m], 2))):
            first[i].wait_recv()

            def one(n):
                inner[m, i, n] = (own[n].astype(F32) + inbox[m, i, n].astype(F32)).astype(BF)

            each(4, one)
            second[i].start()

    def own_rows(m, kind, own, slots_in):
        def one(n):
            total = own[n].astype(F32)
            for i in slots_in:
                total = total + inbox[m, i, n].astype(F32)
            grads[m, tile(n), kind * width:(kind + 1) * width] = total.astype(BF)

        each(4, one)

    def own_key(m, first, second):
        first[2].wait_recv()
        second[0].wait_recv()
        own_rows(m, 1, piece(dkp[m], 0), (2, 4))

    def own_value(m, first, second):
        first[3].wait_recv()
        second[1].wait_recv()
        own_rows(m, 2, piece(dvp[m], 0), (3, 5))

    def out_rows(n):
        acc[3, tile(n), :] = mm(big[0, :, tile(n)], os0[...], TN) + mm(big[1, :, tile(n)], os1[...], TN)

    def weight_rows(m, kind):
        cols = slice(kind * width, (kind + 1) * width)

        def one(n):
            part = mm(big[m, :, tile(n)], grads[m, :, cols], TN)
            acc[kind, tile(n), :] = part if m == 0 else acc[kind, tile(n), :] + part

        each(model // SEG, one)

    def input_rows(m, old):
        def block(r, out):
            def one(n):
                part = jnp.zeros((rows, SEG), F32)
                for kind in range(3):
                    part += mm(
                        grads[m, r * rows:(r + 1) * rows, kind * width:(kind + 1) * width],
                        weight[kind, tile(n), :],
                        NT,
                    )
                out[:, tile(n)] = part.astype(out.dtype)

            each(model // SEG, one)

        for copy in old:
            copy.wait_send()
            pending[:] = [kept for kept in pending if kept is not copy]
        block(3, core_out.at[0])
        hop3 = remote(core_out.at[0], core_in.at[m, 0], {"tensor": near})
        block(2, din.at[m])
        hop3.wait_recv()
        y_out[...] = (din[m] + core_in[m, 0].astype(F32)).astype(BF)
        hop = remote(y_out, y_in.at[m], {"tensor": far})
        block(1, core_out.at[1])
        hop1 = remote(core_out.at[1], core_in.at[m, 1], {"tensor": near})
        block(0, din.at[m])
        return hop1, hop, hop3

    chunk = 32

    def input_norms(m, hops):
        hops[0].wait_recv()
        hops[1].wait_recv()

        def one(i):
            at = pl.ds(pl.multiple_of(i * chunk, chunk), chunk)
            dh1 = din[m, at] + core_in[m, 1, at].astype(F32) + y_in[m, at].astype(F32)
            values = x[m, at].astype(F32)
            center = values - jnp.mean(values, axis=-1, keepdims=True)
            inverse = lax.rsqrt(jnp.mean(center * center, axis=-1, keepdims=True) + EPSILON)
            normed = center * inverse
            small[0] += jnp.sum((dh1 * normed).reshape(chunk // 8, 8, model), axis=0)
            din[m, at] = dr1[m, at] + norm_backward(dh1 * pre[...], normed, inverse)

        each(rows // chunk, one)

    class Chain:
        def __init__(self, kind, order):
            self.order = order
            self.kind, self.base, self.size, self.at, self.step = kind, 0, model, 0, 0
            self.copy, self.back, self.done = None, False, False

        def reduce_send(self):
            mask = self.order[self.step]
            half = self.size // 2
            out = pl.ds(pl.multiple_of(self.base + (1 - bit_of(mask)) * half, 16), half)
            slot = pl.ds(self.at, half)
            stage[self.kind, slot, :] = acc[self.kind, out, :].astype(BF)
            self.copy = remote(stage.at[self.kind, slot, :], arrived.at[self.kind, slot, :], dp_peer(mask))
            self.base, self.size = self.base + bit_of(mask) * half, half

        def reduce_wait(self):
            self.copy.wait_recv()
            mine = pl.ds(pl.multiple_of(self.base, 16), self.size)
            total = acc[self.kind, mine, :] + arrived[self.kind, pl.ds(self.at, self.size), :].astype(F32)
            self.at += self.size
            self.step += 1
            if self.step < len(bits):
                acc[self.kind, mine, :] = total
            else:
                res[self.kind, mine, :] = total.astype(BF)

        def gather_send(self):
            self.step -= 1
            mask = self.order[self.step]
            mine = pl.ds(pl.multiple_of(self.base, 16), self.size)
            self.copy = remote(res.at[self.kind, mine, :], res.at[self.kind, mine, :], dp_peer(mask))
            self.base, self.size = self.base - bit_of(mask) * self.size, 2 * self.size

        def go(self):
            if self.back:
                self.copy.wait_recv()
                if self.step:
                    self.gather_send()
                else:
                    self.done = True
            else:
                self.reduce_wait()
                if self.step < len(bits):
                    self.reduce_send()
                else:
                    self.back = True
                    self.gather_send()

    small[...] = jnp.zeros_like(small)
    small[1:4] = mid_gains[...].reshape(3, 8, model)
    contrib_k[4 * slots] = jnp.zeros((SEG, width), BF)
    contrib_v[4 * slots] = jnp.zeros((SEG, width), BF)
    in_du.wait()
    turned = bits[1:] + bits[:1]
    query, mixer, key, value = [Chain(*a) for a in ((0, bits), (3, turned), (1, bits), (2, turned))]
    each(model // SEG, out_rows)
    mixer.reduce_send()
    in_full = fetch(full_hbm, big)
    in_rest = [fetch(x_hbm, x), fetch(dr1_hbm, dr1)]
    for copy in in_tree:
        copy.wait()

    each(4, lambda step: attend_back(0, step))
    in_tree = fetch_tree(1)
    first0 = first_sends(0)
    second0 = second_pair(0)
    mixer.go()
    for copy in in_tree:
        copy.wait()

    def back1(step):
        attend_back(1, step)

        @pl.when(step == 1)
        def _():
            second_sends(0, first0, second0)

    each(4, back1)
    first1 = first_sends(1)
    second1 = second_pair(1)
    mixer.go()
    in_full.wait()
    weight_rows(0, 0)
    weight_rows(1, 0)
    query.reduce_send()
    own_key(0, first0, second0)
    own_value(0, first0, second0)
    for copy in in_rest:
        copy.wait()
    hops0 = input_rows(0, ())
    second_sends(1, first1, second1)
    weight_rows(0, 1)
    weight_rows(0, 2)
    query.go()
    mixer.go()
    input_norms(0, hops0)
    query.go()
    own_key(1, first1, second1)
    weight_rows(1, 1)
    key.reduce_send()
    own_value(1, first1, second1)
    weight_rows(1, 2)
    value.reduce_send()
    query.go()
    mixer.go()
    hops1 = input_rows(1, hops0)
    key.go()
    value.go()
    query.go()
    mixer.go()
    input_norms(1, hops1)
    totals = jnp.zeros((8, model), F32)
    place_row = lax.broadcasted_iota(jnp.int32, (8, model), 0)
    for i in range(5):
        totals = jnp.where(place_row == i, jnp.sum(small[i], axis=0, keepdims=True), totals)
    small[0] = totals
    small_copy = remote(small.at[0], small_in.at[0], {"tensor": near})
    key.go()
    value.go()
    query.go()
    mixer.go()
    small_copy.wait_recv()
    small[1] = small[0] + jnp.where(place_row < 3, small_in[0], 0.0)
    small_copy = remote(small.at[1], small_in.at[1], {"tensor": far})
    key.go()
    value.go()
    small_copy.wait_recv()
    small[2] = small[1] + jnp.where(place_row < 3, small_in[1], 0.0)
    for step, mask in enumerate(bits):
        small_copy = remote(small.at[2 + step], small_in.at[2 + step], dp_peer(mask))
        for chain in (key, value, query, mixer):
            if not chain.done:
                chain.go()
        small_copy.wait_recv()
        small[3 + step] = small[2 + step] + small_in[2 + step]
    while not (key.done and value.done and query.done and mixer.done):
        for chain in (key, value, query, mixer):
            if not chain.done:
                chain.go()
    small_out[...] = small[2 + len(bits)]

    for copy in ready + gathers[-1]:
        copy.wait_recv()
    in_share[-1].wait()
    for copy in pending:
        copy.wait_send()


def closing_call(parents, qs, os_pair, lses, scale_row, weight, pre, mid_gains, kt, vt, dos, outs, full, du, x, dr1, shares):
    micro, rows, model = x.shape
    tokens, width = qs[0].shape
    size = lax.axis_size("dp")
    bits = tuple(2**b for b in range(size.bit_length() - 1))
    vmem = pl.BlockSpec(memory_space=pltpu.VMEM)
    count, half = shares.shape[0], shares.shape[1]
    slots = DEPTH + 1
    segs = pltpu.VMEM((4 * tokens // SEG, SEG, width), BF)
    return pl.pallas_call(
        partial(closing, bits),
        out_shape=(
            jax.ShapeDtypeStruct((micro, rows, model), F32),
            jax.ShapeDtypeStruct((4, model, width), BF),
            jax.ShapeDtypeStruct((8, model), F32),
            jax.ShapeDtypeStruct((2, count // 2, 2 * half, model), BF),
        ),
        in_specs=[pl.BlockSpec(memory_space=pltpu.SMEM)] + [vmem] * 10 + [HBM] * 10,
        out_specs=(vmem, vmem, vmem, HBM),
        scratch_shapes=[
            segs,
            segs,
            pltpu.VMEM((tokens, width), F32),
            pltpu.VMEM((tokens, width), F32),
            pltpu.VMEM((SEG, SEG), F32),
            pltpu.VMEM((width, SEG), F32),
            pltpu.VMEM((4 * slots + 1, SEG, width), BF),
            pltpu.VMEM((4 * slots + 1, SEG, width), BF),
            segs,
            segs,
            segs,
            segs,
            pltpu.VMEM((micro, 6, tokens // SEG, SEG, width), BF),
            pltpu.VMEM((micro, 2, tokens // SEG, SEG, width), BF),
            pltpu.VMEM((micro, tokens, 3 * width), BF),
            pltpu.VMEM((4, model, width), F32),
            pltpu.VMEM((4, model, width), BF),
            pltpu.VMEM((4, model, width), BF),
            pltpu.VMEM((2, rows, model), BF),
            pltpu.VMEM((micro, 2, rows, model), BF),
            pltpu.VMEM((rows, model), BF),
            pltpu.VMEM((micro, rows, model), BF),
            pltpu.VMEM((3 + len(bits) + 2, 8, model), F32),
            pltpu.VMEM((2 + len(bits), 8, model), F32),
            pltpu.VMEM((micro, tokens, model), BF),
            pltpu.VMEM((micro, rows, model), BF),
            pltpu.VMEM((micro, rows, model), F32),
            pltpu.SemaphoreType.DMA((28 + 14 * len(bits),)),
            pltpu.SemaphoreType.DMA((28 + 14 * len(bits),)),
            pltpu.SemaphoreType.DMA((20,)),
        ],
        compiler_params=pltpu.CompilerParams(
            collective_id=1, has_side_effects=True, vmem_limit_bytes=62 << 20
        ),
        cost_estimate=pl.CostEstimate(flops=120 * 10**9, transcendentals=0, bytes_accessed=30 << 20),
        name="closing",
    )(
        parents, *qs, *os_pair, *lses, scale_row, weight, pre, mid_gains, shares, kt, vt, dos, *outs, full, du, x, dr1
    )


def body(
    block_input,
    cotangent,
    parent,
    pre_attn_gain,
    qkv_weight,
    head_scale,
    out_weight,
    post_attn_gain,
    pre_ffn_gain,
    fc1_weight,
    ffn_norm_gain,
    fc2_weight,
):
    tokens = cotangent.shape[1]
    width = qkv_weight.shape[2]
    parents = parent.reshape(-1)
    scale_row = jnp.repeat(head_scale, HEAD_DIM)[None, :]

    q0, q1, o0, o1, os0, os1, lse0, lse1, mixed, full1, keys, values = opening_call(
        parents, block_input, pre_attn_gain[None], qkv_weight, scale_row, out_weight
    )
    full1 = full1.reshape(MICRO, tokens, -1)
    du, dos, dr1, f_own, f_far, mid_gains, shares = middle_call(
        (os0, os1),
        mixed,
        block_input,
        cotangent,
        fc1_weight,
        fc2_weight,
        out_weight,
        post_attn_gain[None],
        pre_ffn_gain[None],
        ffn_norm_gain[None],
    )
    f_got = swap(f_far, "tensor", 2)
    outputs = (f_own + f_got.astype(F32)).astype(BF)
    din, narrow, small, whole = closing_call(
        parents,
        (q0, q1),
        (os0, os1),
        (lse0, lse1),
        scale_row,
        qkv_weight,
        pre_attn_gain[None],
        mid_gains,
        keys,
        values,
        dos,
        (o0, o1),
        full1,
        du,
        block_input,
        dr1,
        shares,
    )
    head_grad = small[4, 0:width].reshape(-1, HEAD_DIM).sum(-1)
    whole = whole.reshape(2, -1, whole.shape[-1])
    return (
        outputs,
        din,
        small[0],
        narrow[0:3].astype(F32),
        head_grad,
        narrow[3].T.astype(F32),
        small[1],
        small[2],
        whole[0].astype(F32),
        small[3],
        whole[1].astype(F32),
    )


def solution(mesh):
    in_specs = (
        P(None, ("dp", "tensor"), None),
        P(None, "dp", None),
        P(),
        P(),
        P(None, None, "tensor"),
        P("tensor"),
        P("tensor", None),
        P(),
        P(),
        P(None, "tensor"),
        P("tensor"),
        P("tensor", None),
    )
    out_specs = (
        P(None, ("dp", "tensor"), None),
        P(None, ("dp", "tensor"), None),
        P(),
        P(None, None, "tensor"),
        P("tensor"),
        P("tensor", None),
        P(),
        P(),
        P(None, "tensor"),
        P("tensor"),
        P("tensor", None),
    )
    return jax.shard_map(body, mesh=mesh, in_specs=in_specs, out_specs=out_specs, check_vma=False)
```
